128 devices in a mesh: dp: 16 (over y, x), seq: 8 (over z, core).
Axes of the slice: x: 4, y: 4, z: 4, core: 2. Of those that a mesh axis runs over, the one named last changes fastest.
Arguments:
- hidden_in: bfloat16 [32768, 2048], P(('dp', 'seq')), may hold values from -6 to 6
- mix_values: bfloat16 [32768, 4096], P(('dp', 'seq')), may hold values from -6 to 6
- mix_gate: bfloat16 [32768, 4096], P(('dp', 'seq')), may hold values from -6 to 6
- state_proj: bfloat16 [32768, 2048], P(('dp', 'seq')), may hold values from -2 to 2
- step_raw: bfloat16 [32768, 64], P(('dp', 'seq')), may hold values from -4 to 4
- step_bias: float32 [64], replicated, may hold values from -1 to 0.5
- decay_rate: float32 [64], replicated, may hold values from 0.1 to 40
- skip_gain: float32 [64], replicated, may hold values from 0.5 to 1.5
- norm_gain: float32 [4096], replicated, may hold values from 0.5 to 1.5
- out_weight: bfloat16 [4096, 2048], P('seq'), may hold values from -0.09375 to 0.09375
- ffn_gain: float32 [2048], replicated, may hold values from 0.5 to 1.5
- expert_ids: int32 [32768, 8], P(('dp', 'seq')), may hold values from 0 to 127, all different within a row; in each aligned block of 256 rows (0 to 255, 256 to 511, ...) at most 18 rows name the same one
- route_weights: float32 [32768, 8], P(('dp', 'seq')), may hold values from 0.05 to 0.25
- gate_up: bfloat16 [128, 2048, 1536], P(('dp', 'seq')), may hold values from -0.125 to 0.125
- down_proj: bfloat16 [128, 768, 2048], P(('dp', 'seq')), may hold values from -0.21875 to 0.21875
- doc_lengths: int32 [16, 3], P('dp'), may hold values from 1 to 1536, 2048 in all within a row
Outputs:
- block_out: bfloat16 [32768, 2048], P(('dp', 'seq'))
The draws below stay inside these ranges and needn't reach their ends.
Inputs may be any that keep to these rules, and one draw needn't show every extreme that they name: `expert_ids`: in the rows of one device (aligned blocks of 256 tokens) no expert is chosen more than 18 times, a bound that some block reaches; a token's 8 experts differ. `doc_lengths`: each row sums to 2048; its largest length is exactly three quarters of 2048, rounded down.
All inputs are finite; a program needn't handle non-finite values.
Results may differ from the reference program's by a relative error of at most 0.019.
Values may be sent and summed in bfloat16 or wider, within the bound.
No kernel may reach another device: no remote copies, remote signals or barrier semaphores. Data moves between devices by JAX's collectives and lax.ppermute only.
A program may use at most 256 MiB of HBM per device.

```python
import math
import jax
import jax.numpy as jnp
import numpy as np
from jax import lax

D = 2048
HEADS = 64
HEADDIM = 64
STATE = 128
GROUPS = 8
SPAN = 256
FF = 768
TOP = 8
DOCS = 3
TOK_DEV = 256
SEQ_TOK = 2048
TOKENS = 32768
DI = 4096
EXPERTS = 128
CAP = 18
N_DP = 16


def level_of(key, extent, cuts, least, top_value):
    def one(axis_at, shards_of):
        steps = jax.random.uniform(jax.random.fold_in(jax.random.fold_in(key, 6), axis_at), (shards_of,), jnp.float32, least / len(cuts), top_value / len(cuts))
        return jnp.repeat(jnp.exp(steps), extent[axis_at] // shards_of).reshape((-1,) + (1,) * (len(extent) - axis_at - 1))

    level = one(*cuts[0])
    for cut in cuts[1:]:
        level = level * one(*cut)
    return level


def length_profile(amount, total, most, slope):
    weights = [(1 << 20) // math.isqrt(rank ** slope) + 1 for rank in range(2, amount + 1)]
    rest, given = total - most - (amount - 1), [1] * (amount - 1)
    while rest > 0:
        candidates = [i for i in range(amount - 1) if given[i] < most]
        whole, budget = sum([weights[i] for i in candidates]), rest
        for i in candidates:
            addition = min(most - given[i], max(1, budget * weights[i] // whole), rest)
            given[i] = given[i] + addition
            rest = rest - addition
    return np.array([most] + given)


def ragged(key, count, total, limit, lean):
    if count == 2:
        one = jax.random.randint(key, (), max(1, total - limit), min(limit, total - 1) + 1)
        return jnp.stack([one, total - one])
    tallies = jnp.asarray(length_profile(count, total, limit, lean), jnp.int32)
    couples = (count - 1) // 2
    donor, sink = tallies[1:1 + 2 * couples:2], tallies[2:2 + 2 * couples:2]
    slack = jnp.minimum(donor - 1, limit - sink)
    passed = jax.random.randint(jax.random.fold_in(key, 1), (couples,), 0, 1 << 20) % (slack + 1)
    tallies = tallies.at[1:1 + 2 * couples:2].set(donor - passed).at[2:2 + 2 * couples:2].set(sink + passed)
    return tallies[jax.random.permutation(jax.random.fold_in(key, 2), count)]


def shared_out(rng, own, number, rows, amount, top, bound, slope):
    sequence = jax.random.permutation(rng, amount)
    heavy_load, usual = shares(amount, rows * top, bound, slope, True), shares(amount, rows * top, bound, slope, False)
    places = jnp.arange(amount)

    def named(tallies, rotation):
        used = int((tallies > 0).sum())
        fixed = max(1, used // 4)
        moved = fixed + (places - fixed + rotation * (used - fixed)) % max(1, amount - fixed)
        return jnp.zeros((amount,), jnp.int32).at[sequence[jnp.where(places < fixed, places, moved)]].set(jnp.asarray(tallies, jnp.int32))

    tallies = jnp.where(number % 4 == 0, named(heavy_load, number // 4), named(usual, number - number // 4 - 1))
    mixed = jax.random.permutation(jax.random.fold_in(own, 3), amount)
    donor, taker = mixed[0:amount // 2 * 2:2], mixed[1:amount // 2 * 2:2]
    slack = jnp.minimum(tallies[donor] - 1, bound - tallies[taker]) // 2
    slack = jnp.where((donor == sequence[0]) | (taker == sequence[0]) | (tallies[taker] == 0), 0, jnp.maximum(slack, 0))
    moved = jax.random.randint(jax.random.fold_in(own, 4), (amount // 2,), 0, 1 << 20) % (slack + 1)
    tallies = tallies.at[donor].add(-moved).at[taker].add(moved)
    labels = jnp.searchsorted(jnp.cumsum(tallies), jnp.arange(rows * top), side="right").astype(jnp.int32)
    table = labels.reshape(top, rows).T
    table = table[jax.random.permutation(jax.random.fold_in(own, 1), rows)]
    rotation = jax.random.randint(jax.random.fold_in(own, 2), (rows, 1), 0, top)
    return jnp.take_along_axis(table, (jnp.arange(top)[None, :] + rotation) % top, axis=1)


def shares(amount, total, most, slope, full):
    loads = [(1 << 20) // math.isqrt(rank ** slope) + 1 for rank in range(1, amount + 1)]
    largest = most if full else min(most, max(-(-total // amount), total * loads[0] // sum(loads)))
    least = 1 if total - largest >= amount - 1 else 0
    holding, rest = [largest] + [least] * (amount - 1), total - largest - least * (amount - 1)
    while rest > 0:
        free = [i for i in range(1, amount) if holding[i] < largest] or [i for i in range(1, amount) if holding[i] < most]
        whole, left = sum([loads[i] for i in free]), rest
        for i in free:
            more = min(most - holding[i], max(1, left * loads[i] // whole), rest)
            holding[i] = holding[i] + more
            rest = rest - more
    return np.array(holding)


def normal_values(own_key, extent, scale, most, shards=(), kind=jnp.bfloat16):
    level = level_of(own_key, extent, shards, -0.22, 0.18) if shards else 1.0
    values = jax.random.normal(own_key, extent, jnp.float32) * scale * level
    return jnp.minimum(jnp.maximum(values, -most), most).astype(kind)


def setup_inputs(seed: int = 0) -> dict:
    streams_of = jax.random.split(jax.random.key(seed), 17)
    hidden_in = normal_values(streams_of[0], (TOKENS, D), 1.0, 6.0, ((0, 128),))
    mix_values = normal_values(streams_of[1], (TOKENS, DI), 1.0, 6.0, ((0, 128),))
    mix_gate = normal_values(streams_of[2], (TOKENS, DI), 1.0, 6.0, ((0, 128),))
    state_proj = normal_values(streams_of[3], (TOKENS, 2 * GROUPS * STATE), 0.3, 2.0, ((0, 128),))
    step_raw = normal_values(streams_of[4], (TOKENS, HEADS), 1.0, 4.0, ((0, 128),))
    step_bias = jnp.clip(jax.random.uniform(streams_of[5], (HEADS,), jnp.float32, -1.0, 0.5), -1.0, 0.5)
    decay_rate = jnp.clip(jnp.exp(jax.random.uniform(streams_of[6], (HEADS,), jnp.float32, math.log(0.1), math.log(40.0))), 0.1, 40.0)
    skip_gain = jnp.clip(jax.random.uniform(streams_of[7], (HEADS,), jnp.float32, 0.5, 1.5), 0.5, 1.5)
    norm_gain = jnp.clip(1.0 + 0.1 * jax.random.normal(streams_of[8], (DI,), jnp.float32), 0.5, 1.5)
    out_weight = normal_values(streams_of[9], (DI, D), DI ** -0.5, 0.09375, ((0, 8),))
    ffn_gain = jnp.clip(1.0 + 0.1 * jax.random.normal(streams_of[10], (D,), jnp.float32), 0.5, 1.5)
    expert_ids_keys = jax.random.split(jax.random.fold_in(streams_of[11], 1), TOKENS // TOK_DEV)
    expert_ids_turns = jax.random.permutation(jax.random.fold_in(streams_of[11], 3), TOKENS // TOK_DEV)
    expert_ids = jax.vmap(lambda own, number: shared_out(jax.random.fold_in(streams_of[11], 2), own, number, TOK_DEV, EXPERTS, TOP, CAP, 2))(expert_ids_keys, expert_ids_turns).reshape((TOKENS, TOP))
    route_weights = jnp.clip(0.05 + 0.2 * jax.random.uniform(streams_of[12], (TOKENS, TOP), jnp.float32) ** level_of(streams_of[12], (TOKENS, TOP), ((0, 128),), -0.2, 0.2), 0.05, 0.25)
    gate_up = normal_values(streams_of[13], (EXPERTS, D, 2 * FF), D ** -0.5, 0.125, ((0, 128),))
    down_proj = normal_values(streams_of[14], (EXPERTS, FF, D), FF ** -0.5, 0.21875, ((0, 128),))
    doc_lengths = jax.vmap(lambda own: ragged(own, DOCS, SEQ_TOK, SEQ_TOK * 3 // 4, 2))(jax.random.split(streams_of[15], N_DP)).reshape((N_DP, DOCS)).astype(jnp.int32)
    return {"hidden_in": hidden_in, "mix_values": mix_values, "mix_gate": mix_gate, "state_proj": state_proj, "step_raw": step_raw, "step_bias": step_bias, "decay_rate": decay_rate, "skip_gain": skip_gain, "norm_gain": norm_gain, "out_weight": out_weight, "ffn_gain": ffn_gain, "expert_ids": expert_ids, "route_weights": route_weights, "gate_up": gate_up, "down_proj": down_proj, "doc_lengths": doc_lengths}


precise = lax.Precision.HIGHEST
epsilon = 1e-05

def segment_of(lengths, positions):
    bounds = jnp.cumsum(lengths).astype(jnp.int32)
    return lax.optimization_barrier(jnp.sum((positions[:, None] >= bounds[None, :]).astype(jnp.int32), axis=1)).astype(jnp.int32)

def span_pass(carry, inputs):
    carry_state, segment_before = carry
    values, step_sizes, log_decay, segment, b_group, c_group = inputs
    length = values.shape[0]
    per_group = values.shape[1] // b_group.shape[1]
    cumulated = jnp.cumsum(log_decay, axis=0)
    row_ids = jnp.arange(length)
    allowed = (row_ids[:, None] >= row_ids[None, :]) & (segment[:, None] == segment[None, :])
    spread = jnp.transpose(cumulated[:, None, :] - cumulated[None, :, :], (2, 0, 1))
    decays = jnp.where(allowed[None], jnp.exp(jnp.minimum(spread, 0.0)), 0.0)
    scores = jnp.einsum('ign,jgn->gij', c_group, b_group, precision=precise)
    scores = jnp.repeat(scores, per_group, axis=0)
    weights = decays * scores * jnp.transpose(step_sizes)[:, None, :]
    inside = jnp.einsum('hij,jhp->ihp', weights, values, precision=precise)
    c_heads = jnp.repeat(c_group, per_group, axis=1)
    b_heads = jnp.repeat(b_group, per_group, axis=1)
    living = (segment == segment_before).astype(jnp.float32)
    reach = living[:, None] * jnp.exp(cumulated)
    carried = jnp.einsum('hpn,ihn->ihp', carry_state, c_heads, precision=precise) * reach[:, :, None]
    final_log = cumulated[-1]
    tail_weight = jnp.where((segment == segment[-1])[:, None], jnp.exp(jnp.minimum(final_log[None, :] - cumulated, 0.0)), 0.0) * step_sizes
    fresh_state = jnp.einsum('jhp,jhn->hpn', values * tail_weight[:, :, None], b_heads, precision=precise)
    keep_factor = (segment[-1] == segment_before).astype(jnp.float32) * jnp.exp(final_log)
    carry_state = keep_factor[:, None, None] * carry_state + fresh_state
    return ((carry_state, segment[-1]), inside + carried)

def run_spans(values, step_sizes, log_decay, segment, b_group, c_group, zero_state, segment_before):
    number = values.shape[0] // SPAN

    def blocked(array):
        return array.reshape((number, SPAN) + array.shape[1:])
    inputs = tuple((blocked(array) for array in (values, step_sizes, log_decay, segment, b_group, c_group)))
    (end_state, ignored), outputs = lax.scan(span_pass, (zero_state, segment_before), inputs)
    return (outputs.reshape(values.shape), end_state)

def gated_norm(mixed_out, gate, gain, groups):
    gated = mixed_out * jax.nn.silu(gate.astype(jnp.float32))
    parts = gated.reshape(gated.shape[0], groups, -1)
    scale = lax.rsqrt(lax.optimization_barrier(jnp.mean(parts * parts, axis=-1, keepdims=True)) + epsilon)
    return ((parts * scale).reshape(gated.shape) * gain[None, :]).astype(jnp.bfloat16)

def reference(hidden_in, mix_values, mix_gate, state_proj, step_raw, step_bias, decay_rate, skip_gain, norm_gain, out_weight, ffn_gain, expert_ids, route_weights, gate_up, down_proj, doc_lengths):
    step_all = jax.nn.softplus(step_raw.astype(jnp.float32) + step_bias[None, :])
    log_all = -step_all * decay_rate[None, :] / SEQ_TOK
    values_all = mix_values.astype(jnp.float32).reshape(N_DP, SEQ_TOK, HEADS, HEADDIM)
    proj_all = state_proj.astype(jnp.float32).reshape(N_DP, SEQ_TOK, GROUPS, 2, STATE)
    positions = jnp.arange(SEQ_TOK, dtype=jnp.int32)

    def group_segments(lengths):
        return segment_of(lengths, positions)
    segments = lax.map(group_segments, doc_lengths)

    def one_group(inputs):
        values, step_sizes, log_decay, segment, projected = inputs
        zero_state = jnp.zeros((HEADS, HEADDIM, STATE), jnp.float32)
        mixed_out, ignored = run_spans(values, step_sizes, log_decay, segment, projected[:, :, 0], projected[:, :, 1], zero_state, jnp.array(-1, jnp.int32))
        return mixed_out
    mixed_all = lax.map(one_group, (values_all, step_all.reshape(N_DP, SEQ_TOK, HEADS), log_all.reshape(N_DP, SEQ_TOK, HEADS), segments, proj_all))
    mixed_all = mixed_all + skip_gain[None, None, :, None] * values_all
    normed_mix = gated_norm(mixed_all.reshape(TOKENS, HEADS * HEADDIM), mix_gate, norm_gain, GROUPS)
    mixer_out = jnp.dot(normed_mix, out_weight, preferred_element_type=jnp.float32)
    merged = lax.optimization_barrier((hidden_in.astype(jnp.float32) + mixer_out).astype(jnp.bfloat16))
    merged_f = merged.astype(jnp.float32)
    square_mean = lax.optimization_barrier(jnp.mean(merged_f * merged_f, axis=-1, keepdims=True))
    normed = (merged_f * lax.rsqrt(square_mean + epsilon) * ffn_gain[None, :]).astype(jnp.bfloat16)
    blocks = TOKENS // TOK_DEV
    per_block = TOK_DEV * TOP
    block_ids = expert_ids.reshape(blocks, per_block)

    def block_rank(ids_block):
        onehot = (ids_block[:, None] == jnp.arange(EXPERTS, dtype=jnp.int32)[None, :]).astype(jnp.int32)
        return lax.optimization_barrier(jnp.sum((jnp.cumsum(onehot, axis=0) - onehot) * onehot, axis=1)).astype(jnp.int32)
    ranks = lax.map(block_rank, block_ids)
    block_index = jnp.arange(blocks, dtype=jnp.int32)[:, None]
    slots = ((block_ids * blocks + block_index) * CAP + ranks).reshape(-1).astype(jnp.int32)
    route_token = jnp.arange(TOKENS * TOP, dtype=jnp.int32) // TOP
    slot_token = jnp.zeros((EXPERTS * blocks * CAP,), jnp.int32).at[slots].set(route_token)
    slot_weight = jnp.zeros((EXPERTS * blocks * CAP,), jnp.float32).at[slots].set(route_weights.reshape(-1))

    def add_expert(total, inputs):
        tokens_here, weight_here, first_proj, second_proj = inputs
        rows_in = normed[tokens_here]
        hidden = jnp.dot(rows_in, first_proj, preferred_element_type=jnp.float32)
        active = (jax.nn.silu(hidden[:, :FF]) * hidden[:, FF:]).astype(jnp.bfloat16)
        result = jnp.dot(active, second_proj, preferred_element_type=jnp.float32).astype(jnp.bfloat16)
        return (total.at[tokens_here].add(weight_here[:, None] * result.astype(jnp.float32)), None)
    total, ignored = lax.scan(add_expert, jnp.zeros((TOKENS, D), jnp.float32), (slot_token.reshape(EXPERTS, -1), slot_weight.reshape(EXPERTS, -1), gate_up, down_proj))
    return (merged_f + total).astype(jnp.bfloat16)
```

```python
import functools

import jax
import jax.numpy as jnp
from jax import lax
from jax.experimental import pallas as pl
from jax.experimental.pallas import tpu as pltpu
from jax.sharding import PartitionSpec as P

D = 2048
HEADS = 64
HEADDIM = 64
STATE = 128
GROUPS = 8
HPG = HEADS // GROUPS
CH = HPG * HEADDIM
FF = 768
TOP = 8
TOK = 256
EXPERTS = 128
EPS = 1e-05
MAIN = 16
ROWS = 72
QW = 512
NQ = 4
EB = 16
SB = 16

f32 = jnp.float32
bf16 = jnp.bfloat16


def params(limit_mib, n=1):
    return pltpu.CompilerParams(
        vmem_limit_bytes=limit_mib << 20, dimension_semantics=("arbitrary",) * n
    )


def mm(a, b):
    return jnp.dot(a, b, preferred_element_type=f32)


def mm_t(a, b, da, db):
    return lax.dot_general(a, b, (((da,), (db,)), ((), ())), preferred_element_type=f32)


def split2(v):
    hi = v.astype(bf16)
    lo = (v - hi.astype(f32)).astype(bf16)
    return hi, lo


def spread(v, e):
    hi, lo = split2(v)
    return mm(hi, e) + mm(lo, e)


def head_onehot(g):
    h = lax.broadcasted_iota(jnp.int32, (HEADS, CH), 0)
    c = lax.broadcasted_iota(jnp.int32, (HEADS, CH), 1)
    return (h == g * HPG + c // HEADDIM).astype(f32).astype(bf16)


def segments(s_ref, shape, dim):
    pos = s_ref[3] + lax.broadcasted_iota(jnp.int32, shape, dim)
    return sum((pos >= s_ref[i]).astype(jnp.int32) for i in range(3))


def segment_at(s_ref, pos):
    return sum((pos >= s_ref[i]).astype(jnp.int32) for i in range(3))


def segment_before(s_ref, start):
    return jnp.where(start == 0, -1, segment_at(s_ref, start - 1))


def state_kernel(s_ref, raw_ref, bias_ref, rate_ref, x_ref, p_ref, fresh_ref, cum_ref, xs_ref, a_s, e_s):
    g = pl.program_id(0)

    @pl.when(g == 0)
    def _():
        v = raw_ref[...].astype(f32) + bias_ref[...]
        step = jnp.maximum(v, 0.0) + jnp.log(1.0 + jnp.exp(-jnp.abs(v)))
        logd = -step * rate_ref[...] * (1.0 / 2048.0)
        r = lax.broadcasted_iota(jnp.int32, (TOK, TOK), 0)
        c = lax.broadcasted_iota(jnp.int32, (TOK, TOK), 1)
        tri = (r >= c).astype(f32)
        cum = jnp.dot(tri, logd, preferred_element_type=f32, precision=lax.Precision.HIGHEST)
        cum_ref[...] = cum
        a_s[...] = step * jnp.exp(-cum)
        e_s[...] = jnp.exp(cum[TOK - 8 :, :])

    e = head_onehot(g)
    xs = (x_ref[...].astype(f32) * spread(a_s[...], e)).astype(bf16)
    xs_ref[...] = xs
    last = segment_at(s_ref, s_ref[3] + TOK - 1)
    b = jnp.where(segments(s_ref, (TOK, STATE), 0) == last, p_ref[:, :STATE].astype(f32), 0.0).astype(bf16)
    end = spread(e_s[...], e)[7:8, :]
    fresh_ref[0, :STATE, :] = (mm_t(b, xs, 0, 0) * end).astype(bf16)
    hi = end.astype(bf16).astype(f32)
    row = lax.broadcasted_iota(jnp.int32, (16, CH), 0)
    tail = jnp.where(row == 0, hi, jnp.where(row == 1, end - hi, 0.0))
    fresh_ref[0, STATE:, :] = tail.astype(bf16)


def span_states(scal, raw, bias, rate, x, p):
    smem = pl.BlockSpec(memory_space=pltpu.SMEM)
    return pl.pallas_call(
        state_kernel,
        grid=(GROUPS,),
        in_specs=[
            smem,
            pl.BlockSpec((TOK, HEADS), lambda g: (0, 0)),
            pl.BlockSpec((1, HEADS), lambda g: (0, 0)),
            pl.BlockSpec((1, HEADS), lambda g: (0, 0)),
            pl.BlockSpec((TOK, CH), lambda g: (0, g)),
            pl.BlockSpec((TOK, 2 * STATE), lambda g: (0, g)),
        ],
        out_specs=[
            pl.BlockSpec((1, STATE + 16, CH), lambda g: (g, 0, 0)),
            pl.BlockSpec((TOK, HEADS), lambda g: (0, 0)),
            pl.BlockSpec((TOK, CH), lambda g: (0, g)),
        ],
        out_shape=[
            jax.ShapeDtypeStruct((GROUPS, STATE + 16, CH), bf16),
            jax.ShapeDtypeStruct((TOK, HEADS), f32),
            jax.ShapeDtypeStruct((TOK, HEADS * HEADDIM), bf16),
        ],
        scratch_shapes=[pltpu.VMEM((TOK, HEADS), f32), pltpu.VMEM((8, HEADS), f32)],
        compiler_params=params(32),
        name="span_states",
    )(scal, raw, bias, rate, x, p)


def prefix_kernel(s_ref, in_ref, out_ref):
    carry = jnp.zeros((STATE, CH), f32)
    for r in range(8):
        out_ref[r] = carry.astype(bf16)
        tail = in_ref[r, STATE:, :].astype(f32)
        keep = tail[0:1, :] + tail[1:2, :]
        start = r * TOK
        same = segment_at(s_ref, start + TOK - 1) == segment_before(s_ref, jnp.int32(start))
        keep = keep * same.astype(f32)
        carry = carry * keep + in_ref[r, :STATE, :].astype(f32)


def prefix(scal, fresh):
    return pl.pallas_call(
        prefix_kernel,
        in_specs=[pl.BlockSpec(memory_space=pltpu.SMEM), pl.BlockSpec(memory_space=pltpu.VMEM)],
        out_specs=pl.BlockSpec(memory_space=pltpu.VMEM),
        out_shape=jax.ShapeDtypeStruct((8, STATE, CH), bf16),
        compiler_params=pltpu.CompilerParams(vmem_limit_bytes=16 << 20),
        name="span_prefix",
    )(scal, fresh)


def mixer_kernel(
    s_ref, x_ref, z_ref, p_ref, xs_ref, cum_ref, carry_ref, skip_ref, gain_ref, w_ref, hid_ref,
    fgain_ref, merged_ref, normed_ref, acc_ref,
):
    g = pl.program_id(0)
    e = head_onehot(g)
    b, c = p_ref[:, :STATE], p_ref[:, STATE:]
    scores = mm_t(c, b, 1, 1)
    i = lax.broadcasted_iota(jnp.int32, (TOK, TOK), 0)
    j = lax.broadcasted_iota(jnp.int32, (TOK, TOK), 1)
    ok = (i >= j) & (segments(s_ref, (TOK, TOK), 0) == segments(s_ref, (TOK, TOK), 1))
    m = jnp.where(ok, scores, 0.0).astype(bf16)
    before = segment_before(s_ref, s_ref[3])
    cl = jnp.where(segments(s_ref, (TOK, STATE), 0) == before, c.astype(f32), 0.0).astype(bf16)
    acc = mm(m, xs_ref[...]) + mm(cl, carry_ref[0])
    x = x_ref[...].astype(f32)
    skip = spread(jnp.broadcast_to(skip_ref[...], (8, HEADS)), e)[0:1, :]
    mixed = acc * spread(jnp.exp(cum_ref[...]), e) + skip * x
    z = z_ref[...].astype(f32)
    u = mixed * (z / (1.0 + jnp.exp(-z)))
    ms = jnp.mean(u * u, axis=-1, keepdims=True)
    n = (u * lax.rsqrt(ms + EPS) * gain_ref[...]).astype(bf16)
    w = w_ref[...].reshape(CH, D)
    part = mm(n, w)

    @pl.when(g == 0)
    def _():
        acc_ref[...] = part

    @pl.when(g > 0)
    def _():
        acc_ref[...] += part

    @pl.when(g == GROUPS - 1)
    def _():
        merged = (hid_ref[...].astype(f32) + acc_ref[...]).astype(bf16)
        merged_ref[...] = merged
        mf = merged.astype(f32)
        sq = jnp.mean(mf * mf, axis=-1, keepdims=True)
        normed_ref[...] = (mf * lax.rsqrt(sq + EPS) * fgain_ref[...]).astype(bf16)


def mixer(scal, x, z, p, xs, cum, carry, skip, gain, w, hid, fgain):
    fixed = lambda g: (0, 0)
    col = lambda g: (0, g)
    return pl.pallas_call(
        mixer_kernel,
        grid=(GROUPS,),
        in_specs=[
            pl.BlockSpec(memory_space=pltpu.SMEM),
            pl.BlockSpec((TOK, CH), col),
            pl.BlockSpec((TOK, CH), col),
            pl.BlockSpec((TOK, 2 * STATE), col),
            pl.BlockSpec((TOK, CH), col),
            pl.BlockSpec((TOK, HEADS), fixed),
            pl.BlockSpec((1, STATE, CH), lambda g: (g, 0, 0)),
            pl.BlockSpec((1, HEADS), fixed),
            pl.BlockSpec((1, CH), col),
            pl.BlockSpec((16, 1, CH // 16, D), lambda g: (0, g, 0, 0)),
            pl.BlockSpec((TOK, D), fixed),
            pl.BlockSpec((1, D), fixed),
        ],
        out_specs=[pl.BlockSpec((TOK, D), fixed), pl.BlockSpec((TOK, D), fixed)],
        out_shape=[jax.ShapeDtypeStruct((TOK, D), bf16)] * 2,
        scratch_shapes=[pltpu.VMEM((TOK, D), f32)],
        compiler_params=params(40),
        name="mixer",
    )(scal, x, z, p, xs, cum, carry, skip, gain, w, hid, fgain)


def route_kernel(ids_ref, rw_ref, rank_ref, wt_ref):
    e = lax.broadcasted_iota(jnp.int32, (EXPERTS, TOK), 0)
    member = jnp.zeros((EXPERTS, TOK), f32)
    weight = jnp.zeros((EXPERTS, TOK), f32)
    for k in range(TOP):
        hit = ids_ref[k : k + 1, :] == e
        member += jnp.where(hit, 1.0, 0.0)
        weight += jnp.where(hit, rw_ref[k : k + 1, :], 0.0)
    r = lax.broadcasted_iota(jnp.int32, (TOK, TOK), 0)
    c = lax.broadcasted_iota(jnp.int32, (TOK, TOK), 1)
    before = (r < c).astype(f32).astype(bf16)
    rank = mm(member.astype(bf16), before)
    rank_ref[...] = jnp.where(member > 0.5, rank, -1.0)
    wt_ref[...] = weight


def route_tables(ids_t, rw_t):
    vm = pl.BlockSpec(memory_space=pltpu.VMEM)
    return pl.pallas_call(
        route_kernel,
        in_specs=[vm, vm],
        out_specs=[vm, vm],
        out_shape=[jax.ShapeDtypeStruct((EXPERTS, TOK), f32)] * 2,
        name="route_tables",
    )(ids_t, rw_t)


def slot_hits(rank):
    n = rank.shape[0]
    r3 = jnp.broadcast_to(rank[:, None, :], (n, MAIN, TOK))
    c = lax.broadcasted_iota(jnp.int32, (n, MAIN, TOK), 1).astype(f32)
    main = (r3 == c).reshape(n * MAIN, TOK)
    o3 = jnp.broadcast_to(rank[:, None, :], (n, 8, TOK))
    j = (lax.broadcasted_iota(jnp.int32, (n, 8, TOK), 1) % 2 + MAIN).astype(f32)
    over = (o3 == j).reshape(n * 8, TOK)
    return main, over


def dispatch_kernel(rank_ref, x_ref, out_ref):
    rank = rank_ref[...]
    main, over = slot_hits(rank)
    rows = mm(main.astype(f32).astype(bf16), x_ref[...]).astype(bf16)
    orow = mm(over.astype(f32).astype(bf16), x_ref[...])
    q_of = (lax.broadcasted_iota(jnp.int32, (EB * 8, QW), 0) % 8) // 2
    o = jnp.zeros((EB * 8, QW), f32)
    for q in range(NQ):
        out_ref[:, q * MAIN : (q + 1) * MAIN, :] = rows[:, q * QW : (q + 1) * QW].reshape(EB, MAIN, QW)
        o = jnp.where(q_of == q, orow[:, q * QW : (q + 1) * QW], o)
    out_ref[:, NQ * MAIN :, :] = o.reshape(EB, 8, QW).astype(bf16)


def dispatch(rank, normed):
    return pl.pallas_call(
        dispatch_kernel,
        grid=(EXPERTS // EB,),
        in_specs=[
            pl.BlockSpec((EB, TOK), lambda i: (i, 0)),
            pl.BlockSpec((TOK, D), lambda i: (0, 0)),
        ],
        out_specs=pl.BlockSpec((EB, ROWS, QW), lambda i: (i, 0, 0)),
        out_shape=jax.ShapeDtypeStruct((EXPERTS, ROWS, QW), bf16),
        compiler_params=params(32),
        name="dispatch",
    )(rank, normed)


def over_perm():
    r = lax.broadcasted_iota(jnp.int32, (SB * 8, SB * 8), 0)
    c = lax.broadcasted_iota(jnp.int32, (SB * 8, SB * 8), 1)
    q, s, j = r // (2 * SB), (r % (2 * SB)) // 2, r % 2
    return (c == s * 8 + q * 2 + j).astype(f32).astype(bf16)


def expert_kernel(in_ref, gu_ref, dn_ref, out_ref):
    perm = over_perm()
    over = mm(perm, in_ref[:, NQ * MAIN :, :].reshape(SB * 8, QW)).astype(bf16)
    parts = []
    for q in range(NQ):
        main = in_ref[:, q * MAIN : (q + 1) * MAIN, :].reshape(SB * MAIN, QW)
        parts.append(jnp.concatenate([main, over[q * 2 * SB : (q + 1) * 2 * SB]], axis=0))
    lhs = jnp.concatenate(parts, axis=1)
    hidden = mm(lhs, gu_ref[0])
    gate = hidden[:, :FF]
    active = (gate / (1.0 + jnp.exp(-gate)) * hidden[:, FF:]).astype(bf16)
    res = mm(active, dn_ref[0]).astype(bf16)
    n = SB * MAIN
    for q in range(NQ):
        out_ref[:, q * MAIN : (q + 1) * MAIN, :] = res[:n, q * QW : (q + 1) * QW].reshape(SB, MAIN, QW)
    o = jnp.concatenate([res[n:, q * QW : (q + 1) * QW] for q in range(NQ)], axis=0)
    out_ref[:, NQ * MAIN :, :] = mm_t(perm, o, 0, 0).reshape(SB, 8, QW).astype(bf16)


def expert_ffn(arrived, gate_up, down):
    n = arrived.shape[0]
    return pl.pallas_call(
        expert_kernel,
        grid=(n // SB,),
        in_specs=[
            pl.BlockSpec((SB, ROWS, QW), lambda i: (i, 0, 0)),
            pl.BlockSpec((1, D, 2 * FF), lambda i: (0, 0, 0), pipeline_mode=pl.Buffered(1)),
            pl.BlockSpec((1, FF, D), lambda i: (0, 0, 0), pipeline_mode=pl.Buffered(1)),
        ],
        out_specs=pl.BlockSpec((SB, ROWS, QW), lambda i: (i, 0, 0)),
        out_shape=jax.ShapeDtypeStruct(arrived.shape, bf16),
        compiler_params=params(48),
        name="expert_ffn",
    )(arrived, gate_up, down)


def combine_kernel(rank_ref, wt_ref, ret_ref, merged_ref, out_ref, acc_ref):
    i = pl.program_id(0)

    @pl.when(i == 0)
    def _():
        acc_ref[...] = merged_ref[...].astype(f32)

    main, over = slot_hits(rank_ref[...])
    wt = wt_ref[...]
    wm = jnp.broadcast_to(wt[:, None, :], (EB, MAIN, TOK)).reshape(EB * MAIN, TOK)
    wo = jnp.broadcast_to(wt[:, None, :], (EB, 8, TOK)).reshape(EB * 8, TOK)
    wm = jnp.where(main, wm, 0.0)
    wo = jnp.where(over, wo, 0.0)
    mhi, mlo = split2(wm)
    q_of = (lax.broadcasted_iota(jnp.int32, (EB * 8, TOK), 0) % 8) // 2
    ro = ret_ref[:, NQ * MAIN :, :].reshape(EB * 8, QW)
    for q in range(NQ):
        rq = ret_ref[:, q * MAIN : (q + 1) * MAIN, :].reshape(EB * MAIN, QW)
        ohi, olo = split2(jnp.where(q_of == q, wo, 0.0))
        part = mm_t(mhi, rq, 0, 0) + mm_t(mlo, rq, 0, 0) + mm_t(ohi, ro, 0, 0) + mm_t(olo, ro, 0, 0)
        acc_ref[:, q * QW : (q + 1) * QW] += part

    @pl.when(i == pl.num_programs(0) - 1)
    def _():
        out_ref[...] = acc_ref[...].astype(bf16)


def combine(rank, wt, returned, merged):
    return pl.pallas_call(
        combine_kernel,
        grid=(EXPERTS // EB,),
        in_specs=[
            pl.BlockSpec((EB, TOK), lambda i: (i, 0)),
            pl.BlockSpec((EB, TOK), lambda i: (i, 0)),
            pl.BlockSpec((EB, ROWS, QW), lambda i: (i, 0, 0)),
            pl.BlockSpec((TOK, D), lambda i: (0, 0)),
        ],
        out_specs=pl.BlockSpec((TOK, D), lambda i: (0, 0)),
        out_shape=jax.ShapeDtypeStruct((TOK, D), bf16),
        scratch_shapes=[pltpu.VMEM((TOK, D), f32)],
        compiler_params=params(32),
        name="combine",
    )(rank, wt, returned, merged)


def body(
    hidden_in, mix_values, mix_gate, state_proj, step_raw, step_bias, decay_rate, skip_gain,
    norm_gain, out_weight, ffn_gain, expert_ids, route_weights, gate_up, down_proj, doc_lengths,
):
    both = ("dp", "seq")
    seq_rank = lax.axis_index("seq")
    dp_rank = lax.axis_index("dp")
    bounds = jnp.cumsum(doc_lengths[0]).astype(jnp.int32)
    scal = jnp.concatenate([bounds, (seq_rank * TOK).astype(jnp.int32)[None]])

    share = out_weight.shape[0] // 16
    w_mine = lax.dynamic_slice_in_dim(out_weight, dp_rank * share, share)
    w_all = lax.all_gather(w_mine, both, axis=0, tiled=True).reshape(16, GROUPS, share, D)

    rank, wt = route_tables(expert_ids.T, route_weights.T)
    fresh, cum, xs = span_states(
        scal, step_raw, step_bias[None], decay_rate[None], mix_values, state_proj
    )
    fresh = lax.all_to_all(fresh, "seq", split_axis=0, concat_axis=0, tiled=True)
    carry = prefix(scal, fresh)
    carry = lax.all_to_all(carry, "seq", split_axis=0, concat_axis=0, tiled=True)
    merged, normed = mixer(
        scal, mix_values, mix_gate, state_proj, xs, cum, carry, skip_gain[None], norm_gain[None],
        w_all, hidden_in, ffn_gain[None],
    )
    outgoing = dispatch(rank, normed)
    arrived = lax.all_to_all(outgoing, both, split_axis=0, concat_axis=0, tiled=True)
    result = expert_ffn(arrived, gate_up, down_proj)
    returned = lax.all_to_all(result, both, split_axis=0, concat_axis=0, tiled=True)
    return combine(rank, wt, returned, merged)


def solution(mesh):
    tok = P(("dp", "seq"), None)
    in_specs = (
        tok, tok, tok, tok, tok, P(), P(), P(), P(), P("seq", None), P(), tok, tok,
        P(("dp", "seq"), None, None), P(("dp", "seq"), None, None), P("dp", None),
    )
    return jax.shard_map(body, mesh=mesh, in_specs=in_specs, out_specs=tok, check_vma=False)
```

```python
import functools

import jax
import jax.numpy as jnp
from jax import lax
from jax.experimental import pallas as pl
from jax.experimental.pallas import tpu as pltpu
from jax.sharding import PartitionSpec as P

D = 2048
HEADS = 64
HEADDIM = 64
STATE = 128
GROUPS = 8
HPG = HEADS // GROUPS
CH = HPG * HEADDIM
FF = 768
TOP = 8
TOK = 256
EXPERTS = 128
EPS = 1e-05
MAIN = 8
ROWS = 72
QW = 256
NQ = 8
SB = 32
BIG = 58

f32 = jnp.float32
bf16 = jnp.bfloat16


def params(limit_mib, n=1):
    return pltpu.CompilerParams(
        vmem_limit_bytes=limit_mib << 20, dimension_semantics=("arbitrary",) * n
    )


def mm(a, b):
    return jnp.dot(a, b, preferred_element_type=f32)


def mm_t(a, b, da, db):
    return lax.dot_general(a, b, (((da,), (db,)), ((), ())), preferred_element_type=f32)


def split2(v):
    hi = v.astype(bf16)
    lo = (v - hi.astype(f32)).astype(bf16)
    return hi, lo


def spread(v, e):
    hi, lo = split2(v)
    return mm(hi, e) + mm(lo, e)


def head_onehot(g):
    h = lax.broadcasted_iota(jnp.int32, (HEADS, CH), 0)
    c = lax.broadcasted_iota(jnp.int32, (HEADS, CH), 1)
    return (h == g * HPG + c // HEADDIM).astype(f32).astype(bf16)


def segments(s_ref, shape, dim):
    return segment_at(s_ref, s_ref[3] + lax.broadcasted_iota(jnp.int32, shape, dim))


def segment_at(s_ref, pos):
    b0 = s_ref[0]
    b1 = b0 + s_ref[1]
    b2 = b1 + s_ref[2]
    return sum((pos >= b).astype(jnp.int32) for b in (b0, b1, b2))


def segment_before(s_ref, start):
    return jnp.where(start == 0, -1, segment_at(s_ref, start - 1))


def state_kernel(s_ref, raw_ref, bias_ref, rate_ref, x_ref, p_ref, fresh_ref, cum_ref, xs_ref, a_s, e_s):
    g = pl.program_id(0)

    @pl.when(g == 0)
    def _():
        v = raw_ref[...].astype(f32).T + bias_ref[...]
        step = jnp.maximum(v, 0.0) + jnp.log(1.0 + jnp.exp(-jnp.abs(v)))
        logd = -step * rate_ref[...] * (1.0 / 2048.0)
        r = lax.broadcasted_iota(jnp.int32, (TOK, TOK), 0)
        c = lax.broadcasted_iota(jnp.int32, (TOK, TOK), 1)
        tri = (r >= c).astype(f32)
        cum = jnp.dot(tri, logd, preferred_element_type=f32, precision=lax.Precision.HIGHEST)
        cum_ref[...] = cum
        a_s[...] = step * jnp.exp(-cum)
        e_s[...] = jnp.exp(cum[TOK - 8 :, :])

    e = head_onehot(g)
    xs = (x_ref[...].astype(f32) * spread(a_s[...], e)).astype(bf16)
    xs_ref[...] = xs
    last = segment_at(s_ref, s_ref[3] + TOK - 1)
    b = jnp.where(segments(s_ref, (TOK, STATE), 0) == last, p_ref[:, :STATE].astype(f32), 0.0).astype(bf16)
    end = spread(e_s[...], e)[7:8, :]
    fresh_ref[0, :STATE, :] = (mm_t(b, xs, 0, 0) * end).astype(bf16)
    hi = end.astype(bf16).astype(f32)
    row = lax.broadcasted_iota(jnp.int32, (16, CH), 0)
    tail = jnp.where(row == 0, hi, jnp.where(row == 1, end - hi, 0.0))
    fresh_ref[0, STATE:, :] = tail.astype(bf16)


def span_states(scal, raw, bias, rate, x, p):
    smem = pl.BlockSpec(memory_space=pltpu.SMEM)
    return pl.pallas_call(
        state_kernel,
        grid=(GROUPS,),
        in_specs=[
            smem,
            pl.BlockSpec((HEADS, TOK), lambda g: (0, 0)),
            pl.BlockSpec((1, HEADS), lambda g: (0, 0)),
            pl.BlockSpec((1, HEADS), lambda g: (0, 0)),
            pl.BlockSpec((TOK, CH), lambda g: (0, g)),
            pl.BlockSpec((TOK, 2 * STATE), lambda g: (0, g)),
        ],
        out_specs=[
            pl.BlockSpec((1, STATE + 16, CH), lambda g: (g, 0, 0)),
            pl.BlockSpec((TOK, HEADS), lambda g: (0, 0)),
            pl.BlockSpec((TOK, CH), lambda g: (0, g)),
        ],
        out_shape=[
            jax.ShapeDtypeStruct((GROUPS, STATE + 16, CH), bf16),
            jax.ShapeDtypeStruct((TOK, HEADS), f32),
            jax.ShapeDtypeStruct((TOK, HEADS * HEADDIM), bf16),
        ],
        scratch_shapes=[pltpu.VMEM((TOK, HEADS), f32), pltpu.VMEM((8, HEADS), f32)],
        compiler_params=params(BIG),
        name="span_states",
    )(scal, raw, bias, rate, x, p)


def prefix_kernel(s_ref, in_ref, out_ref):
    carry = jnp.zeros((STATE, CH), f32)
    for r in range(8):
        out_ref[r] = carry.astype(bf16)
        tail = in_ref[r, STATE:, :].astype(f32)
        keep = tail[0:1, :] + tail[1:2, :]
        start = r * TOK
        same = segment_at(s_ref, start + TOK - 1) == segment_before(s_ref, jnp.int32(start))
        keep = keep * same.astype(f32)
        carry = carry * keep + in_ref[r, :STATE, :].astype(f32)


def prefix(scal, fresh):
    return pl.pallas_call(
        prefix_kernel,
        in_specs=[pl.BlockSpec(memory_space=pltpu.SMEM), pl.BlockSpec(memory_space=pltpu.VMEM)],
        out_specs=pl.BlockSpec(memory_space=pltpu.VMEM),
        out_shape=jax.ShapeDtypeStruct((8, STATE, CH), bf16),
        compiler_params=pltpu.CompilerParams(vmem_limit_bytes=16 << 20),
        name="span_prefix",
    )(scal, fresh)


def mixer_kernel(s_ref, x_ref, z_ref, p_ref, xs_ref, cum_ref, carry_ref, skip_ref, gain_ref, n_ref):
    g = pl.program_id(0)
    e = head_onehot(g)
    b, c = p_ref[:, :STATE], p_ref[:, STATE:]
    scores = mm_t(c, b, 1, 1)
    i = lax.broadcasted_iota(jnp.int32, (TOK, TOK), 0)
    j = lax.broadcasted_iota(jnp.int32, (TOK, TOK), 1)
    ok = (i >= j) & (segments(s_ref, (TOK, TOK), 0) == segments(s_ref, (TOK, TOK), 1))
    m = jnp.where(ok, scores, 0.0).astype(bf16)
    before = segment_before(s_ref, s_ref[3])
    cl = jnp.where(segments(s_ref, (TOK, STATE), 0) == before, c.astype(f32), 0.0).astype(bf16)
    acc = mm(m, xs_ref[...]) + mm(cl, carry_ref[0])
    x = x_ref[...].astype(f32)
    skip = spread(jnp.broadcast_to(skip_ref[...], (8, HEADS)), e)[0:1, :]
    mixed = acc * spread(jnp.exp(cum_ref[...]), e) + skip * x
    z = z_ref[...].astype(f32)
    u = mixed * (z / (1.0 + jnp.exp(-z)))
    ms = jnp.mean(u * u, axis=-1, keepdims=True)
    n_ref[...] = (u * lax.rsqrt(ms + EPS) * gain_ref[...]).astype(bf16)


def mixer(scal, x, z, p, xs, cum, carry, skip, gain):
    fixed = lambda g: (0, 0)
    col = lambda g: (0, g)
    return pl.pallas_call(
        mixer_kernel,
        grid=(GROUPS,),
        in_specs=[
            pl.BlockSpec(memory_space=pltpu.SMEM),
            pl.BlockSpec((TOK, CH), col),
            pl.BlockSpec((TOK, CH), col),
            pl.BlockSpec((TOK, 2 * STATE), col),
            pl.BlockSpec((TOK, CH), col),
            pl.BlockSpec((TOK, HEADS), fixed),
            pl.BlockSpec((1, STATE, CH), lambda g: (g, 0, 0)),
            pl.BlockSpec((1, HEADS), fixed),
            pl.BlockSpec((1, CH), col),
        ],
        out_specs=pl.BlockSpec((TOK, CH), col),
        out_shape=jax.ShapeDtypeStruct((TOK, HEADS * HEADDIM), bf16),
        compiler_params=params(BIG),
        cost_estimate=pl.CostEstimate(flops=1 << 31, bytes_accessed=10 << 20, transcendentals=1 << 21),
        name="mixer",
    )(scal, x, z, p, xs, cum, carry, skip, gain)


def project_kernel(n_ref, w_ref, hid_ref, fgain_ref, merged_ref, normed_ref, acc_ref):
    g = pl.program_id(0)
    part = mm(n_ref[...], w_ref[...].reshape(CH, D))

    @pl.when(g == 0)
    def _():
        acc_ref[...] = part

    @pl.when(g > 0)
    def _():
        acc_ref[...] += part

    @pl.when(g == GROUPS - 1)
    def _():
        merged = (hid_ref[...].astype(f32) + acc_ref[...]).astype(bf16)
        merged_ref[...] = merged
        mf = merged.astype(f32)
        sq = jnp.mean(mf * mf, axis=-1, keepdims=True)
        normed_ref[...] = (mf * lax.rsqrt(sq + EPS) * fgain_ref[...]).astype(bf16)


def project(n, w, hid, fgain):
    fixed = lambda g: (0, 0)
    return pl.pallas_call(
        project_kernel,
        grid=(GROUPS,),
        in_specs=[
            pl.BlockSpec((TOK, CH), lambda g: (0, g)),
            pl.BlockSpec((16, 1, CH // 16, D), lambda g: (0, g, 0, 0)),
            pl.BlockSpec((TOK, D), fixed),
            pl.BlockSpec((1, D), fixed),
        ],
        out_specs=[pl.BlockSpec((TOK, D), fixed), pl.BlockSpec((TOK, D), fixed)],
        out_shape=[jax.ShapeDtypeStruct((TOK, D), bf16)] * 2,
        scratch_shapes=[pltpu.VMEM((TOK, D), f32)],
        compiler_params=params(BIG),
        cost_estimate=pl.CostEstimate(flops=1 << 32, bytes_accessed=22 << 20, transcendentals=0),
        name="project",
    )(n, w, hid, fgain)


def route_kernel(ids_ref, rw_ref, rank_ref, wt_ref):
    e = lax.broadcasted_iota(jnp.int32, (EXPERTS, TOK), 0)
    member = jnp.zeros((EXPERTS, TOK), f32)
    weight = jnp.zeros((EXPERTS, TOK), f32)
    for k in range(TOP):
        hit = ids_ref[k : k + 1, :] == e
        member += jnp.where(hit, 1.0, 0.0)
        weight += jnp.where(hit, rw_ref[k : k + 1, :], 0.0)
    r = lax.broadcasted_iota(jnp.int32, (TOK, TOK), 0)
    c = lax.broadcasted_iota(jnp.int32, (TOK, TOK), 1)
    before = (r < c).astype(f32).astype(bf16)
    rank = mm(member.astype(bf16), before)
    rank_ref[...] = jnp.where(member > 0.5, rank, -1.0)
    wt_ref[...] = weight


def route_tables(ids_t, rw_t):
    vm = pl.BlockSpec(memory_space=pltpu.VMEM)
    return pl.pallas_call(
        route_kernel,
        in_specs=[vm, vm],
        out_specs=[vm, vm],
        out_shape=[jax.ShapeDtypeStruct((EXPERTS, TOK), f32)] * 2,
        name="route_tables",
    )(ids_t, rw_t)


def over_perm(transposed=False):
    n = SB * NQ
    r = lax.broadcasted_iota(jnp.int32, (n, n), 1 if transposed else 0)
    c = lax.broadcasted_iota(jnp.int32, (n, n), 0 if transposed else 1)
    return (c == (r % SB) * NQ + r // SB).astype(f32).astype(bf16)


def unpack(ref):
    n = SB * NQ
    over = mm(over_perm(), ref[:, NQ * MAIN :, :].reshape(n, QW)).astype(bf16)
    parts = []
    for q in range(NQ):
        main = ref[:, q * MAIN : (q + 1) * MAIN, :].reshape(SB * MAIN, QW)
        parts.append(jnp.concatenate([main, over[q * SB : (q + 1) * SB]], axis=0))
    return jnp.concatenate(parts, axis=1)


def pack(ref, rows):
    n = SB * MAIN
    for q in range(NQ):
        ref[:, q * MAIN : (q + 1) * MAIN, :] = (
            rows[:n, q * QW : (q + 1) * QW].reshape(SB, MAIN, QW).astype(bf16)
        )
    over = jnp.concatenate([rows[n:, q * QW : (q + 1) * QW] for q in range(NQ)], axis=0)
    over = mm(over_perm(True), over.astype(bf16))
    ref[:, NQ * MAIN :, :] = over.reshape(SB, NQ, QW).astype(bf16)


def slot_hits(rank, half):
    r3 = jnp.broadcast_to(rank[:, None, :], (SB, MAIN, TOK))
    c = lax.broadcasted_iota(jnp.int32, (SB, MAIN, TOK), 1) + half * MAIN
    main = (r3 == c.astype(f32)).reshape(SB * MAIN, TOK)
    return main, rank == float(2 * MAIN + half)


def dispatch_kernel(half, rank_ref, x_ref, out_ref):
    main, over = slot_hits(rank_ref[...], half)
    hit = jnp.concatenate([main.astype(f32), over.astype(f32)], axis=0).astype(bf16)
    pack(out_ref, mm(hit, x_ref[...]))


def dispatch(rank, normed, half):
    return pl.pallas_call(
        functools.partial(dispatch_kernel, half),
        grid=(EXPERTS // SB,),
        in_specs=[
            pl.BlockSpec((SB, TOK), lambda i: (i, 0)),
            pl.BlockSpec((TOK, D), lambda i: (0, 0)),
        ],
        out_specs=pl.BlockSpec((SB, ROWS, QW), lambda i: (i, 0, 0)),
        out_shape=jax.ShapeDtypeStruct((EXPERTS, ROWS, QW), bf16),
        compiler_params=params(BIG),
        cost_estimate=pl.CostEstimate(flops=1 << 31, bytes_accessed=6 << 20, transcendentals=0),
        name="dispatch",
    )(rank, normed)


def expert_kernel(in_ref, gu_ref, dn_ref, out_ref):
    hidden = mm(unpack(in_ref), gu_ref[0])
    gate = hidden[:, :FF]
    active = (gate / (1.0 + jnp.exp(-gate)) * hidden[:, FF:]).astype(bf16)
    pack(out_ref, mm(active, dn_ref[0]))


def expert_ffn(arrived, gate_up, down):
    n = arrived.shape[0]
    return pl.pallas_call(
        expert_kernel,
        grid=(n // SB,),
        in_specs=[
            pl.BlockSpec((SB, ROWS, QW), lambda i: (i, 0, 0)),
            pl.BlockSpec((1, D, 2 * FF), lambda i: (0, 0, 0), pipeline_mode=pl.Buffered(1)),
            pl.BlockSpec((1, FF, D), lambda i: (0, 0, 0), pipeline_mode=pl.Buffered(1)),
        ],
        out_specs=pl.BlockSpec((SB, ROWS, QW), lambda i: (i, 0, 0)),
        out_shape=jax.ShapeDtypeStruct(arrived.shape, bf16),
        compiler_params=params(BIG),
        cost_estimate=pl.CostEstimate(flops=11 << 30, bytes_accessed=20 << 20, transcendentals=1 << 20),
        name="expert_ffn",
    )(arrived, gate_up, down)


def combine_kernel(half, last, rank_ref, wt_ref, ret_ref, base_ref, out_ref, acc_ref):
    i = pl.program_id(0)

    @pl.when(i == 0)
    def _():
        acc_ref[...] = base_ref[...].astype(f32)

    main, over = slot_hits(rank_ref[...], half)
    wt = wt_ref[...]
    wm = jnp.broadcast_to(wt[:, None, :], (SB, MAIN, TOK)).reshape(SB * MAIN, TOK)
    w = jnp.concatenate([jnp.where(main, wm, 0.0), jnp.where(over, wt, 0.0)], axis=0)
    acc_ref[...] += mm_t(w.astype(bf16), unpack(ret_ref), 0, 0)

    @pl.when(i == pl.num_programs(0) - 1)
    def _():
        out_ref[...] = acc_ref[...].astype(out_ref.dtype)


def combine(rank, wt, returned, base, half, last):
    return pl.pallas_call(
        functools.partial(combine_kernel, half, last),
        grid=(EXPERTS // SB,),
        in_specs=[
            pl.BlockSpec((SB, TOK), lambda i: (i, 0)),
            pl.BlockSpec((SB, TOK), lambda i: (i, 0)),
            pl.BlockSpec((SB, ROWS, QW), lambda i: (i, 0, 0)),
            pl.BlockSpec((TOK, D), lambda i: (0, 0)),
        ],
        out_specs=pl.BlockSpec((TOK, D), lambda i: (0, 0)),
        out_shape=jax.ShapeDtypeStruct((TOK, D), bf16 if last else f32),
        scratch_shapes=[pltpu.VMEM((TOK, D), f32)],
        compiler_params=params(BIG),
        cost_estimate=pl.CostEstimate(flops=1 << 32, bytes_accessed=9 << 20, transcendentals=0),
        name="combine",
    )(rank, wt, returned, base)


def body(
    hidden_in, mix_values, mix_gate, state_proj, step_raw, step_bias, decay_rate, skip_gain,
    norm_gain, out_weight, ffn_gain, expert_ids, route_weights, gate_up, down_proj, doc_lengths,
):
    both = ("dp", "seq")
    seq_rank = lax.axis_index("seq")
    dp_rank = lax.axis_index("dp")
    scal = jnp.concatenate([doc_lengths[0], (seq_rank * TOK).astype(jnp.int32)[None]])

    share = out_weight.shape[0] // 16
    w_mine = lax.dynamic_slice_in_dim(out_weight, dp_rank * share, share)
    w_all = lax.all_gather(w_mine, both, axis=0, tiled=True).reshape(16, GROUPS, share, D)

    rank, wt = route_tables(expert_ids.T, route_weights.T)
    fresh, cum, xs = span_states(
        scal, step_raw.T, step_bias[None], decay_rate[None], mix_values, state_proj
    )
    fresh = lax.all_to_all(fresh, "seq", split_axis=0, concat_axis=0, tiled=True)
    carry = prefix(scal, fresh)
    carry = lax.all_to_all(carry, "seq", split_axis=0, concat_axis=0, tiled=True)
    normed_mix = mixer(
        scal, mix_values, mix_gate, state_proj, xs, cum, carry, skip_gain[None], norm_gain[None]
    )
    merged, normed = project(normed_mix, w_all, hidden_in, ffn_gain[None])
    def exchange(v):
        return lax.all_to_all(v, both, split_axis=0, concat_axis=0, tiled=True)

    arrived = [exchange(dispatch(rank, normed, h)) for h in range(2)]
    returned = [exchange(expert_ffn(a, gate_up, down_proj)) for a in arrived]
    partial = combine(rank, wt, returned[0], merged, 0, False)
    return combine(rank, wt, returned[1], partial, 1, True)


def solution(mesh):
    tok = P(("dp", "seq"), None)
    in_specs = (
        tok, tok, tok, tok, tok, P(), P(), P(), P(), P("seq", None), P(), tok, tok,
        P(("dp", "seq"), None, None), P(("dp", "seq"), None, None), P("dp", None),
    )
    return jax.shard_map(body, mesh=mesh, in_specs=in_specs, out_specs=tok, check_vma=False)
```

```python
import functools

import jax
import jax.numpy as jnp
from jax import lax
from jax.experimental import pallas as pl
from jax.experimental.pallas import tpu as pltpu
from jax.sharding import PartitionSpec as P

D = 2048
HEADS = 64
HEADDIM = 64
STATE = 128
GROUPS = 8
HPG = HEADS // GROUPS
CH = HPG * HEADDIM
FF = 768
TOP = 8
TOK = 256
EXPERTS = 128
EPS = 1e-05
MAIN = 8
ROWS = 72
QW = 256
NQ = 8
SB = 32
BIG = 58
BLOCKS = EXPERTS // SB
STREAMS = 4

f32 = jnp.float32
bf16 = jnp.bfloat16


def params(limit_mib, n=1):
    return pltpu.CompilerParams(
        vmem_limit_bytes=limit_mib << 20, dimension_semantics=("arbitrary",) * n
    )


def mm(a, b):
    return jnp.dot(a, b, preferred_element_type=f32)


def mm_t(a, b, da, db):
    return lax.dot_general(a, b, (((da,), (db,)), ((), ())), preferred_element_type=f32)


def split2(v):
    hi = v.astype(bf16)
    lo = (v - hi.astype(f32)).astype(bf16)
    return hi, lo


def spread(v, e):
    hi, lo = split2(v)
    return mm(hi, e) + mm(lo, e)


def head_onehot(g):
    h = lax.broadcasted_iota(jnp.int32, (HEADS, CH), 0)
    c = lax.broadcasted_iota(jnp.int32, (HEADS, CH), 1)
    return (h == g * HPG + c // HEADDIM).astype(f32).astype(bf16)


def segments(s_ref, shape, dim):
    return segment_at(s_ref, s_ref[3] + lax.broadcasted_iota(jnp.int32, shape, dim))


def segment_at(s_ref, pos):
    b0 = s_ref[0]
    b1 = b0 + s_ref[1]
    b2 = b1 + s_ref[2]
    return sum((pos >= b).astype(jnp.int32) for b in (b0, b1, b2))


def segment_before(s_ref, start):
    return jnp.where(start == 0, -1, segment_at(s_ref, start - 1))


def state_kernel(s_ref, raw_ref, bias_ref, rate_ref, x_ref, p_ref, fresh_ref, cum_ref, xs_ref, a_s, e_s):
    g = pl.program_id(0)

    @pl.when(g == 0)
    def _():
        v = raw_ref[...].astype(f32).T + bias_ref[...]
        step = jnp.maximum(v, 0.0) + jnp.log(1.0 + jnp.exp(-jnp.abs(v)))
        logd = -step * rate_ref[...] * (1.0 / 2048.0)
        r = lax.broadcasted_iota(jnp.int32, (TOK, TOK), 0)
        c = lax.broadcasted_iota(jnp.int32, (TOK, TOK), 1)
        tri = (r >= c).astype(f32)
        cum = jnp.dot(tri, logd, preferred_element_type=f32, precision=lax.Precision.HIGHEST)
        cum_ref[...] = cum
        a_s[...] = step * jnp.exp(-cum)
        e_s[...] = jnp.exp(cum[TOK - 8 :, :])

    e = head_onehot(g)
    xs = (x_ref[...].astype(f32) * spread(a_s[...], e)).astype(bf16)
    xs_ref[...] = xs
    last = segment_at(s_ref, s_ref[3] + TOK - 1)
    b = jnp.where(segments(s_ref, (TOK, STATE), 0) == last, p_ref[:, :STATE].astype(f32), 0.0).astype(bf16)
    end = spread(e_s[...], e)[7:8, :]
    fresh_ref[0, :STATE, :] = (mm_t(b, xs, 0, 0) * end).astype(bf16)
    hi = end.astype(bf16).astype(f32)
    row = lax.broadcasted_iota(jnp.int32, (16, CH), 0)
    tail = jnp.where(row == 0, hi, jnp.where(row == 1, end - hi, 0.0))
    fresh_ref[0, STATE:, :] = tail.astype(bf16)


def span_states(scal, raw, bias, rate, x, p):
    smem = pl.BlockSpec(memory_space=pltpu.SMEM)
    return pl.pallas_call(
        state_kernel,
        grid=(GROUPS,),
        in_specs=[
            smem,
            pl.BlockSpec((HEADS, TOK), lambda g: (0, 0)),
            pl.BlockSpec((1, HEADS), lambda g: (0, 0)),
            pl.BlockSpec((1, HEADS), lambda g: (0, 0)),
            pl.BlockSpec((TOK, CH), lambda g: (0, g)),
            pl.BlockSpec((TOK, 2 * STATE), lambda g: (0, g)),
        ],
        out_specs=[
            pl.BlockSpec((1, STATE + 16, CH), lambda g: (g, 0, 0)),
            pl.BlockSpec((TOK, HEADS), lambda g: (0, 0)),
            pl.BlockSpec((TOK, CH), lambda g: (0, g)),
        ],
        out_shape=[
            jax.ShapeDtypeStruct((GROUPS, STATE + 16, CH), bf16),
            jax.ShapeDtypeStruct((TOK, HEADS), f32),
            jax.ShapeDtypeStruct((TOK, HEADS * HEADDIM), bf16),
        ],
        scratch_shapes=[pltpu.VMEM((TOK, HEADS), f32), pltpu.VMEM((8, HEADS), f32)],
        compiler_params=params(BIG),
        name="span_states",
    )(scal, raw, bias, rate, x, p)


def prefix_kernel(s_ref, in_ref, out_ref):
    carry = jnp.zeros((STATE, CH), f32)
    for r in range(8):
        out_ref[r] = carry.astype(bf16)
        tail = in_ref[r, STATE:, :].astype(f32)
        keep = tail[0:1, :] + tail[1:2, :]
        start = r * TOK
        same = segment_at(s_ref, start + TOK - 1) == segment_before(s_ref, jnp.int32(start))
        keep = keep * same.astype(f32)
        carry = carry * keep + in_ref[r, :STATE, :].astype(f32)


def prefix(scal, fresh):
    return pl.pallas_call(
        prefix_kernel,
        in_specs=[pl.BlockSpec(memory_space=pltpu.SMEM), pl.BlockSpec(memory_space=pltpu.VMEM)],
        out_specs=pl.BlockSpec(memory_space=pltpu.VMEM),
        out_shape=jax.ShapeDtypeStruct((8, STATE, CH), bf16),
        compiler_params=pltpu.CompilerParams(vmem_limit_bytes=16 << 20),
        name="span_prefix",
    )(scal, fresh)


def mixer_kernel(s_ref, x_ref, z_ref, p_ref, xs_ref, cum_ref, carry_ref, skip_ref, gain_ref, n_ref):
    g = pl.program_id(0)
    e = head_onehot(g)
    b, c = p_ref[:, :STATE], p_ref[:, STATE:]
    scores = mm_t(c, b, 1, 1)
    i = lax.broadcasted_iota(jnp.int32, (TOK, TOK), 0)
    j = lax.broadcasted_iota(jnp.int32, (TOK, TOK), 1)
    ok = (i >= j) & (segments(s_ref, (TOK, TOK), 0) == segments(s_ref, (TOK, TOK), 1))
    m = jnp.where(ok, scores, 0.0).astype(bf16)
    before = segment_before(s_ref, s_ref[3])
    cl = jnp.where(segments(s_ref, (TOK, STATE), 0) == before, c.astype(f32), 0.0).astype(bf16)
    acc = mm(m, xs_ref[...]) + mm(cl, carry_ref[0])
    x = x_ref[...].astype(f32)
    skip = spread(jnp.broadcast_to(skip_ref[...], (8, HEADS)), e)[0:1, :]
    mixed = acc * spread(jnp.exp(cum_ref[...]), e) + skip * x
    z = z_ref[...].astype(f32)
    u = mixed * (z / (1.0 + jnp.exp(-z)))
    ms = jnp.mean(u * u, axis=-1, keepdims=True)
    n_ref[...] = (u * lax.rsqrt(ms + EPS) * gain_ref[...]).astype(bf16)


def mixer(scal, x, z, p, xs, cum, carry, skip, gain):
    fixed = lambda g: (0, 0)
    col = lambda g: (0, g)
    return pl.pallas_call(
        mixer_kernel,
        grid=(GROUPS,),
        in_specs=[
            pl.BlockSpec(memory_space=pltpu.SMEM),
            pl.BlockSpec((TOK, CH), col),
            pl.BlockSpec((TOK, CH), col),
            pl.BlockSpec((TOK, 2 * STATE), col),
            pl.BlockSpec((TOK, CH), col),
            pl.BlockSpec((TOK, HEADS), fixed),
            pl.BlockSpec((1, STATE, CH), lambda g: (g, 0, 0)),
            pl.BlockSpec((1, HEADS), fixed),
            pl.BlockSpec((1, CH), col),
        ],
        out_specs=pl.BlockSpec((TOK, CH), col),
        out_shape=jax.ShapeDtypeStruct((TOK, HEADS * HEADDIM), bf16),
        compiler_params=params(BIG),
        cost_estimate=pl.CostEstimate(flops=1 << 31, bytes_accessed=10 << 20, transcendentals=1 << 21),
        name="mixer",
    )(scal, x, z, p, xs, cum, carry, skip, gain)


def project_kernel(n_ref, *refs):
    w_refs, (hid_ref, fgain_ref, hit_ref, merged_ref, normed_ref, out_ref, acc_ref) = refs[:STREAMS], refs[STREAMS:]
    g = pl.program_id(0)

    @pl.when(g < GROUPS)
    def _():
        w = jnp.concatenate([r[...].reshape(CH // STREAMS, D) for r in w_refs], axis=0)
        part = mm(n_ref[...], w)

        @pl.when(g == 0)
        def _():
            acc_ref[...] = part

        @pl.when(g > 0)
        def _():
            acc_ref[...] += part

    @pl.when(g == GROUPS - 1)
    def _():
        merged = (hid_ref[...].astype(f32) + acc_ref[...]).astype(bf16)
        merged_ref[...] = merged
        mf = merged.astype(f32)
        sq = jnp.mean(mf * mf, axis=-1, keepdims=True)
        normed_ref[...] = (mf * lax.rsqrt(sq + EPS) * fgain_ref[...]).astype(bf16)

    @pl.when(g >= GROUPS)
    def _():
        pack(out_ref, mm(hit_ref[0], normed_ref[...]))


def project(n, w, hid, fgain, hit):
    fixed = lambda g: (0, 0)
    block = lambda g: (jnp.maximum(g - GROUPS, 0), 0, 0)
    group = lambda g: jnp.minimum(g, GROUPS - 1)
    part = 16 // STREAMS
    return pl.pallas_call(
        project_kernel,
        grid=(GROUPS + BLOCKS,),
        in_specs=[pl.BlockSpec((TOK, CH), lambda g: (0, group(g)))]
        + [
            pl.BlockSpec((part, 1, CH // 16, D), lambda g, i=i: (i, group(g), 0, 0))
            for i in range(STREAMS)
        ]
        + [
            pl.BlockSpec((TOK, D), fixed),
            pl.BlockSpec((1, D), fixed),
            pl.BlockSpec((1, SB * MAIN + SB, TOK), block),
        ],
        out_specs=[
            pl.BlockSpec((TOK, D), fixed),
            pl.BlockSpec((TOK, D), fixed),
            pl.BlockSpec((SB, ROWS, QW), block),
        ],
        out_shape=[jax.ShapeDtypeStruct((TOK, D), bf16)] * 2
        + [jax.ShapeDtypeStruct((EXPERTS, ROWS, QW), bf16)],
        scratch_shapes=[pltpu.VMEM((TOK, D), f32)],
        compiler_params=params(BIG),
        cost_estimate=pl.CostEstimate(flops=6 << 30, bytes_accessed=28 << 20, transcendentals=0),
        name="project",
    )(n, *[w] * STREAMS, hid, fgain, hit)


def slot_hits(rank, half):
    r3 = jnp.broadcast_to(rank[:, None, :], (SB, MAIN, TOK))
    c = lax.broadcasted_iota(jnp.int32, (SB, MAIN, TOK), 1) + half * MAIN
    main = (r3 == c.astype(f32)).reshape(SB * MAIN, TOK)
    return main, rank == float(2 * MAIN + half)


def route_kernel(ids_ref, rw_ref, hit_ref, wgt_ref):
    e = lax.broadcasted_iota(jnp.int32, (EXPERTS, TOK), 0)
    member = jnp.zeros((EXPERTS, TOK), f32)
    weight = jnp.zeros((EXPERTS, TOK), f32)
    for k in range(TOP):
        hit = ids_ref[k : k + 1, :] == e
        member += jnp.where(hit, 1.0, 0.0)
        weight += jnp.where(hit, rw_ref[k : k + 1, :], 0.0)
    r = lax.broadcasted_iota(jnp.int32, (TOK, TOK), 0)
    c = lax.broadcasted_iota(jnp.int32, (TOK, TOK), 1)
    before = (r < c).astype(f32).astype(bf16)
    rank = jnp.where(member > 0.5, mm(member.astype(bf16), before), -1.0)
    for half in range(2):
        for i in range(BLOCKS):
            rows = slice(i * SB, (i + 1) * SB)
            main, over = slot_hits(rank[rows], half)
            wt = weight[rows]
            wm = jnp.broadcast_to(wt[:, None, :], (SB, MAIN, TOK)).reshape(SB * MAIN, TOK)
            hit = jnp.concatenate([main.astype(f32), over.astype(f32)], axis=0)
            hit_ref[half, i] = hit.astype(bf16)
            w = hit * jnp.concatenate([wm, wt], axis=0)
            wgt_ref[half, i] = w.T.astype(bf16)


def route_tables(ids_t, rw_t):
    vm = pl.BlockSpec(memory_space=pltpu.VMEM)
    n = SB * MAIN + SB
    return pl.pallas_call(
        route_kernel,
        in_specs=[vm, vm],
        out_specs=[vm, vm],
        out_shape=[
            jax.ShapeDtypeStruct((2, BLOCKS, n, TOK), bf16),
            jax.ShapeDtypeStruct((2, BLOCKS, TOK, n), bf16),
        ],
        compiler_params=pltpu.CompilerParams(vmem_limit_bytes=32 << 20),
        cost_estimate=pl.CostEstimate(flops=1 << 28, bytes_accessed=3 << 20, transcendentals=0),
        name="route_tables",
    )(ids_t, rw_t)


def over_perm(transposed=False):
    n = SB * NQ
    r = lax.broadcasted_iota(jnp.int32, (n, n), 1 if transposed else 0)
    c = lax.broadcasted_iota(jnp.int32, (n, n), 0 if transposed else 1)
    return (c == (r % SB) * NQ + r // SB).astype(f32).astype(bf16)


def unpack(ref):
    n = SB * NQ
    over = mm(over_perm(), ref[:, NQ * MAIN :, :].reshape(n, QW)).astype(bf16)
    parts = []
    for q in range(NQ):
        main = ref[:, q * MAIN : (q + 1) * MAIN, :].reshape(SB * MAIN, QW)
        parts.append(jnp.concatenate([main, over[q * SB : (q + 1) * SB]], axis=0))
    return jnp.concatenate(parts, axis=1)


def pack(ref, rows):
    n = SB * MAIN
    for q in range(NQ):
        ref[:, q * MAIN : (q + 1) * MAIN, :] = (
            rows[:n, q * QW : (q + 1) * QW].reshape(SB, MAIN, QW).astype(bf16)
        )
    over = jnp.concatenate([rows[n:, q * QW : (q + 1) * QW] for q in range(NQ)], axis=0)
    over = mm(over_perm(True), over.astype(bf16))
    ref[:, NQ * MAIN :, :] = over.reshape(SB, NQ, QW).astype(bf16)


def dispatch_kernel(hit_ref, x_ref, out_ref):
    pack(out_ref, mm(hit_ref[0], x_ref[...]))


def dispatch(hit, normed):
    n = SB * MAIN + SB
    return pl.pallas_call(
        dispatch_kernel,
        grid=(BLOCKS,),
        in_specs=[
            pl.BlockSpec((1, n, TOK), lambda i: (i, 0, 0)),
            pl.BlockSpec((TOK, D), lambda i: (0, 0)),
        ],
        out_specs=pl.BlockSpec((SB, ROWS, QW), lambda i: (i, 0, 0)),
        out_shape=jax.ShapeDtypeStruct((EXPERTS, ROWS, QW), bf16),
        compiler_params=params(BIG),
        cost_estimate=pl.CostEstimate(flops=1 << 31, bytes_accessed=6 << 20, transcendentals=0),
        name="dispatch",
    )(hit, normed)


def expert_kernel(in_ref, gu_ref, dn_ref, out_ref):
    hidden = mm(unpack(in_ref), gu_ref[0])
    gate = hidden[:, :FF]
    active = (gate / (1.0 + jnp.exp(-gate)) * hidden[:, FF:]).astype(bf16)
    pack(out_ref, mm(active, dn_ref[0]))


def expert_ffn(arrived, gate_up, down):
    n = arrived.shape[0]
    return pl.pallas_call(
        expert_kernel,
        grid=(n // SB,),
        in_specs=[
            pl.BlockSpec((SB, ROWS, QW), lambda i: (i, 0, 0)),
            pl.BlockSpec((1, D, 2 * FF), lambda i: (0, 0, 0), pipeline_mode=pl.Buffered(1)),
            pl.BlockSpec((1, FF, D), lambda i: (0, 0, 0), pipeline_mode=pl.Buffered(1)),
        ],
        out_specs=pl.BlockSpec((SB, ROWS, QW), lambda i: (i, 0, 0)),
        out_shape=jax.ShapeDtypeStruct(arrived.shape, bf16),
        compiler_params=params(BIG),
        cost_estimate=pl.CostEstimate(flops=11 << 30, bytes_accessed=20 << 20, transcendentals=1 << 20),
        name="expert_ffn",
    )(arrived, gate_up, down)


def combine_kernel(wgt_ref, ret_ref, base_ref, out_ref, acc_ref):
    i = pl.program_id(0)
    part = mm(wgt_ref[0], unpack(ret_ref))

    @pl.when(i == 0)
    def _():
        acc_ref[...] = part

    @pl.when(i > 0)
    def _():
        acc_ref[...] += part

    cols = pl.ds(pl.multiple_of(i * (D // BLOCKS), D // BLOCKS), D // BLOCKS)
    acc_ref[:, cols] += base_ref[...].astype(f32)

    @pl.when(i == pl.num_programs(0) - 1)
    def _():
        out_ref[...] = acc_ref[...].astype(out_ref.dtype)


def combine(wgt, returned, base, kind):
    n = SB * MAIN + SB
    return pl.pallas_call(
        combine_kernel,
        grid=(BLOCKS,),
        in_specs=[
            pl.BlockSpec((1, TOK, n), lambda i: (i, 0, 0)),
            pl.BlockSpec((SB, ROWS, QW), lambda i: (i, 0, 0)),
            pl.BlockSpec((TOK, D // BLOCKS), lambda i: (0, i)),
        ],
        out_specs=pl.BlockSpec((TOK, D), lambda i: (0, 0)),
        out_shape=jax.ShapeDtypeStruct((TOK, D), kind),
        scratch_shapes=[pltpu.VMEM((TOK, D), f32)],
        compiler_params=params(BIG),
        cost_estimate=pl.CostEstimate(flops=1 << 32, bytes_accessed=9 << 20, transcendentals=0),
        name="combine",
    )(wgt, returned, base)


def body(
    hidden_in, mix_values, mix_gate, state_proj, step_raw, step_bias, decay_rate, skip_gain,
    norm_gain, out_weight, ffn_gain, expert_ids, route_weights, gate_up, down_proj, doc_lengths,
):
    both = ("dp", "seq")
    seq_rank = lax.axis_index("seq")
    dp_rank = lax.axis_index("dp")
    scal = jnp.concatenate([doc_lengths[0], (seq_rank * TOK).astype(jnp.int32)[None]])

    share = out_weight.shape[0] // 16
    w_mine = lax.dynamic_slice_in_dim(out_weight, dp_rank * share, share)
    w_all = lax.all_gather(w_mine, both, axis=0, tiled=True).reshape(16, GROUPS, share, D)

    hit, wgt = route_tables(expert_ids.T, route_weights.T)
    fresh, cum, xs = span_states(
        scal, step_raw.T, step_bias[None], decay_rate[None], mix_values, state_proj
    )
    fresh = lax.all_to_all(fresh, "seq", split_axis=0, concat_axis=0, tiled=True)
    carry = prefix(scal, fresh)
    carry = lax.all_to_all(carry, "seq", split_axis=0, concat_axis=0, tiled=True)
    normed_mix = mixer(
        scal, mix_values, mix_gate, state_proj, xs, cum, carry, skip_gain[None], norm_gain[None]
    )
    merged, normed, first = project(normed_mix, w_all, hidden_in, ffn_gain[None], hit[0])
    def exchange(v):
        return lax.all_to_all(v, both, split_axis=0, concat_axis=0, tiled=True)

    arrived = [exchange(first), exchange(dispatch(hit[1], normed))]
    returned = [exchange(expert_ffn(a, gate_up, down_proj)) for a in arrived]
    partial = combine(wgt[0], returned[0], merged, f32)
    return combine(wgt[1], returned[1], partial, bf16)


def solution(mesh):
    tok = P(("dp", "seq"), None)
    in_specs = (
        tok, tok, tok, tok, tok, P(), P(), P(), P(), P("seq", None), P(), tok, tok,
        P(("dp", "seq"), None, None), P(("dp", "seq"), None, None), P("dp", None),
    )
    return jax.shard_map(body, mesh=mesh, in_specs=in_specs, out_specs=tok, check_vma=False)
```

```python
import functools

import jax
import jax.numpy as jnp
from jax import lax
from jax.experimental import pallas as pl
from jax.experimental.pallas import tpu as pltpu
from jax.sharding import PartitionSpec as P

D = 2048
HEADS = 64
HEADDIM = 64
STATE = 128
GROUPS = 8
HPG = HEADS // GROUPS
CH = HPG * HEADDIM
FF = 768
TOP = 8
TOK = 256
EXPERTS = 128
EPS = 1e-05
MAIN = 8
ROWS = 72
QW = 256
NQ = 8
SB = 32
BIG = 58
BLOCKS = EXPERTS // SB
SLICES = 4
LANES = CH // SLICES
HALF = D // 2

f32 = jnp.float32
bf16 = jnp.bfloat16


def params(limit_mib, n=1):
    return pltpu.CompilerParams(
        vmem_limit_bytes=limit_mib << 20, dimension_semantics=("arbitrary",) * n
    )


def mm(a, b):
    return jnp.dot(a, b, preferred_element_type=f32)


def mm_t(a, b, da, db):
    return lax.dot_general(a, b, (((da,), (db,)), ((), ())), preferred_element_type=f32)


def split2(v):
    hi = v.astype(bf16)
    lo = (v - hi.astype(f32)).astype(bf16)
    return hi, lo


def spread(v, e):
    hi, lo = split2(v)
    return mm(hi, e) + mm(lo, e)


def head_onehot(g):
    h = lax.broadcasted_iota(jnp.int32, (HEADS, CH), 0)
    c = lax.broadcasted_iota(jnp.int32, (HEADS, CH), 1)
    return (h == g * HPG + c // HEADDIM).astype(f32).astype(bf16)


def segments(s_ref, shape, dim):
    return segment_at(s_ref, s_ref[3] + lax.broadcasted_iota(jnp.int32, shape, dim))


def segment_at(s_ref, pos):
    b0 = s_ref[0]
    b1 = b0 + s_ref[1]
    b2 = b1 + s_ref[2]
    return sum((pos >= b).astype(jnp.int32) for b in (b0, b1, b2))


def segment_before(s_ref, start):
    return jnp.where(start == 0, -1, segment_at(s_ref, start - 1))


def state_kernel(s_ref, raw_ref, bias_ref, rate_ref, x_ref, p_ref, fresh_ref, cum_ref, xs_ref, a_s, e_s):
    g = pl.program_id(0)

    @pl.when(g == 0)
    def _():
        v = raw_ref[...].astype(f32).T + bias_ref[...]
        step = jnp.maximum(v, 0.0) + jnp.log(1.0 + jnp.exp(-jnp.abs(v)))
        logd = -step * rate_ref[...] * (1.0 / 2048.0)
        r = lax.broadcasted_iota(jnp.int32, (TOK, TOK), 0)
        c = lax.broadcasted_iota(jnp.int32, (TOK, TOK), 1)
        tri = (r >= c).astype(f32)
        cum = jnp.dot(tri, logd, preferred_element_type=f32, precision=lax.Precision.HIGHEST)
        cum_ref[...] = cum
        a_s[...] = step * jnp.exp(-cum)
        e_s[...] = jnp.exp(cum[TOK - 8 :, :])

    e = head_onehot(g)
    xs = (x_ref[...].astype(f32) * spread(a_s[...], e)).astype(bf16)
    xs_ref[...] = xs
    last = segment_at(s_ref, s_ref[3] + TOK - 1)
    b = jnp.where(segments(s_ref, (TOK, STATE), 0) == last, p_ref[:, :STATE].astype(f32), 0.0).astype(bf16)
    end = spread(e_s[...], e)[7:8, :]
    fresh_ref[0, :STATE, :] = (mm_t(b, xs, 0, 0) * end).astype(bf16)
    hi = end.astype(bf16).astype(f32)
    row = lax.broadcasted_iota(jnp.int32, (16, CH), 0)
    tail = jnp.where(row == 0, hi, jnp.where(row == 1, end - hi, 0.0))
    fresh_ref[0, STATE:, :] = tail.astype(bf16)


def span_states(scal, raw, bias, rate, x, p):
    smem = pl.BlockSpec(memory_space=pltpu.SMEM)
    return pl.pallas_call(
        state_kernel,
        grid=(GROUPS,),
        in_specs=[
            smem,
            pl.BlockSpec((HEADS, TOK), lambda g: (0, 0)),
            pl.BlockSpec((1, HEADS), lambda g: (0, 0)),
            pl.BlockSpec((1, HEADS), lambda g: (0, 0)),
            pl.BlockSpec((TOK, CH), lambda g: (0, g)),
            pl.BlockSpec((TOK, 2 * STATE), lambda g: (0, g)),
        ],
        out_specs=[
            pl.BlockSpec((1, STATE + 16, CH), lambda g: (g, 0, 0)),
            pl.BlockSpec((TOK, HEADS), lambda g: (0, 0)),
            pl.BlockSpec((TOK, CH), lambda g: (0, g)),
        ],
        out_shape=[
            jax.ShapeDtypeStruct((GROUPS, STATE + 16, CH), bf16),
            jax.ShapeDtypeStruct((TOK, HEADS), f32),
            jax.ShapeDtypeStruct((TOK, HEADS * HEADDIM), bf16),
        ],
        scratch_shapes=[pltpu.VMEM((TOK, HEADS), f32), pltpu.VMEM((8, HEADS), f32)],
        compiler_params=params(BIG),
        cost_estimate=pl.CostEstimate(flops=1 << 31, bytes_accessed=30 << 20, transcendentals=1 << 20),
        name="span_states",
    )(scal, raw, bias, rate, x, p)


def prefix_kernel(s_ref, in_ref, out_ref):
    carry = jnp.zeros((STATE, CH), f32)
    for r in range(8):
        out_ref[r] = carry.astype(bf16)
        tail = in_ref[r, STATE:, :].astype(f32)
        keep = tail[0:1, :] + tail[1:2, :]
        start = r * TOK
        same = segment_at(s_ref, start + TOK - 1) == segment_before(s_ref, jnp.int32(start))
        keep = keep * same.astype(f32)
        carry = carry * keep + in_ref[r, :STATE, :].astype(f32)


def prefix(scal, fresh):
    return pl.pallas_call(
        prefix_kernel,
        in_specs=[pl.BlockSpec(memory_space=pltpu.SMEM), pl.BlockSpec(memory_space=pltpu.VMEM)],
        out_specs=pl.BlockSpec(memory_space=pltpu.VMEM),
        out_shape=jax.ShapeDtypeStruct((8, STATE, CH), bf16),
        compiler_params=pltpu.CompilerParams(vmem_limit_bytes=16 << 20),
        name="span_prefix",
    )(scal, fresh)


def mixer_kernel(s_ref, x_ref, z_ref, p_ref, xs_ref, cum_ref, carry_ref, skip_ref, gain_ref, n_ref):
    g = pl.program_id(0)
    e = head_onehot(g)
    b, c = p_ref[:, :STATE], p_ref[:, STATE:]
    scores = mm_t(c, b, 1, 1)
    i = lax.broadcasted_iota(jnp.int32, (TOK, TOK), 0)
    j = lax.broadcasted_iota(jnp.int32, (TOK, TOK), 1)
    ok = (i >= j) & (segments(s_ref, (TOK, TOK), 0) == segments(s_ref, (TOK, TOK), 1))
    m = jnp.where(ok, scores, 0.0).astype(bf16)
    before = segment_before(s_ref, s_ref[3])
    cl = jnp.where(segments(s_ref, (TOK, STATE), 0) == before, c.astype(f32), 0.0).astype(bf16)
    acc = mm(m, xs_ref[...]) + mm(cl, carry_ref[0])
    x = x_ref[...].astype(f32)
    skip = spread(jnp.broadcast_to(skip_ref[...], (8, HEADS)), e)[0:1, :]
    mixed = acc * spread(jnp.exp(cum_ref[...]), e) + skip * x
    z = z_ref[...].astype(f32)
    u = mixed * (z / (1.0 + jnp.exp(-z)))
    ms = jnp.mean(u * u, axis=-1, keepdims=True)
    n = (u * lax.rsqrt(ms + EPS) * gain_ref[...]).astype(bf16)
    for k in range(SLICES):
        n_ref[0, k] = n[:, k * LANES : (k + 1) * LANES]


def mixer(scal, x, z, p, xs, cum, carry, skip, gain):
    fixed = lambda g: (0, 0)
    col = lambda g: (0, g)
    return pl.pallas_call(
        mixer_kernel,
        grid=(GROUPS,),
        in_specs=[
            pl.BlockSpec(memory_space=pltpu.SMEM),
            pl.BlockSpec((TOK, CH), col),
            pl.BlockSpec((TOK, CH), col),
            pl.BlockSpec((TOK, 2 * STATE), col),
            pl.BlockSpec((TOK, CH), col),
            pl.BlockSpec((TOK, HEADS), fixed),
            pl.BlockSpec((1, STATE, CH), lambda g: (g, 0, 0)),
            pl.BlockSpec((1, HEADS), fixed),
            pl.BlockSpec((1, CH), col),
        ],
        out_specs=pl.BlockSpec((1, SLICES, TOK, LANES), lambda g: (g, 0, 0, 0)),
        out_shape=jax.ShapeDtypeStruct((GROUPS, SLICES, TOK, LANES), bf16),
        compiler_params=params(BIG),
        cost_estimate=pl.CostEstimate(flops=1 << 31, bytes_accessed=40 << 20, transcendentals=1 << 21),
        name="mixer",
    )(scal, x, z, p, xs, cum, carry, skip, gain)


def project_kernel(s_ref, mine_ref, theirs_ref, own_ref, *refs):
    w_refs, (keep_ref, send_ref, acc_ref) = refs[:10], refs[10:]
    t = pl.program_id(0)

    def lhs(at):
        parts = []
        for k in range(SLICES):
            j = k if at is None else s_ref[at + k]
            parts.append(jnp.concatenate([mine_ref[0, j], theirs_ref[0, j]], axis=0))
        return jnp.concatenate(parts, axis=1)

    @pl.when(t == 0)
    def _():
        acc_ref[...] = mm(lhs(None), own_ref[...])

    @pl.when(t > 0)
    def _():
        for h in range(2):
            w = jnp.concatenate([r[0] for r in w_refs[5 * h : 5 * h + 5]], axis=0)
            acc_ref[:, h * HALF : (h + 1) * HALF] += mm(lhs(8 + 4 * h), w)

    @pl.when(t == pl.num_programs(0) - 1)
    def _():
        keep_ref[...] = acc_ref[:TOK]
        send_ref[...] = acc_ref[TOK:].astype(bf16)


def project(scal, mine, theirs, own, slices):
    fixed = lambda t, s: (0, 0)
    return pl.pallas_call(
        project_kernel,
        grid_spec=pltpu.PrefetchScalarGridSpec(
            num_scalar_prefetch=1,
            grid=(4,),
            in_specs=[
                pl.BlockSpec((1, SLICES, TOK, LANES), lambda t, s: (s[t], 0, 0, 0)),
                pl.BlockSpec((1, SLICES, TOK, LANES), lambda t, s: (s[4 + t], 0, 0, 0)),
                pl.BlockSpec((CH, D), fixed),
            ]
            + [
                pl.BlockSpec((1, rows, HALF), lambda t, s: (jnp.maximum(t - 1, 0), 0, 0))
                for rows in (LANES, LANES, LANES, LANES // 2, LANES // 2)
            ]
            * 2,
            out_specs=[pl.BlockSpec((TOK, D), fixed), pl.BlockSpec((TOK, D), fixed)],
            scratch_shapes=[pltpu.VMEM((2 * TOK, D), f32)],
        ),
        out_shape=[jax.ShapeDtypeStruct((TOK, D), f32), jax.ShapeDtypeStruct((TOK, D), bf16)],
        compiler_params=params(BIG),
        cost_estimate=pl.CostEstimate(flops=1 << 32, bytes_accessed=14 << 20, transcendentals=0),
        name="project",
    )(scal, mine, theirs, own, *slices)


def merge_kernel(keep_ref, other_ref, hid_ref, fgain_ref, hit_ref, merged_ref, normed_ref, out_ref):
    @pl.when(pl.program_id(0) == 0)
    def _():
        total = keep_ref[...] + other_ref[...].astype(f32)
        merged = (hid_ref[...].astype(f32) + total).astype(bf16)
        merged_ref[...] = merged
        mf = merged.astype(f32)
        sq = jnp.mean(mf * mf, axis=-1, keepdims=True)
        normed_ref[...] = (mf * lax.rsqrt(sq + EPS) * fgain_ref[...]).astype(bf16)

    pack(out_ref, mm(hit_ref[0], normed_ref[...]))


def merge(keep, other, hid, fgain, hit):
    fixed = lambda i: (0, 0)
    return pl.pallas_call(
        merge_kernel,
        grid=(BLOCKS,),
        in_specs=[pl.BlockSpec((TOK, D), fixed)] * 3
        + [
            pl.BlockSpec((1, D), fixed),
            pl.BlockSpec((1, SB * MAIN + SB, TOK), lambda i: (i, 0, 0)),
        ],
        out_specs=[
            pl.BlockSpec((TOK, D), fixed),
            pl.BlockSpec((TOK, D), fixed),
            pl.BlockSpec((SB, ROWS, QW), lambda i: (i, 0, 0)),
        ],
        out_shape=[jax.ShapeDtypeStruct((TOK, D), bf16)] * 2
        + [jax.ShapeDtypeStruct((EXPERTS, ROWS, QW), bf16)],
        compiler_params=params(BIG),
        cost_estimate=pl.CostEstimate(flops=1 << 31, bytes_accessed=12 << 20, transcendentals=0),
        name="merge",
    )(keep, other, hid, fgain, hit)


def shift_z(v, k):
    return lax.ppermute(v, "seq", [(s, (s + 2 * k) % 8) for s in range(8)])


def shift_x(v, k):
    return lax.ppermute(v, "dp", [(d, d // 4 * 4 + (d + k) % 4) for d in range(16)])


def shift_y(v, k):
    return lax.ppermute(v, "dp", [(d, (d + 4 * k) % 16) for d in range(16)])


def swap_cores(v):
    return lax.ppermute(v, "seq", [(s, s ^ 1) for s in range(8)])


def fetch_weight(w, x, y):
    a = lax.dynamic_slice(w, (x * LANES, 0), (LANES, HALF))
    b = lax.dynamic_slice(w, (y * LANES, HALF), (LANES, HALF))
    slab = jnp.stack([a, b])
    got = [shift_z(slab, k) for k in (1, -1, 2)]
    return jnp.stack([v[0] for v in got]), jnp.stack([v[1] for v in got])


def near(v, shift):
    return [shift(v, 1), shift(v, -1)]


def far(pair, shift):
    h = LANES // 2
    return [shift(pair[0][:, :h], 1), shift(pair[1][:, h:], -1)]


def slot_hits(rank, half):
    r3 = jnp.broadcast_to(rank[:, None, :], (SB, MAIN, TOK))
    c = lax.broadcasted_iota(jnp.int32, (SB, MAIN, TOK), 1) + half * MAIN
    main = (r3 == c.astype(f32)).reshape(SB * MAIN, TOK)
    return main, rank == float(2 * MAIN + half)


def route_kernel(ids_ref, rw_ref, hit_ref, wgt_ref):
    e = lax.broadcasted_iota(jnp.int32, (EXPERTS, TOK), 0)
    member = jnp.zeros((EXPERTS, TOK), f32)
    weight = jnp.zeros((EXPERTS, TOK), f32)
    for k in range(TOP):
        hit = ids_ref[k : k + 1, :] == e
        member += jnp.where(hit, 1.0, 0.0)
        weight += jnp.where(hit, rw_ref[k : k + 1, :], 0.0)
    r = lax.broadcasted_iota(jnp.int32, (TOK, TOK), 0)
    c = lax.broadcasted_iota(jnp.int32, (TOK, TOK), 1)
    before = (r < c).astype(f32).astype(bf16)
    rank = jnp.where(member > 0.5, mm(member.astype(bf16), before), -1.0)
    for half in range(2):
        for i in range(BLOCKS):
            rows = slice(i * SB, (i + 1) * SB)
            main, over = slot_hits(rank[rows], half)
            wt = weight[rows]
            wm = jnp.broadcast_to(wt[:, None, :], (SB, MAIN, TOK)).reshape(SB * MAIN, TOK)
            hit = jnp.concatenate([main.astype(f32), over.astype(f32)], axis=0)
            hit_ref[half, i] = hit.astype(bf16)
            w = hit * jnp.concatenate([wm, wt], axis=0)
            wgt_ref[half, i] = w.T.astype(bf16)


def route_tables(ids_t, rw_t):
    vm = pl.BlockSpec(memory_space=pltpu.VMEM)
    n = SB * MAIN + SB
    return pl.pallas_call(
        route_kernel,
        in_specs=[vm, vm],
        out_specs=[vm, vm],
        out_shape=[
            jax.ShapeDtypeStruct((2, BLOCKS, n, TOK), bf16),
            jax.ShapeDtypeStruct((2, BLOCKS, TOK, n), bf16),
        ],
        compiler_params=pltpu.CompilerParams(vmem_limit_bytes=32 << 20),
        cost_estimate=pl.CostEstimate(flops=1 << 28, bytes_accessed=3 << 20, transcendentals=0),
        name="route_tables",
    )(ids_t, rw_t)


def over_perm(transposed=False):
    n = SB * NQ
    r = lax.broadcasted_iota(jnp.int32, (n, n), 1 if transposed else 0)
    c = lax.broadcasted_iota(jnp.int32, (n, n), 0 if transposed else 1)
    return (c == (r % SB) * NQ + r // SB).astype(f32).astype(bf16)


def unpack(ref):
    n = SB * NQ
    over = mm(over_perm(), ref[:, NQ * MAIN :, :].reshape(n, QW)).astype(bf16)
    parts = []
    for q in range(NQ):
        main = ref[:, q * MAIN : (q + 1) * MAIN, :].reshape(SB * MAIN, QW)
        parts.append(jnp.concatenate([main, over[q * SB : (q + 1) * SB]], axis=0))
    return jnp.concatenate(parts, axis=1)


def pack(ref, rows):
    n = SB * MAIN
    for q in range(NQ):
        ref[:, q * MAIN : (q + 1) * MAIN, :] = (
            rows[:n, q * QW : (q + 1) * QW].reshape(SB, MAIN, QW).astype(bf16)
        )
    over = jnp.concatenate([rows[n:, q * QW : (q + 1) * QW] for q in range(NQ)], axis=0)
    over = mm(over_perm(True), over.astype(bf16))
    ref[:, NQ * MAIN :, :] = over.reshape(SB, NQ, QW).astype(bf16)


def dispatch_kernel(hit_ref, x_ref, out_ref):
    pack(out_ref, mm(hit_ref[0], x_ref[...]))


def dispatch(hit, normed):
    n = SB * MAIN + SB
    return pl.pallas_call(
        dispatch_kernel,
        grid=(BLOCKS,),
        in_specs=[
            pl.BlockSpec((1, n, TOK), lambda i: (i, 0, 0)),
            pl.BlockSpec((TOK, D), lambda i: (0, 0)),
        ],
        out_specs=pl.BlockSpec((SB, ROWS, QW), lambda i: (i, 0, 0)),
        out_shape=jax.ShapeDtypeStruct((EXPERTS, ROWS, QW), bf16),
        compiler_params=params(BIG),
        cost_estimate=pl.CostEstimate(flops=1 << 31, bytes_accessed=6 << 20, transcendentals=0),
        name="dispatch",
    )(hit, normed)


def expert_kernel(in_ref, gu_ref, dn_ref, out_ref):
    hidden = mm(unpack(in_ref), gu_ref[0])
    gate = hidden[:, :FF]
    active = (gate / (1.0 + jnp.exp(-gate)) * hidden[:, FF:]).astype(bf16)
    pack(out_ref, mm(active, dn_ref[0]))


def expert_ffn(arrived, gate_up, down):
    n = arrived.shape[0]
    return pl.pallas_call(
        expert_kernel,
        grid=(n // SB,),
        in_specs=[
            pl.BlockSpec((SB, ROWS, QW), lambda i: (i, 0, 0)),
            pl.BlockSpec((1, D, 2 * FF), lambda i: (0, 0, 0), pipeline_mode=pl.Buffered(1)),
            pl.BlockSpec((1, FF, D), lambda i: (0, 0, 0), pipeline_mode=pl.Buffered(1)),
        ],
        out_specs=pl.BlockSpec((SB, ROWS, QW), lambda i: (i, 0, 0)),
        out_shape=jax.ShapeDtypeStruct(arrived.shape, bf16),
        compiler_params=params(BIG),
        cost_estimate=pl.CostEstimate(flops=11 << 30, bytes_accessed=20 << 20, transcendentals=1 << 20),
        name="expert_ffn",
    )(arrived, gate_up, down)


def combine_kernel(wgt_ref, ret_ref, base_ref, out_ref, acc_ref):
    i = pl.program_id(0)
    part = mm(wgt_ref[0], unpack(ret_ref))

    @pl.when(i == 0)
    def _():
        acc_ref[...] = part

    @pl.when(i > 0)
    def _():
        acc_ref[...] += part

    cols = pl.ds(pl.multiple_of(i * (D // BLOCKS), D // BLOCKS), D // BLOCKS)
    acc_ref[:, cols] += base_ref[...].astype(f32)

    @pl.when(i == pl.num_programs(0) - 1)
    def _():
        out_ref[...] = acc_ref[...].astype(out_ref.dtype)


def combine(wgt, returned, base, kind):
    n = SB * MAIN + SB
    return pl.pallas_call(
        combine_kernel,
        grid=(BLOCKS,),
        in_specs=[
            pl.BlockSpec((1, TOK, n), lambda i: (i, 0, 0)),
            pl.BlockSpec((SB, ROWS, QW), lambda i: (i, 0, 0)),
            pl.BlockSpec((TOK, D // BLOCKS), lambda i: (0, i)),
        ],
        out_specs=pl.BlockSpec((TOK, D), lambda i: (0, 0)),
        out_shape=jax.ShapeDtypeStruct((TOK, D), kind),
        scratch_shapes=[pltpu.VMEM((TOK, D), f32)],
        compiler_params=params(BIG),
        cost_estimate=pl.CostEstimate(flops=1 << 32, bytes_accessed=9 << 20, transcendentals=0),
        name="combine",
    )(wgt, returned, base)


def body(
    hidden_in, mix_values, mix_gate, state_proj, step_raw, step_bias, decay_rate, skip_gain,
    norm_gain, out_weight, ffn_gain, expert_ids, route_weights, gate_up, down_proj, doc_lengths,
):
    both = ("dp", "seq")
    seq_rank = lax.axis_index("seq")
    dp_rank = lax.axis_index("dp")
    scal = jnp.concatenate([doc_lengths[0], (seq_rank * TOK).astype(jnp.int32)[None]])

    x, y, z, core = dp_rank % 4, dp_rank // 4, seq_rank // 2, seq_rank % 2
    around = jnp.array([0, -1, 1, 2], jnp.int32)
    zs, xs_at, ys_at = ((v + around) % 4 for v in (z, x, y))
    order = jnp.concatenate([zs * 2 + core, zs, xs_at, ys_at]).astype(jnp.int32)
    xa, yb = fetch_weight(out_weight, x, y)

    hit, wgt = route_tables(expert_ids.T, route_weights.T)
    fresh, cum, xs = span_states(
        scal, step_raw.T, step_bias[None], decay_rate[None], mix_values, state_proj
    )
    near_x, near_y = near(xa, shift_x), near(yb, shift_y)
    fresh = lax.all_to_all(fresh, "seq", split_axis=0, concat_axis=0, tiled=True)
    carry = prefix(scal, fresh)
    carry = lax.all_to_all(carry, "seq", split_axis=0, concat_axis=0, tiled=True)
    carry, near_x, near_y = lax.optimization_barrier((carry, near_x, near_y))
    far_x, far_y = far(near_x, shift_x), far(near_y, shift_y)
    normed_mix = mixer(
        scal, mix_values, mix_gate, state_proj, xs, cum, carry, skip_gain[None], norm_gain[None]
    )
    other = lax.dynamic_index_in_dim(
        normed_mix.reshape(4, 2, SLICES, TOK, LANES), 1 - core, axis=1, keepdims=False
    )
    other, far_x, far_y = lax.optimization_barrier((other, far_x, far_y))
    slices = [xa] + near_x + far_x + [yb] + near_y + far_y
    keep, send = project(order, normed_mix, swap_cores(other), out_weight, slices)
    merged, normed, first = merge(keep, swap_cores(send), hidden_in, ffn_gain[None], hit[0])

    def exchange(v):
        return lax.all_to_all(v, both, split_axis=0, concat_axis=0, tiled=True)

    arrived = [exchange(first), exchange(dispatch(hit[1], normed))]
    returned = [exchange(expert_ffn(a, gate_up, down_proj)) for a in arrived]
    partial = combine(wgt[0], returned[0], merged, f32)
    return combine(wgt[1], returned[1], partial, bf16)


def solution(mesh):
    tok = P(("dp", "seq"), None)
    in_specs = (
        tok, tok, tok, tok, tok, P(), P(), P(), P(), P("seq", None), P(), tok, tok,
        P(("dp", "seq"), None, None), P(("dp", "seq"), None, None), P("dp", None),
    )
    return jax.shard_map(body, mesh=mesh, in_specs=in_specs, out_specs=tok, check_vma=False)
```

```python
import functools

import jax
import jax.numpy as jnp
from jax import lax
from jax.experimental import pallas as pl
from jax.experimental.pallas import tpu as pltpu
from jax.sharding import PartitionSpec as P

D = 2048
HEADS = 64
HEADDIM = 64
STATE = 128
GROUPS = 8
HPG = HEADS // GROUPS
CH = HPG * HEADDIM
FF = 768
TOP = 8
TOK = 256
EXPERTS = 128
EPS = 1e-05
MAIN = 8
ROWS = 72
QW = 256
NQ = 8
SB = 32
BIG = 58
BLOCKS = EXPERTS // SB
SLICES = 4
LANES = CH // SLICES
HALF = D // 2

f32 = jnp.float32
bf16 = jnp.bfloat16


def params(limit_mib, n=1):
    return pltpu.CompilerParams(
        vmem_limit_bytes=limit_mib << 20, dimension_semantics=("arbitrary",) * n
    )


def mm(a, b):
    return jnp.dot(a, b, preferred_element_type=f32)


def mm_t(a, b, da, db):
    return lax.dot_general(a, b, (((da,), (db,)), ((), ())), preferred_element_type=f32)


def split2(v):
    hi = v.astype(bf16)
    lo = (v - hi.astype(f32)).astype(bf16)
    return hi, lo


def spread(v, e):
    hi, lo = split2(v)
    return mm(hi, e) + mm(lo, e)


def head_onehot(g):
    h = lax.broadcasted_iota(jnp.int32, (HEADS, CH), 0)
    c = lax.broadcasted_iota(jnp.int32, (HEADS, CH), 1)
    return (h == g * HPG + c // HEADDIM).astype(f32).astype(bf16)


def segments(s_ref, shape, dim):
    return segment_at(s_ref, s_ref[3] + lax.broadcasted_iota(jnp.int32, shape, dim))


def segment_at(s_ref, pos):
    b0 = s_ref[0]
    b1 = b0 + s_ref[1]
    b2 = b1 + s_ref[2]
    return sum((pos >= b).astype(jnp.int32) for b in (b0, b1, b2))


def segment_before(s_ref, start):
    return jnp.where(start == 0, -1, segment_at(s_ref, start - 1))


def state_kernel(s_ref, raw_ref, bias_ref, rate_ref, x_ref, p_ref, fresh_ref, cum_ref, xs_ref, a_s, e_s):
    g = pl.program_id(0)

    @pl.when(g == 0)
    def _():
        v = raw_ref[...].astype(f32).T + bias_ref[...]
        step = jnp.maximum(v, 0.0) + jnp.log(1.0 + jnp.exp(-jnp.abs(v)))
        logd = -step * rate_ref[...] * (1.0 / 2048.0)
        r = lax.broadcasted_iota(jnp.int32, (TOK, TOK), 0)
        c = lax.broadcasted_iota(jnp.int32, (TOK, TOK), 1)
        tri = (r >= c).astype(f32)
        cum = jnp.dot(tri, logd, preferred_element_type=f32, precision=lax.Precision.HIGHEST)
        cum_ref[...] = cum
        a_s[...] = step * jnp.exp(-cum)
        e_s[...] = jnp.exp(cum[TOK - 8 :, :])

    e = head_onehot(g)
    xs = (x_ref[...].astype(f32) * spread(a_s[...], e)).astype(bf16)
    xs_ref[...] = xs
    last = segment_at(s_ref, s_ref[3] + TOK - 1)
    b = jnp.where(segments(s_ref, (TOK, STATE), 0) == last, p_ref[:, :STATE].astype(f32), 0.0).astype(bf16)
    end = spread(e_s[...], e)[7:8, :]
    fresh_ref[0, :STATE, :] = (mm_t(b, xs, 0, 0) * end).astype(bf16)
    hi = end.astype(bf16).astype(f32)
    row = lax.broadcasted_iota(jnp.int32, (16, CH), 0)
    tail = jnp.where(row == 0, hi, jnp.where(row == 1, end - hi, 0.0))
    fresh_ref[0, STATE:, :] = tail.astype(bf16)


def span_states(scal, raw, bias, rate, x, p):
    smem = pl.BlockSpec(memory_space=pltpu.SMEM)
    return pl.pallas_call(
        state_kernel,
        grid=(GROUPS,),
        in_specs=[
            smem,
            pl.BlockSpec((HEADS, TOK), lambda g: (0, 0)),
            pl.BlockSpec((1, HEADS), lambda g: (0, 0)),
            pl.BlockSpec((1, HEADS), lambda g: (0, 0)),
            pl.BlockSpec((TOK, CH), lambda g: (0, g)),
            pl.BlockSpec((TOK, 2 * STATE), lambda g: (0, g)),
        ],
        out_specs=[
            pl.BlockSpec((1, STATE + 16, CH), lambda g: (g, 0, 0)),
            pl.BlockSpec((TOK, HEADS), lambda g: (0, 0)),
            pl.BlockSpec((TOK, CH), lambda g: (0, g)),
        ],
        out_shape=[
            jax.ShapeDtypeStruct((GROUPS, STATE + 16, CH), bf16),
            jax.ShapeDtypeStruct((TOK, HEADS), f32),
            jax.ShapeDtypeStruct((TOK, HEADS * HEADDIM), bf16),
        ],
        scratch_shapes=[pltpu.VMEM((TOK, HEADS), f32), pltpu.VMEM((8, HEADS), f32)],
        compiler_params=params(BIG),
        cost_estimate=pl.CostEstimate(flops=1 << 31, bytes_accessed=30 << 20, transcendentals=1 << 20),
        name="span_states",
    )(scal, raw, bias, rate, x, p)


def prefix_kernel(s_ref, in_ref, out_ref):
    carry = jnp.zeros((STATE, CH), f32)
    for r in range(8):
        out_ref[r] = carry.astype(bf16)
        tail = in_ref[r, STATE:, :].astype(f32)
        keep = tail[0:1, :] + tail[1:2, :]
        start = r * TOK
        same = segment_at(s_ref, start + TOK - 1) == segment_before(s_ref, jnp.int32(start))
        keep = keep * same.astype(f32)
        carry = carry * keep + in_ref[r, :STATE, :].astype(f32)


def prefix(scal, fresh):
    return pl.pallas_call(
        prefix_kernel,
        in_specs=[pl.BlockSpec(memory_space=pltpu.SMEM), pl.BlockSpec(memory_space=pltpu.VMEM)],
        out_specs=pl.BlockSpec(memory_space=pltpu.VMEM),
        out_shape=jax.ShapeDtypeStruct((8, STATE, CH), bf16),
        compiler_params=pltpu.CompilerParams(vmem_limit_bytes=16 << 20),
        name="span_prefix",
    )(scal, fresh)


def mixer_kernel(s_ref, x_ref, z_ref, p_ref, xs_ref, cum_ref, carry_ref, skip_ref, gain_ref, n_ref):
    g = pl.program_id(0)
    e = head_onehot(g)
    b, c = p_ref[:, :STATE], p_ref[:, STATE:]
    scores = mm_t(c, b, 1, 1)
    i = lax.broadcasted_iota(jnp.int32, (TOK, TOK), 0)
    j = lax.broadcasted_iota(jnp.int32, (TOK, TOK), 1)
    ok = (i >= j) & (segments(s_ref, (TOK, TOK), 0) == segments(s_ref, (TOK, TOK), 1))
    m = jnp.where(ok, scores, 0.0).astype(bf16)
    before = segment_before(s_ref, s_ref[3])
    cl = jnp.where(segments(s_ref, (TOK, STATE), 0) == before, c.astype(f32), 0.0).astype(bf16)
    acc = mm(m, xs_ref[...]) + mm(cl, carry_ref[0])
    x = x_ref[...].astype(f32)
    skip = spread(jnp.broadcast_to(skip_ref[...], (8, HEADS)), e)[0:1, :]
    mixed = acc * spread(jnp.exp(cum_ref[...]), e) + skip * x
    z = z_ref[...].astype(f32)
    u = mixed * (z / (1.0 + jnp.exp(-z)))
    ms = jnp.mean(u * u, axis=-1, keepdims=True)
    n = (u * lax.rsqrt(ms + EPS) * gain_ref[...]).astype(bf16)
    for k in range(SLICES):
        n_ref[0, k] = n[:, k * LANES : (k + 1) * LANES]


def mixer(scal, x, z, p, xs, cum, carry, skip, gain):
    fixed = lambda g: (0, 0)
    col = lambda g: (0, g)
    return pl.pallas_call(
        mixer_kernel,
        grid=(GROUPS,),
        in_specs=[
            pl.BlockSpec(memory_space=pltpu.SMEM),
            pl.BlockSpec((TOK, CH), col),
            pl.BlockSpec((TOK, CH), col),
            pl.BlockSpec((TOK, 2 * STATE), col),
            pl.BlockSpec((TOK, CH), col),
            pl.BlockSpec((TOK, HEADS), fixed),
            pl.BlockSpec((1, STATE, CH), lambda g: (g, 0, 0)),
            pl.BlockSpec((1, HEADS), fixed),
            pl.BlockSpec((1, CH), col),
        ],
        out_specs=pl.BlockSpec((1, SLICES, TOK, LANES), lambda g: (g, 0, 0, 0)),
        out_shape=jax.ShapeDtypeStruct((GROUPS, SLICES, TOK, LANES), bf16),
        compiler_params=params(BIG),
        cost_estimate=pl.CostEstimate(flops=1 << 31, bytes_accessed=40 << 20, transcendentals=1 << 21),
        name="mixer",
    )(scal, x, z, p, xs, cum, carry, skip, gain)


def project_kernel(s_ref, mine_ref, theirs_ref, own_ref, *refs):
    w_refs, (keep_ref, send_ref, acc_ref) = refs[:10], refs[10:]
    t = pl.program_id(0)

    def lhs(at):
        parts = []
        for k in range(SLICES):
            j = k if at is None else s_ref[at + k]
            parts.append(jnp.concatenate([mine_ref[0, j], theirs_ref[0, j]], axis=0))
        return jnp.concatenate(parts, axis=1)

    @pl.when(t == 0)
    def _():
        acc_ref[...] = mm(lhs(None), own_ref[...])

    @pl.when(t > 0)
    def _():
        for h in range(2):
            w = jnp.concatenate([r[0] for r in w_refs[5 * h : 5 * h + 5]], axis=0)
            acc_ref[:, h * HALF : (h + 1) * HALF] += mm(lhs(8 + 4 * h), w)

    @pl.when(t == pl.num_programs(0) - 1)
    def _():
        keep_ref[...] = acc_ref[:TOK]
        send_ref[...] = acc_ref[TOK:].astype(bf16)


def project(scal, mine, theirs, own, slices):
    fixed = lambda t, s: (0, 0)
    return pl.pallas_call(
        project_kernel,
        grid_spec=pltpu.PrefetchScalarGridSpec(
            num_scalar_prefetch=1,
            grid=(4,),
            in_specs=[
                pl.BlockSpec((1, SLICES, TOK, LANES), lambda t, s: (s[t], 0, 0, 0)),
                pl.BlockSpec((1, SLICES, TOK, LANES), lambda t, s: (s[4 + t], 0, 0, 0)),
                pl.BlockSpec((CH, D), fixed),
            ]
            + [
                pl.BlockSpec((1, rows, HALF), lambda t, s: (jnp.maximum(t - 1, 0), 0, 0))
                for rows in (LANES, LANES, LANES, LANES // 2, LANES // 2)
            ]
            * 2,
            out_specs=[pl.BlockSpec((TOK, D), fixed), pl.BlockSpec((TOK, D), fixed)],
            scratch_shapes=[pltpu.VMEM((2 * TOK, D), f32)],
        ),
        out_shape=[jax.ShapeDtypeStruct((TOK, D), f32), jax.ShapeDtypeStruct((TOK, D), bf16)],
        compiler_params=params(BIG),
        cost_estimate=pl.CostEstimate(flops=1 << 32, bytes_accessed=14 << 20, transcendentals=0),
        name="project",
    )(scal, mine, theirs, own, *slices)


def merge_kernel(keep_ref, other_ref, hid_ref, fgain_ref, hit_ref, merged_ref, normed_ref, out_ref):
    @pl.when(pl.program_id(0) == 0)
    def _():
        total = keep_ref[...] + other_ref[...].astype(f32)
        merged = (hid_ref[...].astype(f32) + total).astype(bf16)
        merged_ref[...] = merged
        mf = merged.astype(f32)
        sq = jnp.mean(mf * mf, axis=-1, keepdims=True)
        normed_ref[...] = (mf * lax.rsqrt(sq + EPS) * fgain_ref[...]).astype(bf16)

    pack(out_ref, mm(hit_ref[0], normed_ref[...]))


def merge(keep, other, hid, fgain, hit):
    fixed = lambda i: (0, 0)
    return pl.pallas_call(
        merge_kernel,
        grid=(BLOCKS,),
        in_specs=[pl.BlockSpec((TOK, D), fixed)] * 3
        + [
            pl.BlockSpec((1, D), fixed),
            pl.BlockSpec((1, SB * MAIN + SB, TOK), lambda i: (i, 0, 0)),
        ],
        out_specs=[
            pl.BlockSpec((TOK, D), fixed),
            pl.BlockSpec((TOK, D), fixed),
            pl.BlockSpec((SB, ROWS, QW), lambda i: (i, 0, 0)),
        ],
        out_shape=[jax.ShapeDtypeStruct((TOK, D), bf16)] * 2
        + [jax.ShapeDtypeStruct((EXPERTS, ROWS, QW), bf16)],
        compiler_params=params(BIG),
        cost_estimate=pl.CostEstimate(flops=1 << 31, bytes_accessed=12 << 20, transcendentals=0),
        name="merge",
    )(keep, other, hid, fgain, hit)


def shift_z(v, k):
    return lax.ppermute(v, "seq", [(s, (s + 2 * k) % 8) for s in range(8)])


def shift_x(v, k):
    return lax.ppermute(v, "dp", [(d, d // 4 * 4 + (d + k) % 4) for d in range(16)])


def shift_y(v, k):
    return lax.ppermute(v, "dp", [(d, (d + 4 * k) % 16) for d in range(16)])


def swap_cores(v):
    return lax.ppermute(v, "seq", [(s, s ^ 1) for s in range(8)])


def fetch_weight(w, x, y):
    a = lax.dynamic_slice(w, (x * LANES, 0), (LANES, HALF))
    b = lax.dynamic_slice(w, (y * LANES, HALF), (LANES, HALF))
    slab = jnp.stack([a, b])
    return near(slab, shift_z)


def slabs(pair):
    got = pair + [jnp.concatenate(far(pair, shift_z), axis=1)]
    return jnp.stack([v[0] for v in got]), jnp.stack([v[1] for v in got])


def near(v, shift):
    return [shift(v, 1), shift(v, -1)]


def far(pair, shift):
    h = LANES // 2
    return [shift(pair[0][:, :h], 1), shift(pair[1][:, h:], -1)]


def slot_hits(rank, half):
    r3 = jnp.broadcast_to(rank[:, None, :], (SB, MAIN, TOK))
    c = lax.broadcasted_iota(jnp.int32, (SB, MAIN, TOK), 1) + half * MAIN
    main = (r3 == c.astype(f32)).reshape(SB * MAIN, TOK)
    return main, rank == float(2 * MAIN + half)


def route_kernel(ids_ref, rw_ref, hit_ref, wgt_ref):
    e = lax.broadcasted_iota(jnp.int32, (EXPERTS, TOK), 0)
    member = jnp.zeros((EXPERTS, TOK), f32)
    weight = jnp.zeros((EXPERTS, TOK), f32)
    for k in range(TOP):
        hit = ids_ref[k : k + 1, :] == e
        member += jnp.where(hit, 1.0, 0.0)
        weight += jnp.where(hit, rw_ref[k : k + 1, :], 0.0)
    r = lax.broadcasted_iota(jnp.int32, (TOK, TOK), 0)
    c = lax.broadcasted_iota(jnp.int32, (TOK, TOK), 1)
    before = (r < c).astype(f32).astype(bf16)
    rank = jnp.where(member > 0.5, mm(member.astype(bf16), before), -1.0)
    for half in range(2):
        for i in range(BLOCKS):
            rows = slice(i * SB, (i + 1) * SB)
            main, over = slot_hits(rank[rows], half)
            wt = weight[rows]
            wm = jnp.broadcast_to(wt[:, None, :], (SB, MAIN, TOK)).reshape(SB * MAIN, TOK)
            hit = jnp.concatenate([main.astype(f32), over.astype(f32)], axis=0)
            hit_ref[half, i] = hit.astype(bf16)
            w = hit * jnp.concatenate([wm, wt], axis=0)
            wgt_ref[half, i] = w.T.astype(bf16)


def route_tables(ids_t, rw_t):
    vm = pl.BlockSpec(memory_space=pltpu.VMEM)
    n = SB * MAIN + SB
    return pl.pallas_call(
        route_kernel,
        in_specs=[vm, vm],
        out_specs=[vm, vm],
        out_shape=[
            jax.ShapeDtypeStruct((2, BLOCKS, n, TOK), bf16),
            jax.ShapeDtypeStruct((2, BLOCKS, TOK, n), bf16),
        ],
        compiler_params=pltpu.CompilerParams(vmem_limit_bytes=32 << 20),
        cost_estimate=pl.CostEstimate(flops=1 << 28, bytes_accessed=3 << 20, transcendentals=0),
        name="route_tables",
    )(ids_t, rw_t)


def over_perm(transposed=False):
    n = SB * NQ
    r = lax.broadcasted_iota(jnp.int32, (n, n), 1 if transposed else 0)
    c = lax.broadcasted_iota(jnp.int32, (n, n), 0 if transposed else 1)
    return (c == (r % SB) * NQ + r // SB).astype(f32).astype(bf16)


def unpack(ref):
    n = SB * NQ
    over = mm(over_perm(), ref[:, NQ * MAIN :, :].reshape(n, QW)).astype(bf16)
    parts = []
    for q in range(NQ):
        main = ref[:, q * MAIN : (q + 1) * MAIN, :].reshape(SB * MAIN, QW)
        parts.append(jnp.concatenate([main, over[q * SB : (q + 1) * SB]], axis=0))
    return jnp.concatenate(parts, axis=1)


def pack(ref, rows):
    n = SB * MAIN
    for q in range(NQ):
        ref[:, q * MAIN : (q + 1) * MAIN, :] = (
            rows[:n, q * QW : (q + 1) * QW].reshape(SB, MAIN, QW).astype(bf16)
        )
    over = jnp.concatenate([rows[n:, q * QW : (q + 1) * QW] for q in range(NQ)], axis=0)
    over = mm(over_perm(True), over.astype(bf16))
    ref[:, NQ * MAIN :, :] = over.reshape(SB, NQ, QW).astype(bf16)


def dispatch_kernel(hit_ref, x_ref, out_ref):
    pack(out_ref, mm(hit_ref[0], x_ref[...]))


def dispatch(hit, normed):
    n = SB * MAIN + SB
    return pl.pallas_call(
        dispatch_kernel,
        grid=(BLOCKS,),
        in_specs=[
            pl.BlockSpec((1, n, TOK), lambda i: (i, 0, 0)),
            pl.BlockSpec((TOK, D), lambda i: (0, 0)),
        ],
        out_specs=pl.BlockSpec((SB, ROWS, QW), lambda i: (i, 0, 0)),
        out_shape=jax.ShapeDtypeStruct((EXPERTS, ROWS, QW), bf16),
        compiler_params=params(BIG),
        cost_estimate=pl.CostEstimate(flops=1 << 31, bytes_accessed=6 << 20, transcendentals=0),
        name="dispatch",
    )(hit, normed)


def expert_kernel(in_ref, gu_ref, dn_ref, out_ref):
    hidden = mm(unpack(in_ref), gu_ref[0])
    gate = hidden[:, :FF]
    active = (gate / (1.0 + jnp.exp(-gate)) * hidden[:, FF:]).astype(bf16)
    pack(out_ref, mm(active, dn_ref[0]))


def expert_ffn(arrived, gate_up, down):
    n = arrived.shape[0]
    return pl.pallas_call(
        expert_kernel,
        grid=(n // SB,),
        in_specs=[
            pl.BlockSpec((SB, ROWS, QW), lambda i: (i, 0, 0)),
            pl.BlockSpec((1, D, 2 * FF), lambda i: (0, 0, 0), pipeline_mode=pl.Buffered(1)),
            pl.BlockSpec((1, FF, D), lambda i: (0, 0, 0), pipeline_mode=pl.Buffered(1)),
        ],
        out_specs=pl.BlockSpec((SB, ROWS, QW), lambda i: (i, 0, 0)),
        out_shape=jax.ShapeDtypeStruct(arrived.shape, bf16),
        compiler_params=params(BIG),
        cost_estimate=pl.CostEstimate(flops=11 << 30, bytes_accessed=20 << 20, transcendentals=1 << 20),
        name="expert_ffn",
    )(arrived, gate_up, down)


def combine_kernel(wgt_ref, ret_ref, base_ref, out_ref, acc_ref):
    i = pl.program_id(0)
    part = mm(wgt_ref[0], unpack(ret_ref))

    @pl.when(i == 0)
    def _():
        acc_ref[...] = part

    @pl.when(i > 0)
    def _():
        acc_ref[...] += part

    cols = pl.ds(pl.multiple_of(i * (D // BLOCKS), D // BLOCKS), D // BLOCKS)
    acc_ref[:, cols] += base_ref[...].astype(f32)

    @pl.when(i == pl.num_programs(0) - 1)
    def _():
        out_ref[...] = acc_ref[...].astype(out_ref.dtype)


def combine(wgt, returned, base, kind):
    n = SB * MAIN + SB
    return pl.pallas_call(
        combine_kernel,
        grid=(BLOCKS,),
        in_specs=[
            pl.BlockSpec((1, TOK, n), lambda i: (i, 0, 0)),
            pl.BlockSpec((SB, ROWS, QW), lambda i: (i, 0, 0)),
            pl.BlockSpec((TOK, D // BLOCKS), lambda i: (0, i)),
        ],
        out_specs=pl.BlockSpec((TOK, D), lambda i: (0, 0)),
        out_shape=jax.ShapeDtypeStruct((TOK, D), kind),
        scratch_shapes=[pltpu.VMEM((TOK, D), f32)],
        compiler_params=params(BIG),
        cost_estimate=pl.CostEstimate(flops=1 << 32, bytes_accessed=9 << 20, transcendentals=0),
        name="combine",
    )(wgt, returned, base)


def body(
    hidden_in, mix_values, mix_gate, state_proj, step_raw, step_bias, decay_rate, skip_gain,
    norm_gain, out_weight, ffn_gain, expert_ids, route_weights, gate_up, down_proj, doc_lengths,
):
    both = ("dp", "seq")
    seq_rank = lax.axis_index("seq")
    dp_rank = lax.axis_index("dp")
    scal = jnp.concatenate([doc_lengths[0], (seq_rank * TOK).astype(jnp.int32)[None]])

    x, y, z, core = dp_rank % 4, dp_rank // 4, seq_rank // 2, seq_rank % 2
    around = jnp.array([0, -1, 1, 2], jnp.int32)
    zs, xs_at, ys_at = ((v + around) % 4 for v in (z, x, y))
    order = jnp.concatenate([zs * 2 + core, zs, xs_at, ys_at]).astype(jnp.int32)
    near_z = fetch_weight(out_weight, x, y)

    hit, wgt = route_tables(expert_ids.T, route_weights.T)
    fresh, cum, xs = span_states(
        scal, step_raw.T, step_bias[None], decay_rate[None], mix_values, state_proj
    )
    fresh, near_z = lax.optimization_barrier((fresh, near_z))
    xa, yb = slabs(near_z)
    near_x, near_y = near(xa, shift_x), near(yb, shift_y)
    fresh = lax.all_to_all(fresh, "seq", split_axis=0, concat_axis=0, tiled=True)
    carry = prefix(scal, fresh)
    carry, near_x, near_y = lax.optimization_barrier((carry, near_x, near_y))
    far_x, far_y = far(near_x, shift_x), far(near_y, shift_y)
    carry = lax.all_to_all(carry, "seq", split_axis=0, concat_axis=0, tiled=True)
    normed_mix = mixer(
        scal, mix_values, mix_gate, state_proj, xs, cum, carry, skip_gain[None], norm_gain[None]
    )
    other = lax.dynamic_index_in_dim(
        normed_mix.reshape(4, 2, SLICES, TOK, LANES), 1 - core, axis=1, keepdims=False
    )
    other, far_x, far_y = lax.optimization_barrier((other, far_x, far_y))
    slices = [xa] + near_x + far_x + [yb] + near_y + far_y
    keep, send = project(order, normed_mix, swap_cores(other), out_weight, slices)
    merged, normed, first = merge(keep, swap_cores(send), hidden_in, ffn_gain[None], hit[0])

    def exchange(v):
        return lax.all_to_all(v, both, split_axis=0, concat_axis=0, tiled=True)

    arrived = [exchange(first), exchange(dispatch(hit[1], normed))]
    returned = [exchange(expert_ffn(a, gate_up, down_proj)) for a in arrived]
    partial = combine(wgt[0], returned[0], merged, f32)
    return combine(wgt[1], returned[1], partial, bf16)


def solution(mesh):
    tok = P(("dp", "seq"), None)
    in_specs = (
        tok, tok, tok, tok, tok, P(), P(), P(), P(), P("seq", None), P(), tok, tok,
        P(("dp", "seq"), None, None), P(("dp", "seq"), None, None), P("dp", None),
    )
    return jax.shard_map(body, mesh=mesh, in_specs=in_specs, out_specs=tok, check_vma=False)
```

```python
import functools

import jax
import jax.numpy as jnp
from jax import lax
from jax.experimental import pallas as pl
from jax.experimental.pallas import tpu as pltpu
from jax.sharding import PartitionSpec as P

D = 2048
HEADS = 64
HEADDIM = 64
STATE = 128
GROUPS = 8
HPG = HEADS // GROUPS
CH = HPG * HEADDIM
FF = 768
TOP = 8
TOK = 256
EXPERTS = 128
EPS = 1e-05
MAIN = 8
ROWS = 72
QW = 256
NQ = 8
SB = 32
BIG = 58
BLOCKS = EXPERTS // SB
SLICES = 4
LANES = CH // SLICES
HALF = D // 2

f32 = jnp.float32
bf16 = jnp.bfloat16


def params(limit_mib, n=1):
    return pltpu.CompilerParams(
        vmem_limit_bytes=limit_mib << 20, dimension_semantics=("arbitrary",) * n
    )


def mm(a, b):
    return jnp.dot(a, b, preferred_element_type=f32)


def mm_t(a, b, da, db):
    return lax.dot_general(a, b, (((da,), (db,)), ((), ())), preferred_element_type=f32)


def split2(v):
    hi = v.astype(bf16)
    lo = (v - hi.astype(f32)).astype(bf16)
    return hi, lo


def spread(v, e):
    hi, lo = split2(v)
    return mm(hi, e) + mm(lo, e)


def head_onehot(g):
    h = lax.broadcasted_iota(jnp.int32, (HEADS, CH), 0)
    c = lax.broadcasted_iota(jnp.int32, (HEADS, CH), 1)
    return (h == g * HPG + c // HEADDIM).astype(f32).astype(bf16)


def segments(s_ref, shape, dim):
    return segment_at(s_ref, s_ref[3] + lax.broadcasted_iota(jnp.int32, shape, dim))


def segment_at(s_ref, pos):
    b0 = s_ref[0]
    b1 = b0 + s_ref[1]
    b2 = b1 + s_ref[2]
    return sum((pos >= b).astype(jnp.int32) for b in (b0, b1, b2))


def segment_before(s_ref, start):
    return jnp.where(start == 0, -1, segment_at(s_ref, start - 1))


def state_kernel(s_ref, raw_ref, bias_ref, rate_ref, x_ref, p_ref, fresh_ref, cum_ref, xs_ref, a_s, e_s):
    g = pl.program_id(0)

    @pl.when(g == 0)
    def _():
        v = raw_ref[...].astype(f32).T + bias_ref[...]
        step = jnp.maximum(v, 0.0) + jnp.log(1.0 + jnp.exp(-jnp.abs(v)))
        logd = -step * rate_ref[...] * (1.0 / 2048.0)
        r = lax.broadcasted_iota(jnp.int32, (TOK, TOK), 0)
        c = lax.broadcasted_iota(jnp.int32, (TOK, TOK), 1)
        tri = (r >= c).astype(f32)
        cum = jnp.dot(tri, logd, preferred_element_type=f32, precision=lax.Precision.HIGHEST)
        cum_ref[...] = cum
        a_s[...] = step * jnp.exp(-cum)
        e_s[...] = jnp.exp(cum[TOK - 8 :, :])

    e = head_onehot(g)
    xs = (x_ref[...].astype(f32) * spread(a_s[...], e)).astype(bf16)
    xs_ref[...] = xs
    last = segment_at(s_ref, s_ref[3] + TOK - 1)
    b = jnp.where(segments(s_ref, (TOK, STATE), 0) == last, p_ref[:, :STATE].astype(f32), 0.0).astype(bf16)
    end = spread(e_s[...], e)[7:8, :]
    fresh_ref[0, :STATE, :] = (mm_t(b, xs, 0, 0) * end).astype(bf16)
    hi = end.astype(bf16).astype(f32)
    row = lax.broadcasted_iota(jnp.int32, (16, CH), 0)
    tail = jnp.where(row == 0, hi, jnp.where(row == 1, end - hi, 0.0))
    fresh_ref[0, STATE:, :] = tail.astype(bf16)


def span_states(scal, raw, bias, rate, x, p):
    smem = pl.BlockSpec(memory_space=pltpu.SMEM)
    return pl.pallas_call(
        state_kernel,
        grid=(GROUPS,),
        in_specs=[
            smem,
            pl.BlockSpec((HEADS, TOK), lambda g: (0, 0)),
            pl.BlockSpec((1, HEADS), lambda g: (0, 0)),
            pl.BlockSpec((1, HEADS), lambda g: (0, 0)),
            pl.BlockSpec((TOK, CH), lambda g: (0, g)),
            pl.BlockSpec((TOK, 2 * STATE), lambda g: (0, g)),
        ],
        out_specs=[
            pl.BlockSpec((1, STATE + 16, CH), lambda g: (g, 0, 0)),
            pl.BlockSpec((TOK, HEADS), lambda g: (0, 0)),
            pl.BlockSpec((TOK, CH), lambda g: (0, g)),
        ],
        out_shape=[
            jax.ShapeDtypeStruct((GROUPS, STATE + 16, CH), bf16),
            jax.ShapeDtypeStruct((TOK, HEADS), f32),
            jax.ShapeDtypeStruct((TOK, HEADS * HEADDIM), bf16),
        ],
        scratch_shapes=[pltpu.VMEM((TOK, HEADS), f32), pltpu.VMEM((8, HEADS), f32)],
        compiler_params=params(BIG),
        cost_estimate=pl.CostEstimate(flops=1 << 31, bytes_accessed=30 << 20, transcendentals=1 << 20),
        name="span_states",
    )(scal, raw, bias, rate, x, p)


def prefix_kernel(s_ref, in_ref, out_ref):
    carry = jnp.zeros((STATE, CH), f32)
    for r in range(8):
        out_ref[r] = carry.astype(bf16)
        tail = in_ref[r, STATE:, :].astype(f32)
        keep = tail[0:1, :] + tail[1:2, :]
        start = r * TOK
        same = segment_at(s_ref, start + TOK - 1) == segment_before(s_ref, jnp.int32(start))
        keep = keep * same.astype(f32)
        carry = carry * keep + in_ref[r, :STATE, :].astype(f32)


def prefix(scal, fresh):
    return pl.pallas_call(
        prefix_kernel,
        in_specs=[pl.BlockSpec(memory_space=pltpu.SMEM), pl.BlockSpec(memory_space=pltpu.VMEM)],
        out_specs=pl.BlockSpec(memory_space=pltpu.VMEM),
        out_shape=jax.ShapeDtypeStruct((8, STATE, CH), bf16),
        compiler_params=pltpu.CompilerParams(vmem_limit_bytes=16 << 20),
        name="span_prefix",
    )(scal, fresh)


def mixer_kernel(s_ref, x_ref, z_ref, p_ref, xs_ref, cum_ref, carry_ref, skip_ref, gain_ref, n_ref):
    e = head_onehot(2 * pl.program_id(0) + s_ref[4])
    b, c = p_ref[:, :STATE], p_ref[:, STATE:]
    scores = mm_t(c, b, 1, 1)
    i = lax.broadcasted_iota(jnp.int32, (TOK, TOK), 0)
    j = lax.broadcasted_iota(jnp.int32, (TOK, TOK), 1)
    ok = (i >= j) & (segments(s_ref, (TOK, TOK), 0) == segments(s_ref, (TOK, TOK), 1))
    m = jnp.where(ok, scores, 0.0).astype(bf16)
    before = segment_before(s_ref, s_ref[3])
    cl = jnp.where(segments(s_ref, (TOK, STATE), 0) == before, c.astype(f32), 0.0).astype(bf16)
    acc = mm(m, xs_ref[...]) + mm(cl, carry_ref[0])
    x = x_ref[...].astype(f32)
    skip = spread(jnp.broadcast_to(skip_ref[...], (8, HEADS)), e)[0:1, :]
    mixed = acc * spread(jnp.exp(cum_ref[...]), e) + skip * x
    z = z_ref[...].astype(f32)
    u = mixed * (z / (1.0 + jnp.exp(-z)))
    ms = jnp.mean(u * u, axis=-1, keepdims=True)
    n = (u * lax.rsqrt(ms + EPS) * gain_ref[...]).astype(bf16)
    for k in range(SLICES):
        n_ref[0, k] = n[:, k * LANES : (k + 1) * LANES]


def mixer(scal, x, z, p, xs, cum, carry, skip, gain):
    fixed = lambda g, s: (0, 0)
    col = lambda g, s: (0, 2 * g + s[4])
    return pl.pallas_call(
        mixer_kernel,
        grid_spec=pltpu.PrefetchScalarGridSpec(
            num_scalar_prefetch=1,
            grid=(GROUPS // 2,),
            in_specs=[
                pl.BlockSpec((TOK, CH), col),
                pl.BlockSpec((TOK, CH), col),
                pl.BlockSpec((TOK, 2 * STATE), col),
                pl.BlockSpec((TOK, CH), col),
                pl.BlockSpec((TOK, HEADS), fixed),
                pl.BlockSpec((1, STATE, CH), lambda g, s: (2 * g + s[4], 0, 0)),
                pl.BlockSpec((1, HEADS), fixed),
                pl.BlockSpec((1, CH), col),
            ],
            out_specs=pl.BlockSpec((1, SLICES, TOK, LANES), lambda g, s: (g, 0, 0, 0)),
        ),
        out_shape=jax.ShapeDtypeStruct((GROUPS // 2, SLICES, TOK, LANES), bf16),
        compiler_params=params(BIG),
        cost_estimate=pl.CostEstimate(flops=1 << 30, bytes_accessed=20 << 20, transcendentals=1 << 20),
        name="mixer",
    )(scal, x, z, p, xs, cum, carry, skip, gain)


def project_kernel(s_ref, mine_ref, theirs_ref, own_ref, *refs):
    w_refs, (keep_ref, send_ref, acc_ref) = refs[:10], refs[10:]
    t = pl.program_id(0)

    def lhs(at):
        parts = []
        for k in range(SLICES):
            j = k if at is None else s_ref[at + k]
            parts.append(jnp.concatenate([mine_ref[0, j], theirs_ref[0, j]], axis=0))
        return jnp.concatenate(parts, axis=1)

    @pl.when(t == 0)
    def _():
        acc_ref[...] = mm(lhs(None), own_ref[...])

    @pl.when(t > 0)
    def _():
        for h in range(2):
            w = jnp.concatenate([r[0] for r in w_refs[5 * h : 5 * h + 5]], axis=0)
            acc_ref[:, h * HALF : (h + 1) * HALF] += mm(lhs(4 + 4 * h), w)

    @pl.when(t == pl.num_programs(0) - 1)
    def _():
        keep_ref[...] = acc_ref[:TOK]
        send_ref[...] = acc_ref[TOK:].astype(bf16)


def project(scal, mine, theirs, own, slices):
    fixed = lambda t, s: (0, 0)
    return pl.pallas_call(
        project_kernel,
        grid_spec=pltpu.PrefetchScalarGridSpec(
            num_scalar_prefetch=1,
            grid=(4,),
            in_specs=[
                pl.BlockSpec((1, SLICES, TOK, LANES), lambda t, s: (s[t], 0, 0, 0)),
                pl.BlockSpec((1, SLICES, TOK, LANES), lambda t, s: (s[t], 0, 0, 0)),
                pl.BlockSpec((CH, D), fixed),
            ]
            + [
                pl.BlockSpec((1, rows, HALF), lambda t, s: (jnp.maximum(t - 1, 0), 0, 0))
                for rows in (LANES, LANES, LANES, LANES // 2, LANES // 2)
            ]
            * 2,
            out_specs=[pl.BlockSpec((TOK, D), fixed), pl.BlockSpec((TOK, D), fixed)],
            scratch_shapes=[pltpu.VMEM((2 * TOK, D), f32)],
        ),
        out_shape=[jax.ShapeDtypeStruct((TOK, D), f32), jax.ShapeDtypeStruct((TOK, D), bf16)],
        compiler_params=params(BIG),
        cost_estimate=pl.CostEstimate(flops=1 << 32, bytes_accessed=14 << 20, transcendentals=0),
        name="project",
    )(scal, mine, theirs, own, *slices)


def merge_kernel(keep_ref, other_ref, hid_ref, fgain_ref, hit_ref, merged_ref, normed_ref, out_ref):
    @pl.when(pl.program_id(0) == 0)
    def _():
        total = keep_ref[...] + other_ref[...].astype(f32)
        merged = (hid_ref[...].astype(f32) + total).astype(bf16)
        merged_ref[...] = merged
        mf = merged.astype(f32)
        sq = jnp.mean(mf * mf, axis=-1, keepdims=True)
        normed_ref[...] = (mf * lax.rsqrt(sq + EPS) * fgain_ref[...]).astype(bf16)

    pack(out_ref, mm(hit_ref[0], normed_ref[...]))


def merge(keep, other, hid, fgain, hit):
    fixed = lambda i: (0, 0)
    return pl.pallas_call(
        merge_kernel,
        grid=(BLOCKS,),
        in_specs=[pl.BlockSpec((TOK, D), fixed)] * 3
        + [
            pl.BlockSpec((1, D), fixed),
            pl.BlockSpec((1, SB * MAIN + SB, TOK), lambda i: (i, 0, 0)),
        ],
        out_specs=[
            pl.BlockSpec((TOK, D), fixed),
            pl.BlockSpec((TOK, D), fixed),
            pl.BlockSpec((SB, ROWS, QW), lambda i: (i, 0, 0)),
        ],
        out_shape=[jax.ShapeDtypeStruct((TOK, D), bf16)] * 2
        + [jax.ShapeDtypeStruct((EXPERTS, ROWS, QW), bf16)],
        compiler_params=params(BIG),
        cost_estimate=pl.CostEstimate(flops=1 << 31, bytes_accessed=12 << 20, transcendentals=0),
        name="merge",
    )(keep, other, hid, fgain, hit)


def shift_z(v, k):
    return lax.ppermute(v, "seq", [(s, (s + 2 * k) % 8) for s in range(8)])


def shift_x(v, k):
    return lax.ppermute(v, "dp", [(d, d // 4 * 4 + (d + k) % 4) for d in range(16)])


def shift_y(v, k):
    return lax.ppermute(v, "dp", [(d, (d + 4 * k) % 16) for d in range(16)])


def swap_cores(v):
    return lax.ppermute(v, "seq", [(s, s ^ 1) for s in range(8)])


def fetch_weight(w, x, y):
    a = lax.dynamic_slice(w, (x * LANES, 0), (LANES, HALF))
    b = lax.dynamic_slice(w, (y * LANES, HALF), (LANES, HALF))
    slab = jnp.stack([a, b])
    return near(slab, shift_z)


def slabs(pair):
    got = pair + [jnp.concatenate(far(pair, shift_z), axis=1)]
    return jnp.stack([v[0] for v in got]), jnp.stack([v[1] for v in got])


def near(v, shift):
    return [shift(v, 1), shift(v, -1)]


def far(pair, shift):
    h = LANES // 2
    return [shift(pair[0][:, :h], 1), shift(pair[1][:, h:], -1)]


def slot_hits(rank, half):
    r3 = jnp.broadcast_to(rank[:, None, :], (SB, MAIN, TOK))
    c = lax.broadcasted_iota(jnp.int32, (SB, MAIN, TOK), 1) + half * MAIN
    main = (r3 == c.astype(f32)).reshape(SB * MAIN, TOK)
    return main, rank == float(2 * MAIN + half)


def route_kernel(ids_ref, rw_ref, hit_ref, wgt_ref):
    e = lax.broadcasted_iota(jnp.int32, (EXPERTS, TOK), 0)
    member = jnp.zeros((EXPERTS, TOK), f32)
    weight = jnp.zeros((EXPERTS, TOK), f32)
    for k in range(TOP):
        hit = ids_ref[k : k + 1, :] == e
        member += jnp.where(hit, 1.0, 0.0)
        weight += jnp.where(hit, rw_ref[k : k + 1, :], 0.0)
    r = lax.broadcasted_iota(jnp.int32, (TOK, TOK), 0)
    c = lax.broadcasted_iota(jnp.int32, (TOK, TOK), 1)
    before = (r < c).astype(f32).astype(bf16)
    rank = jnp.where(member > 0.5, mm(member.astype(bf16), before), -1.0)
    for half in range(2):
        for i in range(BLOCKS):
            rows = slice(i * SB, (i + 1) * SB)
            main, over = slot_hits(rank[rows], half)
            wt = weight[rows]
            wm = jnp.broadcast_to(wt[:, None, :], (SB, MAIN, TOK)).reshape(SB * MAIN, TOK)
            hit = jnp.concatenate([main.astype(f32), over.astype(f32)], axis=0)
            hit_ref[half, i] = hit.astype(bf16)
            w = hit * jnp.concatenate([wm, wt], axis=0)
            wgt_ref[half, i] = w.T.astype(bf16)


def route_tables(ids_t, rw_t):
    vm = pl.BlockSpec(memory_space=pltpu.VMEM)
    n = SB * MAIN + SB
    return pl.pallas_call(
        route_kernel,
        in_specs=[vm, vm],
        out_specs=[vm, vm],
        out_shape=[
            jax.ShapeDtypeStruct((2, BLOCKS, n, TOK), bf16),
            jax.ShapeDtypeStruct((2, BLOCKS, TOK, n), bf16),
        ],
        compiler_params=pltpu.CompilerParams(vmem_limit_bytes=32 << 20),
        cost_estimate=pl.CostEstimate(flops=1 << 28, bytes_accessed=3 << 20, transcendentals=0),
        name="route_tables",
    )(ids_t, rw_t)


def over_perm(transposed=False):
    n = SB * NQ
    r = lax.broadcasted_iota(jnp.int32, (n, n), 1 if transposed else 0)
    c = lax.broadcasted_iota(jnp.int32, (n, n), 0 if transposed else 1)
    return (c == (r % SB) * NQ + r // SB).astype(f32).astype(bf16)


def unpack(ref):
    n = SB * NQ
    over = mm(over_perm(), ref[:, NQ * MAIN :, :].reshape(n, QW)).astype(bf16)
    parts = []
    for q in range(NQ):
        main = ref[:, q * MAIN : (q + 1) * MAIN, :].reshape(SB * MAIN, QW)
        parts.append(jnp.concatenate([main, over[q * SB : (q + 1) * SB]], axis=0))
    return jnp.concatenate(parts, axis=1)


def pack(ref, rows):
    n = SB * MAIN
    for q in range(NQ):
        ref[:, q * MAIN : (q + 1) * MAIN, :] = (
            rows[:n, q * QW : (q + 1) * QW].reshape(SB, MAIN, QW).astype(bf16)
        )
    over = jnp.concatenate([rows[n:, q * QW : (q + 1) * QW] for q in range(NQ)], axis=0)
    over = mm(over_perm(True), over.astype(bf16))
    ref[:, NQ * MAIN :, :] = over.reshape(SB, NQ, QW).astype(bf16)


def dispatch_kernel(hit_ref, x_ref, out_ref):
    pack(out_ref, mm(hit_ref[0], x_ref[...]))


def dispatch(hit, normed):
    n = SB * MAIN + SB
    return pl.pallas_call(
        dispatch_kernel,
        grid=(BLOCKS,),
        in_specs=[
            pl.BlockSpec((1, n, TOK), lambda i: (i, 0, 0)),
            pl.BlockSpec((TOK, D), lambda i: (0, 0)),
        ],
        out_specs=pl.BlockSpec((SB, ROWS, QW), lambda i: (i, 0, 0)),
        out_shape=jax.ShapeDtypeStruct((EXPERTS, ROWS, QW), bf16),
        compiler_params=params(BIG),
        cost_estimate=pl.CostEstimate(flops=1 << 31, bytes_accessed=6 << 20, transcendentals=0),
        name="dispatch",
    )(hit, normed)


def expert_kernel(in_ref, gu_ref, dn_ref, out_ref):
    hidden = mm(unpack(in_ref), gu_ref[0])
    gate = hidden[:, :FF]
    active = (gate / (1.0 + jnp.exp(-gate)) * hidden[:, FF:]).astype(bf16)
    pack(out_ref, mm(active, dn_ref[0]))


def expert_ffn(arrived, gate_up, down):
    n = arrived.shape[0]
    return pl.pallas_call(
        expert_kernel,
        grid=(n // SB,),
        in_specs=[
            pl.BlockSpec((SB, ROWS, QW), lambda i: (i, 0, 0)),
            pl.BlockSpec((1, D, 2 * FF), lambda i: (0, 0, 0), pipeline_mode=pl.Buffered(1)),
            pl.BlockSpec((1, FF, D), lambda i: (0, 0, 0), pipeline_mode=pl.Buffered(1)),
        ],
        out_specs=pl.BlockSpec((SB, ROWS, QW), lambda i: (i, 0, 0)),
        out_shape=jax.ShapeDtypeStruct(arrived.shape, bf16),
        compiler_params=params(BIG),
        cost_estimate=pl.CostEstimate(flops=11 << 30, bytes_accessed=20 << 20, transcendentals=1 << 20),
        name="expert_ffn",
    )(arrived, gate_up, down)


def combine_kernel(wgt_ref, ret_ref, base_ref, out_ref, acc_ref):
    i = pl.program_id(0)
    part = mm(wgt_ref[0], unpack(ret_ref))

    @pl.when(i == 0)
    def _():
        acc_ref[...] = part

    @pl.when(i > 0)
    def _():
        acc_ref[...] += part

    cols = pl.ds(pl.multiple_of(i * (D // BLOCKS), D // BLOCKS), D // BLOCKS)
    acc_ref[:, cols] += base_ref[...].astype(f32)

    @pl.when(i == pl.num_programs(0) - 1)
    def _():
        out_ref[...] = acc_ref[...].astype(out_ref.dtype)


def combine(wgt, returned, base, kind):
    n = SB * MAIN + SB
    return pl.pallas_call(
        combine_kernel,
        grid=(BLOCKS,),
        in_specs=[
            pl.BlockSpec((1, TOK, n), lambda i: (i, 0, 0)),
            pl.BlockSpec((SB, ROWS, QW), lambda i: (i, 0, 0)),
            pl.BlockSpec((TOK, D // BLOCKS), lambda i: (0, i)),
        ],
        out_specs=pl.BlockSpec((TOK, D), lambda i: (0, 0)),
        out_shape=jax.ShapeDtypeStruct((TOK, D), kind),
        scratch_shapes=[pltpu.VMEM((TOK, D), f32)],
        compiler_params=params(BIG),
        cost_estimate=pl.CostEstimate(flops=1 << 32, bytes_accessed=9 << 20, transcendentals=0),
        name="combine",
    )(wgt, returned, base)


def body(
    hidden_in, mix_values, mix_gate, state_proj, step_raw, step_bias, decay_rate, skip_gain,
    norm_gain, out_weight, ffn_gain, expert_ids, route_weights, gate_up, down_proj, doc_lengths,
):
    both = ("dp", "seq")
    seq_rank = lax.axis_index("seq")
    dp_rank = lax.axis_index("dp")
    scal = jnp.concatenate([doc_lengths[0], (seq_rank * TOK).astype(jnp.int32)[None]])

    x, y, z, core = dp_rank % 4, dp_rank // 4, seq_rank // 2, seq_rank % 2
    around = jnp.array([0, -1, 1, 2], jnp.int32)
    zs, xs_at, ys_at = ((v + around) % 4 for v in (z, x, y))
    order = jnp.concatenate([zs, xs_at, ys_at]).astype(jnp.int32)
    near_z = fetch_weight(out_weight, x, y)

    hit, wgt = route_tables(expert_ids.T, route_weights.T)
    fresh, cum, xs = span_states(
        scal, step_raw.T, step_bias[None], decay_rate[None], mix_values, state_proj
    )
    fresh, near_z = lax.optimization_barrier((fresh, near_z))
    xa, yb = slabs(near_z)
    near_x, near_y = near(xa, shift_x), near(yb, shift_y)
    fresh = lax.all_to_all(fresh, "seq", split_axis=0, concat_axis=0, tiled=True)
    carry = prefix(scal, fresh)
    carry, near_x, near_y = lax.optimization_barrier((carry, near_x, near_y))
    far_x, far_y = far(near_x, shift_x), far(near_y, shift_y)
    carry = lax.all_to_all(carry, "seq", split_axis=0, concat_axis=0, tiled=True)
    mixed = functools.partial(
        mixer, x=mix_values, z=mix_gate, p=state_proj, xs=xs, cum=cum, skip=skip_gain[None],
        gain=norm_gain[None],
    )
    other = mixed(jnp.concatenate([scal, (1 - core)[None]]), carry=carry)
    carry, other, far_x, far_y = lax.optimization_barrier((carry, other, far_x, far_y))
    theirs = swap_cores(other)
    mine = mixed(jnp.concatenate([scal, core[None]]), carry=carry)
    slices = [xa] + near_x + far_x + [yb] + near_y + far_y
    keep, send = project(order, mine, theirs, out_weight, slices)
    merged, normed, first = merge(keep, swap_cores(send), hidden_in, ffn_gain[None], hit[0])

    def exchange(v):
        return lax.all_to_all(v, both, split_axis=0, concat_axis=0, tiled=True)

    arrived = [exchange(first), exchange(dispatch(hit[1], normed))]
    returned = [exchange(expert_ffn(a, gate_up, down_proj)) for a in arrived]
    partial = combine(wgt[0], returned[0], merged, f32)
    return combine(wgt[1], returned[1], partial, bf16)


def solution(mesh):
    tok = P(("dp", "seq"), None)
    in_specs = (
        tok, tok, tok, tok, tok, P(), P(), P(), P(), P("seq", None), P(), tok, tok,
        P(("dp", "seq"), None, None), P(("dp", "seq"), None, None), P("dp", None),
    )
    return jax.shard_map(body, mesh=mesh, in_specs=in_specs, out_specs=tok, check_vma=False)
```

```python
import functools

import jax
import jax.numpy as jnp
from jax import lax
from jax.experimental import pallas as pl
from jax.experimental.pallas import tpu as pltpu
from jax.sharding import PartitionSpec as P

D = 2048
HEADS = 64
HEADDIM = 64
STATE = 128
GROUPS = 8
HPG = HEADS // GROUPS
CH = HPG * HEADDIM
FF = 768
TOP = 8
TOK = 256
EXPERTS = 128
EPS = 1e-05
MAIN = 8
ROWS = 72
QW = 256
NQ = 8
SB = 32
BIG = 58
BLOCKS = EXPERTS // SB
SLICES = 4
LANES = CH // SLICES
HALF = D // 2

f32 = jnp.float32
bf16 = jnp.bfloat16


def params(limit_mib, n=1):
    return pltpu.CompilerParams(
        vmem_limit_bytes=limit_mib << 20, dimension_semantics=("arbitrary",) * n
    )


def mm(a, b):
    return jnp.dot(a, b, preferred_element_type=f32)


def mm_t(a, b, da, db):
    return lax.dot_general(a, b, (((da,), (db,)), ((), ())), preferred_element_type=f32)


def split2(v):
    hi = v.astype(bf16)
    lo = (v - hi.astype(f32)).astype(bf16)
    return hi, lo


def spread(v, e):
    hi, lo = split2(v)
    return mm(hi, e) + mm(lo, e)


def head_onehot(g):
    h = lax.broadcasted_iota(jnp.int32, (HEADS, CH), 0)
    c = lax.broadcasted_iota(jnp.int32, (HEADS, CH), 1)
    return (h == g * HPG + c // HEADDIM).astype(f32).astype(bf16)


def segments(s_ref, shape, dim):
    return segment_at(s_ref, s_ref[3] + lax.broadcasted_iota(jnp.int32, shape, dim))


def segment_at(s_ref, pos):
    b0 = s_ref[0]
    b1 = b0 + s_ref[1]
    b2 = b1 + s_ref[2]
    return sum((pos >= b).astype(jnp.int32) for b in (b0, b1, b2))


def segment_before(s_ref, start):
    return jnp.where(start == 0, -1, segment_at(s_ref, start - 1))


def state_kernel(s_ref, raw_ref, bias_ref, rate_ref, x_ref, p_ref, fresh_ref, cum_ref, xs_ref, a_s, e_s):
    g = pl.program_id(0)

    @pl.when(g == 0)
    def _():
        v = raw_ref[...].astype(f32).T + bias_ref[...]
        step = jnp.maximum(v, 0.0) + jnp.log(1.0 + jnp.exp(-jnp.abs(v)))
        logd = -step * rate_ref[...] * (1.0 / 2048.0)
        r = lax.broadcasted_iota(jnp.int32, (TOK, TOK), 0)
        c = lax.broadcasted_iota(jnp.int32, (TOK, TOK), 1)
        tri = (r >= c).astype(f32)
        cum = jnp.dot(tri, logd, preferred_element_type=f32, precision=lax.Precision.HIGHEST)
        cum_ref[...] = cum
        a_s[...] = step * jnp.exp(-cum)
        e_s[...] = jnp.exp(cum[TOK - 8 :, :])

    e = head_onehot(g)
    xs = (x_ref[...].astype(f32) * spread(a_s[...], e)).astype(bf16)
    xs_ref[...] = xs
    last = segment_at(s_ref, s_ref[3] + TOK - 1)
    b = jnp.where(segments(s_ref, (TOK, STATE), 0) == last, p_ref[:, :STATE].astype(f32), 0.0).astype(bf16)
    end = spread(e_s[...], e)[7:8, :]
    fresh_ref[0, :STATE, :] = (mm_t(b, xs, 0, 0) * end).astype(bf16)
    hi = end.astype(bf16).astype(f32)
    row = lax.broadcasted_iota(jnp.int32, (16, CH), 0)
    tail = jnp.where(row == 0, hi, jnp.where(row == 1, end - hi, 0.0))
    fresh_ref[0, STATE:, :] = tail.astype(bf16)


def span_states(scal, raw, bias, rate, x, p):
    smem = pl.BlockSpec(memory_space=pltpu.SMEM)
    return pl.pallas_call(
        state_kernel,
        grid=(GROUPS,),
        in_specs=[
            smem,
            pl.BlockSpec((HEADS, TOK), lambda g: (0, 0)),
            pl.BlockSpec((1, HEADS), lambda g: (0, 0)),
            pl.BlockSpec((1, HEADS), lambda g: (0, 0)),
            pl.BlockSpec((TOK, CH), lambda g: (0, g)),
            pl.BlockSpec((TOK, 2 * STATE), lambda g: (0, g)),
        ],
        out_specs=[
            pl.BlockSpec((1, STATE + 16, CH), lambda g: (g, 0, 0)),
            pl.BlockSpec((TOK, HEADS), lambda g: (0, 0)),
            pl.BlockSpec((TOK, CH), lambda g: (0, g)),
        ],
        out_shape=[
            jax.ShapeDtypeStruct((GROUPS, STATE + 16, CH), bf16),
            jax.ShapeDtypeStruct((TOK, HEADS), f32),
            jax.ShapeDtypeStruct((TOK, HEADS * HEADDIM), bf16),
        ],
        scratch_shapes=[pltpu.VMEM((TOK, HEADS), f32), pltpu.VMEM((8, HEADS), f32)],
        compiler_params=params(BIG),
        cost_estimate=pl.CostEstimate(flops=1 << 31, bytes_accessed=30 << 20, transcendentals=1 << 20),
        name="span_states",
    )(scal, raw, bias, rate, x, p)


def prefix_kernel(s_ref, in_ref, out_ref):
    carry = jnp.zeros((STATE, CH), f32)
    for r in range(8):
        out_ref[r] = carry.astype(bf16)
        tail = in_ref[r, STATE:, :].astype(f32)
        keep = tail[0:1, :] + tail[1:2, :]
        start = r * TOK
        same = segment_at(s_ref, start + TOK - 1) == segment_before(s_ref, jnp.int32(start))
        keep = keep * same.astype(f32)
        carry = carry * keep + in_ref[r, :STATE, :].astype(f32)


def prefix(scal, fresh):
    return pl.pallas_call(
        prefix_kernel,
        in_specs=[pl.BlockSpec(memory_space=pltpu.SMEM), pl.BlockSpec(memory_space=pltpu.VMEM)],
        out_specs=pl.BlockSpec(memory_space=pltpu.VMEM),
        out_shape=jax.ShapeDtypeStruct((8, STATE, CH), bf16),
        compiler_params=pltpu.CompilerParams(vmem_limit_bytes=16 << 20),
        name="span_prefix",
    )(scal, fresh)


def mixer_kernel(s_ref, x_ref, z_ref, p_ref, xs_ref, cum_ref, carry_ref, skip_ref, gain_ref, n_ref):
    g = pl.program_id(0)
    e = head_onehot(g)
    b, c = p_ref[:, :STATE], p_ref[:, STATE:]
    scores = mm_t(c, b, 1, 1)
    i = lax.broadcasted_iota(jnp.int32, (TOK, TOK), 0)
    j = lax.broadcasted_iota(jnp.int32, (TOK, TOK), 1)
    ok = (i >= j) & (segments(s_ref, (TOK, TOK), 0) == segments(s_ref, (TOK, TOK), 1))
    m = jnp.where(ok, scores, 0.0).astype(bf16)
    before = segment_before(s_ref, s_ref[3])
    cl = jnp.where(segments(s_ref, (TOK, STATE), 0) == before, c.astype(f32), 0.0).astype(bf16)
    acc = mm(m, xs_ref[...]) + mm(cl, carry_ref[0])
    x = x_ref[...].astype(f32)
    skip = spread(jnp.broadcast_to(skip_ref[...], (8, HEADS)), e)[0:1, :]
    mixed = acc * spread(jnp.exp(cum_ref[...]), e) + skip * x
    z = z_ref[...].astype(f32)
    u = mixed * (z / (1.0 + jnp.exp(-z)))
    ms = jnp.mean(u * u, axis=-1, keepdims=True)
    n = (u * lax.rsqrt(ms + EPS) * gain_ref[...]).astype(bf16)
    for k in range(SLICES):
        n_ref[0, k] = n[:, k * LANES : (k + 1) * LANES]


def mixer(scal, x, z, p, xs, cum, carry, skip, gain):
    fixed = lambda g: (0, 0)
    col = lambda g: (0, g)
    return pl.pallas_call(
        mixer_kernel,
        grid=(GROUPS,),
        in_specs=[
            pl.BlockSpec(memory_space=pltpu.SMEM),
            pl.BlockSpec((TOK, CH), col),
            pl.BlockSpec((TOK, CH), col),
            pl.BlockSpec((TOK, 2 * STATE), col),
            pl.BlockSpec((TOK, CH), col),
            pl.BlockSpec((TOK, HEADS), fixed),
            pl.BlockSpec((1, STATE, CH), lambda g: (g, 0, 0)),
            pl.BlockSpec((1, HEADS), fixed),
            pl.BlockSpec((1, CH), col),
        ],
        out_specs=pl.BlockSpec((1, SLICES, TOK, LANES), lambda g: (g, 0, 0, 0)),
        out_shape=jax.ShapeDtypeStruct((GROUPS, SLICES, TOK, LANES), bf16),
        compiler_params=params(50),
        cost_estimate=pl.CostEstimate(flops=1 << 31, bytes_accessed=40 << 20, transcendentals=1 << 21),
        name="mixer",
    )(scal, x, z, p, xs, cum, carry, skip, gain)


def project_kernel(s_ref, mine_ref, theirs_ref, own_ref, *refs):
    w_refs, (keep_ref, send_ref, acc_ref) = refs[:10], refs[10:]
    t = pl.program_id(0)

    def lhs(at):
        parts = []
        for k in range(SLICES):
            j = k if at is None else s_ref[at + k]
            parts.append(jnp.concatenate([mine_ref[0, j], theirs_ref[0, j]], axis=0))
        return jnp.concatenate(parts, axis=1)

    @pl.when(t == 0)
    def _():
        acc_ref[...] = mm(lhs(None), own_ref[...])

    @pl.when(t > 0)
    def _():
        for h in range(2):
            w = jnp.concatenate([r[0] for r in w_refs[5 * h : 5 * h + 5]], axis=0)
            acc_ref[:, h * HALF : (h + 1) * HALF] += mm(lhs(8 + 4 * h), w)

    @pl.when(t == pl.num_programs(0) - 1)
    def _():
        keep_ref[...] = acc_ref[:TOK]
        send_ref[...] = acc_ref[TOK:].astype(bf16)


def project(scal, mine, theirs, own, slices):
    fixed = lambda t, s: (0, 0)
    return pl.pallas_call(
        project_kernel,
        grid_spec=pltpu.PrefetchScalarGridSpec(
            num_scalar_prefetch=1,
            grid=(4,),
            in_specs=[
                pl.BlockSpec((1, SLICES, TOK, LANES), lambda t, s: (s[t], 0, 0, 0)),
                pl.BlockSpec((1, SLICES, TOK, LANES), lambda t, s: (s[4 + t], 0, 0, 0)),
                pl.BlockSpec((CH, D), fixed),
            ]
            + [
                pl.BlockSpec((1, rows, HALF), lambda t, s: (jnp.maximum(t - 1, 0), 0, 0))
                for rows in (LANES, LANES, LANES, LANES // 2, LANES // 2)
            ]
            * 2,
            out_specs=[pl.BlockSpec((TOK, D), fixed), pl.BlockSpec((TOK, D), fixed)],
            scratch_shapes=[pltpu.VMEM((2 * TOK, D), f32)],
        ),
        out_shape=[jax.ShapeDtypeStruct((TOK, D), f32), jax.ShapeDtypeStruct((TOK, D), bf16)],
        compiler_params=params(48),
        cost_estimate=pl.CostEstimate(flops=1 << 32, bytes_accessed=14 << 20, transcendentals=0),
        name="project",
    )(scal, mine, theirs, own, *slices)


def merge_kernel(keep_ref, other_ref, hid_ref, fgain_ref, hit_ref, merged_ref, normed_ref, out_ref):
    @pl.when(pl.program_id(0) == 0)
    def _():
        total = keep_ref[...] + other_ref[...].astype(f32)
        merged = (hid_ref[...].astype(f32) + total).astype(bf16)
        merged_ref[...] = merged
        mf = merged.astype(f32)
        sq = jnp.mean(mf * mf, axis=-1, keepdims=True)
        normed_ref[...] = (mf * lax.rsqrt(sq + EPS) * fgain_ref[...]).astype(bf16)

    pack(out_ref, mm(hit_ref[0], normed_ref[...]))


def merge(keep, other, hid, fgain, hit):
    fixed = lambda i: (0, 0)
    return pl.pallas_call(
        merge_kernel,
        grid=(BLOCKS,),
        in_specs=[pl.BlockSpec((TOK, D), fixed)] * 3
        + [
            pl.BlockSpec((1, D), fixed),
            pl.BlockSpec((1, SB * MAIN + SB, TOK), lambda i: (i, 0, 0)),
        ],
        out_specs=[
            pl.BlockSpec((TOK, D), fixed),
            pl.BlockSpec((TOK, D), fixed),
            pl.BlockSpec((SB, ROWS, QW), lambda i: (i, 0, 0)),
        ],
        out_shape=[jax.ShapeDtypeStruct((TOK, D), bf16)] * 2
        + [jax.ShapeDtypeStruct((EXPERTS, ROWS, QW), bf16)],
        compiler_params=params(52),
        cost_estimate=pl.CostEstimate(flops=1 << 31, bytes_accessed=12 << 20, transcendentals=0),
        name="merge",
    )(keep, other, hid, fgain, hit)


def shift_z(v, k):
    return lax.ppermute(v, "seq", [(s, (s + 2 * k) % 8) for s in range(8)])


def shift_x(v, k):
    return lax.ppermute(v, "dp", [(d, d // 4 * 4 + (d + k) % 4) for d in range(16)])


def shift_y(v, k):
    return lax.ppermute(v, "dp", [(d, (d + 4 * k) % 16) for d in range(16)])


def swap_cores(v):
    return lax.ppermute(v, "seq", [(s, s ^ 1) for s in range(8)])


def fetch_weight(w, x, y):
    a = lax.dynamic_slice(w, (x * LANES, 0), (LANES, HALF))
    b = lax.dynamic_slice(w, (y * LANES, HALF), (LANES, HALF))
    slab = jnp.stack([a, b])
    return near(slab, shift_z)


def slabs(pair):
    got = pair + [jnp.concatenate(far(pair, shift_z), axis=1)]
    return jnp.stack([v[0] for v in got]), jnp.stack([v[1] for v in got])


def near(v, shift):
    return [shift(v, 1), shift(v, -1)]


def far(pair, shift):
    h = LANES // 2
    return [shift(pair[0][:, :h], 1), shift(pair[1][:, h:], -1)]


def slot_hits(rank, half):
    r3 = jnp.broadcast_to(rank[:, None, :], (SB, MAIN, TOK))
    c = lax.broadcasted_iota(jnp.int32, (SB, MAIN, TOK), 1) + half * MAIN
    main = (r3 == c.astype(f32)).reshape(SB * MAIN, TOK)
    return main, rank == float(2 * MAIN + half)


def route_kernel(ids_ref, rw_ref, hit_ref, wgt_ref):
    e = lax.broadcasted_iota(jnp.int32, (EXPERTS, TOK), 0)
    member = jnp.zeros((EXPERTS, TOK), f32)
    weight = jnp.zeros((EXPERTS, TOK), f32)
    for k in range(TOP):
        hit = ids_ref[k : k + 1, :] == e
        member += jnp.where(hit, 1.0, 0.0)
        weight += jnp.where(hit, rw_ref[k : k + 1, :], 0.0)
    r = lax.broadcasted_iota(jnp.int32, (TOK, TOK), 0)
    c = lax.broadcasted_iota(jnp.int32, (TOK, TOK), 1)
    before = (r < c).astype(f32).astype(bf16)
    rank = jnp.where(member > 0.5, mm(member.astype(bf16), before), -1.0)
    for half in range(2):
        for i in range(BLOCKS):
            rows = slice(i * SB, (i + 1) * SB)
            main, over = slot_hits(rank[rows], half)
            wt = weight[rows]
            wm = jnp.broadcast_to(wt[:, None, :], (SB, MAIN, TOK)).reshape(SB * MAIN, TOK)
            hit = jnp.concatenate([main.astype(f32), over.astype(f32)], axis=0)
            hit_ref[half, i] = hit.astype(bf16)
            w = hit * jnp.concatenate([wm, wt], axis=0)
            wgt_ref[half, i] = w.T.astype(bf16)


def route_tables(ids_t, rw_t):
    vm = pl.BlockSpec(memory_space=pltpu.VMEM)
    n = SB * MAIN + SB
    return pl.pallas_call(
        route_kernel,
        in_specs=[vm, vm],
        out_specs=[vm, vm],
        out_shape=[
            jax.ShapeDtypeStruct((2, BLOCKS, n, TOK), bf16),
            jax.ShapeDtypeStruct((2, BLOCKS, TOK, n), bf16),
        ],
        compiler_params=pltpu.CompilerParams(vmem_limit_bytes=32 << 20),
        cost_estimate=pl.CostEstimate(flops=1 << 28, bytes_accessed=3 << 20, transcendentals=0),
        name="route_tables",
    )(ids_t, rw_t)


def over_perm(transposed=False):
    n = SB * NQ
    r = lax.broadcasted_iota(jnp.int32, (n, n), 1 if transposed else 0)
    c = lax.broadcasted_iota(jnp.int32, (n, n), 0 if transposed else 1)
    return (c == (r % SB) * NQ + r // SB).astype(f32).astype(bf16)


def unpack(ref):
    n = SB * NQ
    over = mm(over_perm(), ref[:, NQ * MAIN :, :].reshape(n, QW)).astype(bf16)
    parts = []
    for q in range(NQ):
        main = ref[:, q * MAIN : (q + 1) * MAIN, :].reshape(SB * MAIN, QW)
        parts.append(jnp.concatenate([main, over[q * SB : (q + 1) * SB]], axis=0))
    return jnp.concatenate(parts, axis=1)


def pack(ref, rows):
    n = SB * MAIN
    for q in range(NQ):
        ref[:, q * MAIN : (q + 1) * MAIN, :] = (
            rows[:n, q * QW : (q + 1) * QW].reshape(SB, MAIN, QW).astype(bf16)
        )
    over = jnp.concatenate([rows[n:, q * QW : (q + 1) * QW] for q in range(NQ)], axis=0)
    over = mm(over_perm(True), over.astype(bf16))
    ref[:, NQ * MAIN :, :] = over.reshape(SB, NQ, QW).astype(bf16)


def dispatch_kernel(hit_ref, x_ref, out_ref):
    pack(out_ref, mm(hit_ref[0], x_ref[...]))


def dispatch(hit, normed):
    n = SB * MAIN + SB
    return pl.pallas_call(
        dispatch_kernel,
        grid=(BLOCKS,),
        in_specs=[
            pl.BlockSpec((1, n, TOK), lambda i: (i, 0, 0)),
            pl.BlockSpec((TOK, D), lambda i: (0, 0)),
        ],
        out_specs=pl.BlockSpec((SB, ROWS, QW), lambda i: (i, 0, 0)),
        out_shape=jax.ShapeDtypeStruct((EXPERTS, ROWS, QW), bf16),
        compiler_params=params(BIG),
        cost_estimate=pl.CostEstimate(flops=1 << 31, bytes_accessed=6 << 20, transcendentals=0),
        name="dispatch",
    )(hit, normed)


def expert_kernel(in_ref, gu_ref, dn_ref, out_ref):
    hidden = mm(unpack(in_ref), gu_ref[0])
    gate = hidden[:, :FF]
    active = (gate / (1.0 + jnp.exp(-gate)) * hidden[:, FF:]).astype(bf16)
    pack(out_ref, mm(active, dn_ref[0]))


def expert_ffn(arrived, gate_up, down):
    n = arrived.shape[0]
    return pl.pallas_call(
        expert_kernel,
        grid=(n // SB,),
        in_specs=[
            pl.BlockSpec((SB, ROWS, QW), lambda i: (i, 0, 0)),
            pl.BlockSpec((1, D, 2 * FF), lambda i: (0, 0, 0), pipeline_mode=pl.Buffered(1)),
            pl.BlockSpec((1, FF, D), lambda i: (0, 0, 0), pipeline_mode=pl.Buffered(1)),
        ],
        out_specs=pl.BlockSpec((SB, ROWS, QW), lambda i: (i, 0, 0)),
        out_shape=jax.ShapeDtypeStruct(arrived.shape, bf16),
        compiler_params=params(BIG),
        cost_estimate=pl.CostEstimate(flops=11 << 30, bytes_accessed=20 << 20, transcendentals=1 << 20),
        name="expert_ffn",
    )(arrived, gate_up, down)


def combine_kernel(wgt_ref, ret_ref, base_ref, out_ref, acc_ref):
    i = pl.program_id(0)
    part = mm(wgt_ref[0], unpack(ret_ref))

    @pl.when(i == 0)
    def _():
        acc_ref[...] = part

    @pl.when(i > 0)
    def _():
        acc_ref[...] += part

    cols = pl.ds(pl.multiple_of(i * (D // BLOCKS), D // BLOCKS), D // BLOCKS)
    acc_ref[:, cols] += base_ref[...].astype(f32)

    @pl.when(i == pl.num_programs(0) - 1)
    def _():
        out_ref[...] = acc_ref[...].astype(out_ref.dtype)


def combine(wgt, returned, base, kind):
    n = SB * MAIN + SB
    return pl.pallas_call(
        combine_kernel,
        grid=(BLOCKS,),
        in_specs=[
            pl.BlockSpec((1, TOK, n), lambda i: (i, 0, 0)),
            pl.BlockSpec((SB, ROWS, QW), lambda i: (i, 0, 0)),
            pl.BlockSpec((TOK, D // BLOCKS), lambda i: (0, i)),
        ],
        out_specs=pl.BlockSpec((TOK, D), lambda i: (0, 0)),
        out_shape=jax.ShapeDtypeStruct((TOK, D), kind),
        scratch_shapes=[pltpu.VMEM((TOK, D), f32)],
        compiler_params=params(BIG),
        cost_estimate=pl.CostEstimate(flops=1 << 32, bytes_accessed=9 << 20, transcendentals=0),
        name="combine",
    )(wgt, returned, base)


def body(
    hidden_in, mix_values, mix_gate, state_proj, step_raw, step_bias, decay_rate, skip_gain,
    norm_gain, out_weight, ffn_gain, expert_ids, route_weights, gate_up, down_proj, doc_lengths,
):
    both = ("dp", "seq")
    seq_rank = lax.axis_index("seq")
    dp_rank = lax.axis_index("dp")
    scal = jnp.concatenate([doc_lengths[0], (seq_rank * TOK).astype(jnp.int32)[None]])

    x, y, z, core = dp_rank % 4, dp_rank // 4, seq_rank // 2, seq_rank % 2
    around = jnp.array([0, -1, 1, 2], jnp.int32)
    zs, xs_at, ys_at = ((v + around) % 4 for v in (z, x, y))
    order = jnp.concatenate([zs * 2 + core, zs, xs_at, ys_at]).astype(jnp.int32)
    near_z = fetch_weight(out_weight, x, y)

    hit, wgt = route_tables(expert_ids.T, route_weights.T)
    fresh, cum, xs = span_states(
        scal, step_raw.T, step_bias[None], decay_rate[None], mix_values, state_proj
    )
    fresh, near_z = lax.optimization_barrier((fresh, near_z))
    xa, yb = slabs(near_z)
    near_x, near_y = near(xa, shift_x), near(yb, shift_y)
    fresh = lax.all_to_all(fresh, "seq", split_axis=0, concat_axis=0, tiled=True)
    carry = prefix(scal, fresh)
    carry, near_x, near_y = lax.optimization_barrier((carry, near_x, near_y))
    far_x, far_y = far(near_x, shift_x), far(near_y, shift_y)
    carry = lax.all_to_all(carry, "seq", split_axis=0, concat_axis=0, tiled=True)
    normed_mix = mixer(
        scal, mix_values, mix_gate, state_proj, xs, cum, carry, skip_gain[None], norm_gain[None]
    )
    other = lax.dynamic_index_in_dim(
        normed_mix.reshape(4, 2, SLICES, TOK, LANES), 1 - core, axis=1, keepdims=False
    )
    other, far_x, far_y = lax.optimization_barrier((other, far_x, far_y))
    slices = [xa] + near_x + far_x + [yb] + near_y + far_y
    keep, send = project(order, normed_mix, swap_cores(other), out_weight, slices)
    merged, normed, first = merge(keep, swap_cores(send), hidden_in, ffn_gain[None], hit[0])

    def exchange(v):
        return lax.all_to_all(v, both, split_axis=0, concat_axis=0, tiled=True)

    arrived = [exchange(first), exchange(dispatch(hit[1], normed))]
    returned = [exchange(expert_ffn(a, gate_up, down_proj)) for a in arrived]
    partial = combine(wgt[0], returned[0], merged, f32)
    return combine(wgt[1], returned[1], partial, bf16)


def solution(mesh):
    tok = P(("dp", "seq"), None)
    in_specs = (
        tok, tok, tok, tok, tok, P(), P(), P(), P(), P("seq", None), P(), tok, tok,
        P(("dp", "seq"), None, None), P(("dp", "seq"), None, None), P("dp", None),
    )
    return jax.shard_map(body, mesh=mesh, in_specs=in_specs, out_specs=tok, check_vma=False)
```

```python
import functools

import jax
import jax.numpy as jnp
from jax import lax
from jax.experimental import pallas as pl
from jax.experimental.pallas import tpu as pltpu
from jax.sharding import PartitionSpec as P

D = 2048
HEADS = 64
HEADDIM = 64
STATE = 128
GROUPS = 8
HPG = HEADS // GROUPS
CH = HPG * HEADDIM
FF = 768
TOP = 8
TOK = 256
EXPERTS = 128
EPS = 1e-05
MAIN = 8
ROWS = 72
QW = 256
NQ = 8
SB = 32
BIG = 58
BLOCKS = EXPERTS // SB
SLICES = 4
LANES = CH // SLICES
HALF = D // 2

f32 = jnp.float32
bf16 = jnp.bfloat16


def params(limit_mib, n=1):
    return pltpu.CompilerParams(
        vmem_limit_bytes=limit_mib << 20, dimension_semantics=("arbitrary",) * n
    )


def mm(a, b):
    return jnp.dot(a, b, preferred_element_type=f32)


def mm_t(a, b, da, db):
    return lax.dot_general(a, b, (((da,), (db,)), ((), ())), preferred_element_type=f32)


def split2(v):
    hi = v.astype(bf16)
    lo = (v - hi.astype(f32)).astype(bf16)
    return hi, lo


def spread(v, e):
    hi, lo = split2(v)
    return mm(hi, e) + mm(lo, e)


def head_onehot(g):
    h = lax.broadcasted_iota(jnp.int32, (HEADS, CH), 0)
    c = lax.broadcasted_iota(jnp.int32, (HEADS, CH), 1)
    return (h == g * HPG + c // HEADDIM).astype(f32).astype(bf16)


def segments(s_ref, shape, dim):
    return segment_at(s_ref, s_ref[3] + lax.broadcasted_iota(jnp.int32, shape, dim))


def segment_at(s_ref, pos):
    b0 = s_ref[0]
    b1 = b0 + s_ref[1]
    b2 = b1 + s_ref[2]
    return sum((pos >= b).astype(jnp.int32) for b in (b0, b1, b2))


def segment_before(s_ref, start):
    return jnp.where(start == 0, -1, segment_at(s_ref, start - 1))


def state_kernel(s_ref, raw_ref, bias_ref, rate_ref, x_ref, p_ref, fresh_ref, cum_ref, xs_ref, a_s, e_s):
    g = pl.program_id(0)

    @pl.when(g == 0)
    def _():
        v = raw_ref[...].astype(f32).T + bias_ref[...]
        step = jnp.maximum(v, 0.0) + jnp.log(1.0 + jnp.exp(-jnp.abs(v)))
        logd = -step * rate_ref[...] * (1.0 / 2048.0)
        r = lax.broadcasted_iota(jnp.int32, (TOK, TOK), 0)
        c = lax.broadcasted_iota(jnp.int32, (TOK, TOK), 1)
        tri = (r >= c).astype(f32)
        cum = jnp.dot(tri, logd, preferred_element_type=f32, precision=lax.Precision.HIGHEST)
        cum_ref[...] = cum
        a_s[...] = step * jnp.exp(-cum)
        e_s[...] = jnp.exp(cum[TOK - 8 :, :])

    e = head_onehot(g)
    xs = (x_ref[...].astype(f32) * spread(a_s[...], e)).astype(bf16)
    xs_ref[...] = xs
    last = segment_at(s_ref, s_ref[3] + TOK - 1)
    b = jnp.where(segments(s_ref, (TOK, STATE), 0) == last, p_ref[:, :STATE].astype(f32), 0.0).astype(bf16)
    end = spread(e_s[...], e)[7:8, :]
    fresh_ref[0, :STATE, :] = (mm_t(b, xs, 0, 0) * end).astype(bf16)
    hi = end.astype(bf16).astype(f32)
    row = lax.broadcasted_iota(jnp.int32, (16, CH), 0)
    tail = jnp.where(row == 0, hi, jnp.where(row == 1, end - hi, 0.0))
    fresh_ref[0, STATE:, :] = tail.astype(bf16)


def span_states(scal, raw, bias, rate, x, p):
    smem = pl.BlockSpec(memory_space=pltpu.SMEM)
    return pl.pallas_call(
        state_kernel,
        grid=(GROUPS,),
        in_specs=[
            smem,
            pl.BlockSpec((HEADS, TOK), lambda g: (0, 0)),
            pl.BlockSpec((1, HEADS), lambda g: (0, 0)),
            pl.BlockSpec((1, HEADS), lambda g: (0, 0)),
            pl.BlockSpec((TOK, CH), lambda g: (0, g)),
            pl.BlockSpec((TOK, 2 * STATE), lambda g: (0, g)),
        ],
        out_specs=[
            pl.BlockSpec((1, STATE + 16, CH), lambda g: (g, 0, 0)),
            pl.BlockSpec((TOK, HEADS), lambda g: (0, 0)),
            pl.BlockSpec((TOK, CH), lambda g: (0, g)),
        ],
        out_shape=[
            jax.ShapeDtypeStruct((GROUPS, STATE + 16, CH), bf16),
            jax.ShapeDtypeStruct((TOK, HEADS), f32),
            jax.ShapeDtypeStruct((TOK, HEADS * HEADDIM), bf16),
        ],
        scratch_shapes=[pltpu.VMEM((TOK, HEADS), f32), pltpu.VMEM((8, HEADS), f32)],
        compiler_params=params(BIG),
        cost_estimate=pl.CostEstimate(flops=1 << 31, bytes_accessed=30 << 20, transcendentals=1 << 20),
        name="span_states",
    )(scal, raw, bias, rate, x, p)


def prefix_kernel(s_ref, in_ref, out_ref):
    carry = jnp.zeros((STATE, CH), f32)
    for r in range(8):
        out_ref[r] = carry.astype(bf16)
        tail = in_ref[r, STATE:, :].astype(f32)
        keep = tail[0:1, :] + tail[1:2, :]
        start = r * TOK
        same = segment_at(s_ref, start + TOK - 1) == segment_before(s_ref, jnp.int32(start))
        keep = keep * same.astype(f32)
        carry = carry * keep + in_ref[r, :STATE, :].astype(f32)


def prefix(scal, fresh):
    return pl.pallas_call(
        prefix_kernel,
        in_specs=[pl.BlockSpec(memory_space=pltpu.SMEM), pl.BlockSpec(memory_space=pltpu.VMEM)],
        out_specs=pl.BlockSpec(memory_space=pltpu.VMEM),
        out_shape=jax.ShapeDtypeStruct((8, STATE, CH), bf16),
        compiler_params=pltpu.CompilerParams(vmem_limit_bytes=16 << 20),
        name="span_prefix",
    )(scal, fresh)


def mixer_kernel(s_ref, x_ref, z_ref, p_ref, xs_ref, cum_ref, carry_ref, skip_ref, gain_ref, n_ref):
    g = pl.program_id(0)
    e = head_onehot(g)
    b, c = p_ref[:, :STATE], p_ref[:, STATE:]
    scores = mm_t(c, b, 1, 1)
    i = lax.broadcasted_iota(jnp.int32, (TOK, TOK), 0)
    j = lax.broadcasted_iota(jnp.int32, (TOK, TOK), 1)
    ok = (i >= j) & (segments(s_ref, (TOK, TOK), 0) == segments(s_ref, (TOK, TOK), 1))
    m = jnp.where(ok, scores, 0.0).astype(bf16)
    before = segment_before(s_ref, s_ref[3])
    cl = jnp.where(segments(s_ref, (TOK, STATE), 0) == before, c.astype(f32), 0.0).astype(bf16)
    acc = mm(m, xs_ref[...]) + mm(cl, carry_ref[0])
    x = x_ref[...].astype(f32)
    skip = spread(jnp.broadcast_to(skip_ref[...], (8, HEADS)), e)[0:1, :]
    mixed = acc * spread(jnp.exp(cum_ref[...]), e) + skip * x
    z = z_ref[...].astype(f32)
    u = mixed * (z / (1.0 + jnp.exp(-z)))
    ms = jnp.mean(u * u, axis=-1, keepdims=True)
    n = (u * lax.rsqrt(ms + EPS) * gain_ref[...]).astype(bf16)
    for k in range(SLICES):
        n_ref[0, k] = n[:, k * LANES : (k + 1) * LANES]


def mixer(scal, x, z, p, xs, cum, carry, skip, gain):
    fixed = lambda g: (0, 0)
    col = lambda g: (0, g)
    return pl.pallas_call(
        mixer_kernel,
        grid=(GROUPS,),
        in_specs=[
            pl.BlockSpec(memory_space=pltpu.SMEM),
            pl.BlockSpec((TOK, CH), col),
            pl.BlockSpec((TOK, CH), col),
            pl.BlockSpec((TOK, 2 * STATE), col),
            pl.BlockSpec((TOK, CH), col),
            pl.BlockSpec((TOK, HEADS), fixed),
            pl.BlockSpec((1, STATE, CH), lambda g: (g, 0, 0)),
            pl.BlockSpec((1, HEADS), fixed),
            pl.BlockSpec((1, CH), col),
        ],
        out_specs=pl.BlockSpec((1, SLICES, TOK, LANES), lambda g: (g, 0, 0, 0)),
        out_shape=jax.ShapeDtypeStruct((GROUPS, SLICES, TOK, LANES), bf16),
        compiler_params=params(50),
        cost_estimate=pl.CostEstimate(flops=1 << 31, bytes_accessed=40 << 20, transcendentals=1 << 21),
        name="mixer",
    )(scal, x, z, p, xs, cum, carry, skip, gain)


def project_kernel(s_ref, mine_ref, theirs_ref, own_ref, *refs):
    w_refs, (keep_ref, send_ref, acc_ref) = refs[:10], refs[10:]
    t = pl.program_id(0)

    def lhs(at):
        parts = []
        for k in range(SLICES):
            j = k if at is None else s_ref[at + k]
            parts.append(jnp.concatenate([mine_ref[0, j], theirs_ref[0, j]], axis=0))
        return jnp.concatenate(parts, axis=1)

    @pl.when(t == 0)
    def _():
        acc_ref[...] = mm(lhs(None), own_ref[...])

    @pl.when(t > 0)
    def _():
        for h in range(2):
            w = jnp.concatenate([r[0] for r in w_refs[5 * h : 5 * h + 5]], axis=0)
            acc_ref[:, h * HALF : (h + 1) * HALF] += mm(lhs(8 + 4 * h), w)

    @pl.when(t == pl.num_programs(0) - 1)
    def _():
        keep_ref[...] = acc_ref[:TOK]
        send_ref[...] = acc_ref[TOK:].astype(bf16)


def project(scal, mine, theirs, own, slices):
    fixed = lambda t, s: (0, 0)
    return pl.pallas_call(
        project_kernel,
        grid_spec=pltpu.PrefetchScalarGridSpec(
            num_scalar_prefetch=1,
            grid=(4,),
            in_specs=[
                pl.BlockSpec((1, SLICES, TOK, LANES), lambda t, s: (s[t], 0, 0, 0)),
                pl.BlockSpec((1, SLICES, TOK, LANES), lambda t, s: (s[4 + t], 0, 0, 0)),
                pl.BlockSpec((CH, D), fixed),
            ]
            + [
                pl.BlockSpec((1, rows, HALF), lambda t, s: (jnp.maximum(t - 1, 0), 0, 0))
                for rows in (LANES, LANES, LANES, LANES // 2, LANES // 2)
            ]
            * 2,
            out_specs=[pl.BlockSpec((TOK, D), fixed), pl.BlockSpec((TOK, D), fixed)],
            scratch_shapes=[pltpu.VMEM((2 * TOK, D), f32)],
        ),
        out_shape=[jax.ShapeDtypeStruct((TOK, D), f32), jax.ShapeDtypeStruct((TOK, D), bf16)],
        compiler_params=params(48),
        cost_estimate=pl.CostEstimate(flops=1 << 32, bytes_accessed=14 << 20, transcendentals=0),
        name="project",
    )(scal, mine, theirs, own, *slices)


def merge_kernel(keep_ref, other_ref, hid_ref, fgain_ref, hit_ref, merged_ref, normed_ref, out_ref):
    @pl.when(pl.program_id(0) == 0)
    def _():
        total = keep_ref[...] + other_ref[...].astype(f32)
        merged = (hid_ref[...].astype(f32) + total).astype(bf16)
        merged_ref[...] = merged
        mf = merged.astype(f32)
        sq = jnp.mean(mf * mf, axis=-1, keepdims=True)
        normed_ref[...] = (mf * lax.rsqrt(sq + EPS) * fgain_ref[...]).astype(bf16)

    pack(out_ref, mm(hit_ref[0], normed_ref[...]))


def merge(keep, other, hid, fgain, hit):
    fixed = lambda i: (0, 0)
    return pl.pallas_call(
        merge_kernel,
        grid=(BLOCKS,),
        in_specs=[pl.BlockSpec((TOK, D), fixed)] * 3
        + [
            pl.BlockSpec((1, D), fixed),
            pl.BlockSpec((1, SB * MAIN + SB, TOK), lambda i: (i, 0, 0)),
        ],
        out_specs=[
            pl.BlockSpec((TOK, D), fixed),
            pl.BlockSpec((TOK, D), fixed),
            pl.BlockSpec((SB, ROWS, QW), lambda i: (i, 0, 0)),
        ],
        out_shape=[jax.ShapeDtypeStruct((TOK, D), bf16)] * 2
        + [jax.ShapeDtypeStruct((EXPERTS, ROWS, QW), bf16)],
        compiler_params=params(BIG),
        cost_estimate=pl.CostEstimate(flops=1 << 31, bytes_accessed=12 << 20, transcendentals=0),
        name="merge",
    )(keep, other, hid, fgain, hit)


def shift_z(v, k):
    return lax.ppermute(v, "seq", [(s, (s + 2 * k) % 8) for s in range(8)])


def shift_x(v, k):
    return lax.ppermute(v, "dp", [(d, d // 4 * 4 + (d + k) % 4) for d in range(16)])


def shift_y(v, k):
    return lax.ppermute(v, "dp", [(d, (d + 4 * k) % 16) for d in range(16)])


def swap_cores(v):
    return lax.ppermute(v, "seq", [(s, s ^ 1) for s in range(8)])


def fetch_weight(w, x, y):
    a = lax.dynamic_slice(w, (x * LANES, 0), (LANES, HALF))
    b = lax.dynamic_slice(w, (y * LANES, HALF), (LANES, HALF))
    slab = jnp.stack([a, b])
    return near(slab, shift_z)


def slabs(pair):
    got = pair + [jnp.concatenate(far(pair, shift_z), axis=1)]
    return jnp.stack([v[0] for v in got]), jnp.stack([v[1] for v in got])


def near(v, shift):
    return [shift(v, 1), shift(v, -1)]


def far(pair, shift):
    h = LANES // 2
    return [shift(pair[0][:, :h], 1), shift(pair[1][:, h:], -1)]


def slot_hits(rank, half):
    r3 = jnp.broadcast_to(rank[:, None, :], (SB, MAIN, TOK))
    c = lax.broadcasted_iota(jnp.int32, (SB, MAIN, TOK), 1) + half * MAIN
    main = (r3 == c.astype(f32)).reshape(SB * MAIN, TOK)
    return main, rank == float(2 * MAIN + half)


def route_kernel(ids_ref, rw_ref, hit_ref, wgt_ref):
    e = lax.broadcasted_iota(jnp.int32, (EXPERTS, TOK), 0)
    member = jnp.zeros((EXPERTS, TOK), f32)
    weight = jnp.zeros((EXPERTS, TOK), f32)
    for k in range(TOP):
        hit = ids_ref[k : k + 1, :] == e
        member += jnp.where(hit, 1.0, 0.0)
        weight += jnp.where(hit, rw_ref[k : k + 1, :], 0.0)
    r = lax.broadcasted_iota(jnp.int32, (TOK, TOK), 0)
    c = lax.broadcasted_iota(jnp.int32, (TOK, TOK), 1)
    before = (r < c).astype(f32).astype(bf16)
    rank = jnp.where(member > 0.5, mm(member.astype(bf16), before), -1.0)
    for half in range(2):
        for i in range(BLOCKS):
            rows = slice(i * SB, (i + 1) * SB)
            main, over = slot_hits(rank[rows], half)
            wt = weight[rows]
            wm = jnp.broadcast_to(wt[:, None, :], (SB, MAIN, TOK)).reshape(SB * MAIN, TOK)
            hit = jnp.concatenate([main.astype(f32), over.astype(f32)], axis=0)
            hit_ref[half, i] = hit.astype(bf16)
            w = hit * jnp.concatenate([wm, wt], axis=0)
            wgt_ref[half, i] = w.T.astype(bf16)


def route_tables(ids_t, rw_t):
    vm = pl.BlockSpec(memory_space=pltpu.VMEM)
    n = SB * MAIN + SB
    return pl.pallas_call(
        route_kernel,
        in_specs=[vm, vm],
        out_specs=[vm, vm],
        out_shape=[
            jax.ShapeDtypeStruct((2, BLOCKS, n, TOK), bf16),
            jax.ShapeDtypeStruct((2, BLOCKS, TOK, n), bf16),
        ],
        compiler_params=pltpu.CompilerParams(vmem_limit_bytes=32 << 20),
        cost_estimate=pl.CostEstimate(flops=1 << 28, bytes_accessed=3 << 20, transcendentals=0),
        name="route_tables",
    )(ids_t, rw_t)


def over_perm(transposed=False):
    n = SB * NQ
    r = lax.broadcasted_iota(jnp.int32, (n, n), 1 if transposed else 0)
    c = lax.broadcasted_iota(jnp.int32, (n, n), 0 if transposed else 1)
    return (c == (r % SB) * NQ + r // SB).astype(f32).astype(bf16)


def unpack(ref):
    n = SB * NQ
    over = mm(over_perm(), ref[:, NQ * MAIN :, :].reshape(n, QW)).astype(bf16)
    parts = []
    for q in range(NQ):
        main = ref[:, q * MAIN : (q + 1) * MAIN, :].reshape(SB * MAIN, QW)
        parts.append(jnp.concatenate([main, over[q * SB : (q + 1) * SB]], axis=0))
    return jnp.concatenate(parts, axis=1)


def pack(ref, rows):
    n = SB * MAIN
    for q in range(NQ):
        ref[:, q * MAIN : (q + 1) * MAIN, :] = (
            rows[:n, q * QW : (q + 1) * QW].reshape(SB, MAIN, QW).astype(bf16)
        )
    over = jnp.concatenate([rows[n:, q * QW : (q + 1) * QW] for q in range(NQ)], axis=0)
    over = mm(over_perm(True), over.astype(bf16))
    ref[:, NQ * MAIN :, :] = over.reshape(SB, NQ, QW).astype(bf16)


def dispatch_kernel(hit_ref, x_ref, out_ref):
    pack(out_ref, mm(hit_ref[0], x_ref[...]))


def dispatch(hit, normed):
    n = SB * MAIN + SB
    return pl.pallas_call(
        dispatch_kernel,
        grid=(BLOCKS,),
        in_specs=[
            pl.BlockSpec((1, n, TOK), lambda i: (i, 0, 0)),
            pl.BlockSpec((TOK, D), lambda i: (0, 0)),
        ],
        out_specs=pl.BlockSpec((SB, ROWS, QW), lambda i: (i, 0, 0)),
        out_shape=jax.ShapeDtypeStruct((EXPERTS, ROWS, QW), bf16),
        compiler_params=params(BIG),
        cost_estimate=pl.CostEstimate(flops=1 << 31, bytes_accessed=6 << 20, transcendentals=0),
        name="dispatch",
    )(hit, normed)


def expert_kernel(in_ref, gu_ref, dn_ref, out_ref):
    hidden = mm(unpack(in_ref), gu_ref[0])
    gate = hidden[:, :FF]
    active = (gate / (1.0 + jnp.exp(-gate)) * hidden[:, FF:]).astype(bf16)
    pack(out_ref, mm(active, dn_ref[0]))


def expert_ffn(arrived, gate_up, down):
    n = arrived.shape[0]
    return pl.pallas_call(
        expert_kernel,
        grid=(n // SB,),
        in_specs=[
            pl.BlockSpec((SB, ROWS, QW), lambda i: (i, 0, 0)),
            pl.BlockSpec((1, D, 2 * FF), lambda i: (0, 0, 0), pipeline_mode=pl.Buffered(1)),
            pl.BlockSpec((1, FF, D), lambda i: (0, 0, 0), pipeline_mode=pl.Buffered(1)),
        ],
        out_specs=pl.BlockSpec((SB, ROWS, QW), lambda i: (i, 0, 0)),
        out_shape=jax.ShapeDtypeStruct(arrived.shape, bf16),
        compiler_params=params(BIG),
        cost_estimate=pl.CostEstimate(flops=11 << 30, bytes_accessed=20 << 20, transcendentals=1 << 20),
        name="expert_ffn",
    )(arrived, gate_up, down)


def combine_kernel(wgt_ref, ret_ref, base_ref, out_ref, acc_ref):
    i = pl.program_id(0)
    part = mm(wgt_ref[0], unpack(ret_ref))

    @pl.when(i == 0)
    def _():
        acc_ref[...] = part

    @pl.when(i > 0)
    def _():
        acc_ref[...] += part

    cols = pl.ds(pl.multiple_of(i * (D // BLOCKS), D // BLOCKS), D // BLOCKS)
    acc_ref[:, cols] += base_ref[...].astype(f32)

    @pl.when(i == pl.num_programs(0) - 1)
    def _():
        out_ref[...] = acc_ref[...].astype(out_ref.dtype)


def combine(wgt, returned, base, kind):
    n = SB * MAIN + SB
    return pl.pallas_call(
        combine_kernel,
        grid=(BLOCKS,),
        in_specs=[
            pl.BlockSpec((1, TOK, n), lambda i: (i, 0, 0)),
            pl.BlockSpec((SB, ROWS, QW), lambda i: (i, 0, 0)),
            pl.BlockSpec((TOK, D // BLOCKS), lambda i: (0, i)),
        ],
        out_specs=pl.BlockSpec((TOK, D), lambda i: (0, 0)),
        out_shape=jax.ShapeDtypeStruct((TOK, D), kind),
        scratch_shapes=[pltpu.VMEM((TOK, D), f32)],
        compiler_params=params(48),
        cost_estimate=pl.CostEstimate(flops=1 << 32, bytes_accessed=9 << 20, transcendentals=0),
        name="combine",
    )(wgt, returned, base)


def body(
    hidden_in, mix_values, mix_gate, state_proj, step_raw, step_bias, decay_rate, skip_gain,
    norm_gain, out_weight, ffn_gain, expert_ids, route_weights, gate_up, down_proj, doc_lengths,
):
    both = ("dp", "seq")
    seq_rank = lax.axis_index("seq")
    dp_rank = lax.axis_index("dp")
    scal = jnp.concatenate([doc_lengths[0], (seq_rank * TOK).astype(jnp.int32)[None]])

    x, y, z, core = dp_rank % 4, dp_rank // 4, seq_rank // 2, seq_rank % 2
    around = jnp.array([0, -1, 1, 2], jnp.int32)
    zs, xs_at, ys_at = ((v + around) % 4 for v in (z, x, y))
    order = jnp.concatenate([zs * 2 + core, zs, xs_at, ys_at]).astype(jnp.int32)
    near_z = fetch_weight(out_weight, x, y)

    hit, wgt = route_tables(expert_ids.T, route_weights.T)
    fresh, cum, xs = span_states(
        scal, step_raw.T, step_bias[None], decay_rate[None], mix_values, state_proj
    )
    fresh, near_z = lax.optimization_barrier((fresh, near_z))
    xa, yb = slabs(near_z)
    near_x, near_y = near(xa, shift_x), near(yb, shift_y)
    fresh = lax.all_to_all(fresh, "seq", split_axis=0, concat_axis=0, tiled=True)
    carry = prefix(scal, fresh)
    carry, near_x, near_y = lax.optimization_barrier((carry, near_x, near_y))
    far_x, far_y = far(near_x, shift_x), far(near_y, shift_y)
    carry = lax.all_to_all(carry, "seq", split_axis=0, concat_axis=0, tiled=True)
    normed_mix = mixer(
        scal, mix_values, mix_gate, state_proj, xs, cum, carry, skip_gain[None], norm_gain[None]
    )
    other = lax.dynamic_index_in_dim(
        normed_mix.reshape(4, 2, SLICES, TOK, LANES), 1 - core, axis=1, keepdims=False
    )
    other, far_x, far_y = lax.optimization_barrier((other, far_x, far_y))
    slices = [xa] + near_x + far_x + [yb] + near_y + far_y
    keep, send = project(order, normed_mix, swap_cores(other), out_weight, slices)
    merged, normed, first = merge(keep, swap_cores(send), hidden_in, ffn_gain[None], hit[0])

    def exchange(v):
        return lax.all_to_all(v, both, split_axis=0, concat_axis=0, tiled=True)

    arrived = [exchange(first), exchange(dispatch(hit[1], normed))]
    returned = [exchange(expert_ffn(a, gate_up, down_proj)) for a in arrived]
    partial = combine(wgt[0], returned[0], merged, f32)
    return combine(wgt[1], returned[1], partial, bf16)


def solution(mesh):
    tok = P(("dp", "seq"), None)
    in_specs = (
        tok, tok, tok, tok, tok, P(), P(), P(), P(), P("seq", None), P(), tok, tok,
        P(("dp", "seq"), None, None), P(("dp", "seq"), None, None), P("dp", None),
    )
    return jax.shard_map(body, mesh=mesh, in_specs=in_specs, out_specs=tok, check_vma=False)
```

```python
import functools

import jax
import jax.numpy as jnp
from jax import lax
from jax.experimental import pallas as pl
from jax.experimental.pallas import tpu as pltpu
from jax.sharding import PartitionSpec as P

D = 2048
HEADS = 64
HEADDIM = 64
STATE = 128
GROUPS = 8
HPG = HEADS // GROUPS
CH = HPG * HEADDIM
FF = 768
TOP = 8
TOK = 256
EXPERTS = 128
EPS = 1e-05
MAIN = 8
ROWS = 72
QW = 256
NQ = 8
SB = 32
BIG = 58
BLOCKS = EXPERTS // SB
SLICES = 4
LANES = CH // SLICES
HALF = D // 2

f32 = jnp.float32
bf16 = jnp.bfloat16


def params(limit_mib, n=1):
    return pltpu.CompilerParams(
        vmem_limit_bytes=limit_mib << 20, dimension_semantics=("arbitrary",) * n
    )


def mm(a, b):
    return jnp.dot(a, b, preferred_element_type=f32)


def mm_t(a, b, da, db):
    return lax.dot_general(a, b, (((da,), (db,)), ((), ())), preferred_element_type=f32)


def split2(v):
    hi = v.astype(bf16)
    lo = (v - hi.astype(f32)).astype(bf16)
    return hi, lo


def spread(v, e):
    hi, lo = split2(v)
    return mm(hi, e) + mm(lo, e)


def head_onehot(g):
    h = lax.broadcasted_iota(jnp.int32, (HEADS, CH), 0)
    c = lax.broadcasted_iota(jnp.int32, (HEADS, CH), 1)
    return (h == g * HPG + c // HEADDIM).astype(f32).astype(bf16)


def segments(s_ref, shape, dim):
    return segment_at(s_ref, s_ref[3] + lax.broadcasted_iota(jnp.int32, shape, dim))


def segment_at(s_ref, pos):
    b0 = s_ref[0]
    b1 = b0 + s_ref[1]
    b2 = b1 + s_ref[2]
    return sum((pos >= b).astype(jnp.int32) for b in (b0, b1, b2))


def segment_before(s_ref, start):
    return jnp.where(start == 0, -1, segment_at(s_ref, start - 1))


def state_kernel(s_ref, raw_ref, bias_ref, rate_ref, x_ref, p_ref, fresh_ref, cum_ref, xs_ref, a_s, e_s):
    g = pl.program_id(0)

    @pl.when(g == 0)
    def _():
        v = raw_ref[...].astype(f32).T + bias_ref[...]
        step = jnp.maximum(v, 0.0) + jnp.log(1.0 + jnp.exp(-jnp.abs(v)))
        logd = -step * rate_ref[...] * (1.0 / 2048.0)
        r = lax.broadcasted_iota(jnp.int32, (TOK, TOK), 0)
        c = lax.broadcasted_iota(jnp.int32, (TOK, TOK), 1)
        tri = (r >= c).astype(f32)
        cum = jnp.dot(tri, logd, preferred_element_type=f32, precision=lax.Precision.HIGHEST)
        cum_ref[...] = cum
        a_s[...] = step * jnp.exp(-cum)
        e_s[...] = jnp.exp(cum[TOK - 8 :, :])

    e = head_onehot(g)
    xs = (x_ref[...].astype(f32) * spread(a_s[...], e)).astype(bf16)
    xs_ref[...] = xs
    last = segment_at(s_ref, s_ref[3] + TOK - 1)
    b = jnp.where(segments(s_ref, (TOK, STATE), 0) == last, p_ref[:, :STATE].astype(f32), 0.0).astype(bf16)
    end = spread(e_s[...], e)[7:8, :]
    fresh_ref[0, :STATE, :] = (mm_t(b, xs, 0, 0) * end).astype(bf16)
    hi = end.astype(bf16).astype(f32)
    row = lax.broadcasted_iota(jnp.int32, (16, CH), 0)
    tail = jnp.where(row == 0, hi, jnp.where(row == 1, end - hi, 0.0))
    fresh_ref[0, STATE:, :] = tail.astype(bf16)


def span_states(scal, raw, bias, rate, x, p):
    smem = pl.BlockSpec(memory_space=pltpu.SMEM)
    return pl.pallas_call(
        state_kernel,
        grid=(GROUPS,),
        in_specs=[
            smem,
            pl.BlockSpec((HEADS, TOK), lambda g: (0, 0)),
            pl.BlockSpec((1, HEADS), lambda g: (0, 0)),
            pl.BlockSpec((1, HEADS), lambda g: (0, 0)),
            pl.BlockSpec((TOK, CH), lambda g: (0, g)),
            pl.BlockSpec((TOK, 2 * STATE), lambda g: (0, g)),
        ],
        out_specs=[
            pl.BlockSpec((1, STATE + 16, CH), lambda g: (g, 0, 0)),
            pl.BlockSpec((TOK, HEADS), lambda g: (0, 0)),
            pl.BlockSpec((TOK, CH), lambda g: (0, g)),
        ],
        out_shape=[
            jax.ShapeDtypeStruct((GROUPS, STATE + 16, CH), bf16),
            jax.ShapeDtypeStruct((TOK, HEADS), f32),
            jax.ShapeDtypeStruct((TOK, HEADS * HEADDIM), bf16),
        ],
        scratch_shapes=[pltpu.VMEM((TOK, HEADS), f32), pltpu.VMEM((8, HEADS), f32)],
        compiler_params=params(BIG),
        cost_estimate=pl.CostEstimate(flops=1 << 31, bytes_accessed=30 << 20, transcendentals=1 << 20),
        name="span_states",
    )(scal, raw, bias, rate, x, p)


def prefix_kernel(s_ref, in_ref, out_ref):
    carry = jnp.zeros((STATE, CH), f32)
    for r in range(8):
        out_ref[r] = carry.astype(bf16)
        tail = in_ref[r, STATE:, :].astype(f32)
        keep = tail[0:1, :] + tail[1:2, :]
        start = r * TOK
        same = segment_at(s_ref, start + TOK - 1) == segment_before(s_ref, jnp.int32(start))
        keep = keep * same.astype(f32)
        carry = carry * keep + in_ref[r, :STATE, :].astype(f32)


def prefix(scal, fresh):
    return pl.pallas_call(
        prefix_kernel,
        in_specs=[pl.BlockSpec(memory_space=pltpu.SMEM), pl.BlockSpec(memory_space=pltpu.VMEM)],
        out_specs=pl.BlockSpec(memory_space=pltpu.VMEM),
        out_shape=jax.ShapeDtypeStruct((8, STATE, CH), bf16),
        compiler_params=pltpu.CompilerParams(vmem_limit_bytes=16 << 20),
        name="span_prefix",
    )(scal, fresh)


def mixer_kernel(s_ref, x_ref, z_ref, p_ref, xs_ref, cum_ref, carry_ref, skip_ref, gain_ref, n_ref):
    g = pl.program_id(0)
    e = head_onehot(g)
    b, c = p_ref[:, :STATE], p_ref[:, STATE:]
    scores = mm_t(c, b, 1, 1)
    i = lax.broadcasted_iota(jnp.int32, (TOK, TOK), 0)
    j = lax.broadcasted_iota(jnp.int32, (TOK, TOK), 1)
    ok = (i >= j) & (segments(s_ref, (TOK, TOK), 0) == segments(s_ref, (TOK, TOK), 1))
    m = jnp.where(ok, scores, 0.0).astype(bf16)
    before = segment_before(s_ref, s_ref[3])
    cl = jnp.where(segments(s_ref, (TOK, STATE), 0) == before, c.astype(f32), 0.0).astype(bf16)
    acc = mm(m, xs_ref[...]) + mm(cl, carry_ref[0])
    x = x_ref[...].astype(f32)
    skip = spread(jnp.broadcast_to(skip_ref[...], (8, HEADS)), e)[0:1, :]
    mixed = acc * spread(jnp.exp(cum_ref[...]), e) + skip * x
    z = z_ref[...].astype(f32)
    u = mixed * (z / (1.0 + jnp.exp(-z)))
    ms = jnp.mean(u * u, axis=-1, keepdims=True)
    n = (u * lax.rsqrt(ms + EPS) * gain_ref[...]).astype(bf16)
    for k in range(SLICES):
        n_ref[0, k] = n[:, k * LANES : (k + 1) * LANES]


def mixer(scal, x, z, p, xs, cum, carry, skip, gain):
    fixed = lambda g: (0, 0)
    col = lambda g: (0, g)
    return pl.pallas_call(
        mixer_kernel,
        grid=(GROUPS,),
        in_specs=[
            pl.BlockSpec(memory_space=pltpu.SMEM),
            pl.BlockSpec((TOK, CH), col),
            pl.BlockSpec((TOK, CH), col),
            pl.BlockSpec((TOK, 2 * STATE), col),
            pl.BlockSpec((TOK, CH), col),
            pl.BlockSpec((TOK, HEADS), fixed),
            pl.BlockSpec((1, STATE, CH), lambda g: (g, 0, 0)),
            pl.BlockSpec((1, HEADS), fixed),
            pl.BlockSpec((1, CH), col),
        ],
        out_specs=pl.BlockSpec((1, SLICES, TOK, LANES), lambda g: (g, 0, 0, 0)),
        out_shape=jax.ShapeDtypeStruct((GROUPS, SLICES, TOK, LANES), bf16),
        compiler_params=params(50),
        cost_estimate=pl.CostEstimate(flops=1 << 31, bytes_accessed=40 << 20, transcendentals=1 << 21),
        name="mixer",
    )(scal, x, z, p, xs, cum, carry, skip, gain)


def project_kernel(s_ref, mine_ref, theirs_ref, own_ref, *refs):
    w_refs, (keep_ref, send_ref, acc_ref) = refs[:10], refs[10:]
    t = pl.program_id(0)

    def lhs(at):
        parts = []
        for k in range(SLICES):
            j = k if at is None else s_ref[at + k]
            parts.append(jnp.concatenate([mine_ref[0, j], theirs_ref[0, j]], axis=0))
        return jnp.concatenate(parts, axis=1)

    @pl.when(t == 0)
    def _():
        acc_ref[...] = mm(lhs(None), own_ref[...])

    @pl.when(t > 0)
    def _():
        for h in range(2):
            w = jnp.concatenate([r[0] for r in w_refs[5 * h : 5 * h + 5]], axis=0)
            acc_ref[:, h * HALF : (h + 1) * HALF] += mm(lhs(8 + 4 * h), w)

    @pl.when(t == pl.num_programs(0) - 1)
    def _():
        keep_ref[...] = acc_ref[:TOK]
        send_ref[...] = acc_ref[TOK:].astype(bf16)


def project(scal, mine, theirs, own, slices):
    fixed = lambda t, s: (0, 0)
    return pl.pallas_call(
        project_kernel,
        grid_spec=pltpu.PrefetchScalarGridSpec(
            num_scalar_prefetch=1,
            grid=(4,),
            in_specs=[
                pl.BlockSpec((1, SLICES, TOK, LANES), lambda t, s: (s[t], 0, 0, 0)),
                pl.BlockSpec((1, SLICES, TOK, LANES), lambda t, s: (s[4 + t], 0, 0, 0)),
                pl.BlockSpec((CH, D), fixed),
            ]
            + [
                pl.BlockSpec((1, rows, HALF), lambda t, s: (jnp.maximum(t - 1, 0), 0, 0))
                for rows in (LANES, LANES, LANES, LANES // 2, LANES // 2)
            ]
            * 2,
            out_specs=[pl.BlockSpec((TOK, D), fixed), pl.BlockSpec((TOK, D), fixed)],
            scratch_shapes=[pltpu.VMEM((2 * TOK, D), f32)],
        ),
        out_shape=[jax.ShapeDtypeStruct((TOK, D), f32), jax.ShapeDtypeStruct((TOK, D), bf16)],
        compiler_params=params(48),
        cost_estimate=pl.CostEstimate(flops=1 << 32, bytes_accessed=14 << 20, transcendentals=0),
        name="project",
    )(scal, mine, theirs, own, *slices)


def merge_kernel(keep_ref, other_ref, hid_ref, fgain_ref, hit_ref, merged_ref, normed_ref, out_ref):
    @pl.when(pl.program_id(0) == 0)
    def _():
        total = keep_ref[...] + other_ref[...].astype(f32)
        merged = (hid_ref[...].astype(f32) + total).astype(bf16)
        merged_ref[...] = merged
        mf = merged.astype(f32)
        sq = jnp.mean(mf * mf, axis=-1, keepdims=True)
        normed_ref[...] = (mf * lax.rsqrt(sq + EPS) * fgain_ref[...]).astype(bf16)

    pack(out_ref, mm(hit_ref[0], normed_ref[...]))


def merge(keep, other, hid, fgain, hit):
    fixed = lambda i: (0, 0)
    return pl.pallas_call(
        merge_kernel,
        grid=(BLOCKS,),
        in_specs=[pl.BlockSpec((TOK, D), fixed)] * 3
        + [
            pl.BlockSpec((1, D), fixed),
            pl.BlockSpec((1, SB * MAIN + SB, TOK), lambda i: (i, 0, 0)),
        ],
        out_specs=[
            pl.BlockSpec((TOK, D), fixed),
            pl.BlockSpec((TOK, D), fixed),
            pl.BlockSpec((SB, ROWS, QW), lambda i: (i, 0, 0)),
        ],
        out_shape=[jax.ShapeDtypeStruct((TOK, D), bf16)] * 2
        + [jax.ShapeDtypeStruct((EXPERTS, ROWS, QW), bf16)],
        compiler_params=params(BIG),
        cost_estimate=pl.CostEstimate(flops=1 << 31, bytes_accessed=12 << 20, transcendentals=0),
        name="merge",
    )(keep, other, hid, fgain, hit)


def shift_z(v, k):
    return lax.ppermute(v, "seq", [(s, (s + 2 * k) % 8) for s in range(8)])


def shift_x(v, k):
    return lax.ppermute(v, "dp", [(d, d // 4 * 4 + (d + k) % 4) for d in range(16)])


def shift_y(v, k):
    return lax.ppermute(v, "dp", [(d, (d + 4 * k) % 16) for d in range(16)])


def swap_cores(v):
    return lax.ppermute(v, "seq", [(s, s ^ 1) for s in range(8)])


def fetch_weight(w, x, y):
    a = lax.dynamic_slice(w, (x * LANES, 0), (LANES, HALF))
    b = lax.dynamic_slice(w, (y * LANES, HALF), (LANES, HALF))
    slab = jnp.stack([a, b])
    return near(slab, shift_z)


def slabs(pair):
    got = pair + [jnp.concatenate(far(pair, shift_z), axis=1)]
    return jnp.stack([v[0] for v in got]), jnp.stack([v[1] for v in got])


def near(v, shift):
    return [shift(v, 1), shift(v, -1)]


def far(pair, shift):
    h = LANES // 2
    return [shift(pair[0][:, :h], 1), shift(pair[1][:, h:], -1)]


def slot_hits(rank, half):
    r3 = jnp.broadcast_to(rank[:, None, :], (SB, MAIN, TOK))
    c = lax.broadcasted_iota(jnp.int32, (SB, MAIN, TOK), 1) + half * MAIN
    main = (r3 == c.astype(f32)).reshape(SB * MAIN, TOK)
    return main, rank == float(2 * MAIN + half)


def route_kernel(ids_ref, rw_ref, hit_ref, wgt_ref):
    e = lax.broadcasted_iota(jnp.int32, (EXPERTS, TOK), 0)
    member = jnp.zeros((EXPERTS, TOK), f32)
    weight = jnp.zeros((EXPERTS, TOK), f32)
    for k in range(TOP):
        hit = ids_ref[k : k + 1, :] == e
        member += jnp.where(hit, 1.0, 0.0)
        weight += jnp.where(hit, rw_ref[k : k + 1, :], 0.0)
    r = lax.broadcasted_iota(jnp.int32, (TOK, TOK), 0)
    c = lax.broadcasted_iota(jnp.int32, (TOK, TOK), 1)
    before = (r < c).astype(f32).astype(bf16)
    rank = jnp.where(member > 0.5, mm(member.astype(bf16), before), -1.0)
    for half in range(2):
        for i in range(BLOCKS):
            rows = slice(i * SB, (i + 1) * SB)
            main, over = slot_hits(rank[rows], half)
            wt = weight[rows]
            wm = jnp.broadcast_to(wt[:, None, :], (SB, MAIN, TOK)).reshape(SB * MAIN, TOK)
            hit = jnp.concatenate([main.astype(f32), over.astype(f32)], axis=0)
            hit_ref[half, i] = hit.astype(bf16)
            w = hit * jnp.concatenate([wm, wt], axis=0)
            wgt_ref[half, i] = w.T.astype(bf16)


def route_tables(ids_t, rw_t):
    vm = pl.BlockSpec(memory_space=pltpu.VMEM)
    n = SB * MAIN + SB
    return pl.pallas_call(
        route_kernel,
        in_specs=[vm, vm],
        out_specs=[vm, vm],
        out_shape=[
            jax.ShapeDtypeStruct((2, BLOCKS, n, TOK), bf16),
            jax.ShapeDtypeStruct((2, BLOCKS, TOK, n), bf16),
        ],
        compiler_params=pltpu.CompilerParams(vmem_limit_bytes=32 << 20),
        cost_estimate=pl.CostEstimate(flops=1 << 28, bytes_accessed=3 << 20, transcendentals=0),
        name="route_tables",
    )(ids_t, rw_t)


def over_perm(transposed=False):
    n = SB * NQ
    r = lax.broadcasted_iota(jnp.int32, (n, n), 1 if transposed else 0)
    c = lax.broadcasted_iota(jnp.int32, (n, n), 0 if transposed else 1)
    return (c == (r % SB) * NQ + r // SB).astype(f32).astype(bf16)


def unpack(ref):
    n = SB * NQ
    over = mm(over_perm(), ref[:, NQ * MAIN :, :].reshape(n, QW)).astype(bf16)
    parts = []
    for q in range(NQ):
        main = ref[:, q * MAIN : (q + 1) * MAIN, :].reshape(SB * MAIN, QW)
        parts.append(jnp.concatenate([main, over[q * SB : (q + 1) * SB]], axis=0))
    return jnp.concatenate(parts, axis=1)


def pack(ref, rows):
    n = SB * MAIN
    for q in range(NQ):
        ref[:, q * MAIN : (q + 1) * MAIN, :] = (
            rows[:n, q * QW : (q + 1) * QW].reshape(SB, MAIN, QW).astype(bf16)
        )
    over = jnp.concatenate([rows[n:, q * QW : (q + 1) * QW] for q in range(NQ)], axis=0)
    over = mm(over_perm(True), over.astype(bf16))
    ref[:, NQ * MAIN :, :] = over.reshape(SB, NQ, QW).astype(bf16)


def dispatch_kernel(hit_ref, x_ref, out_ref):
    pack(out_ref, mm(hit_ref[0], x_ref[...]))


def dispatch(hit, normed):
    n = SB * MAIN + SB
    return pl.pallas_call(
        dispatch_kernel,
        grid=(BLOCKS,),
        in_specs=[
            pl.BlockSpec((1, n, TOK), lambda i: (i, 0, 0)),
            pl.BlockSpec((TOK, D), lambda i: (0, 0)),
        ],
        out_specs=pl.BlockSpec((SB, ROWS, QW), lambda i: (i, 0, 0)),
        out_shape=jax.ShapeDtypeStruct((EXPERTS, ROWS, QW), bf16),
        compiler_params=params(BIG),
        cost_estimate=pl.CostEstimate(flops=1 << 31, bytes_accessed=6 << 20, transcendentals=0),
        name="dispatch",
    )(hit, normed)


def expert_kernel(in_ref, gu_ref, dn_ref, out_ref):
    hidden = mm(unpack(in_ref), gu_ref[0])
    gate = hidden[:, :FF]
    active = (gate / (1.0 + jnp.exp(-gate)) * hidden[:, FF:]).astype(bf16)
    pack(out_ref, mm(active, dn_ref[0]))


def expert_ffn(arrived, gate_up, down):
    n = arrived.shape[0]
    return pl.pallas_call(
        expert_kernel,
        grid=(n // SB,),
        in_specs=[
            pl.BlockSpec((SB, ROWS, QW), lambda i: (i, 0, 0)),
            pl.BlockSpec((1, D, 2 * FF), lambda i: (0, 0, 0), pipeline_mode=pl.Buffered(1)),
            pl.BlockSpec((1, FF, D), lambda i: (0, 0, 0), pipeline_mode=pl.Buffered(1)),
        ],
        out_specs=pl.BlockSpec((SB, ROWS, QW), lambda i: (i, 0, 0)),
        out_shape=jax.ShapeDtypeStruct(arrived.shape, bf16),
        compiler_params=params(BIG),
        cost_estimate=pl.CostEstimate(flops=11 << 30, bytes_accessed=20 << 20, transcendentals=1 << 20),
        name="expert_ffn",
    )(arrived, gate_up, down)


def combine_kernel(wgt_ref, ret_ref, base_ref, out_ref, acc_ref):
    i = pl.program_id(0)
    part = mm(wgt_ref[0], unpack(ret_ref))

    @pl.when(i == 0)
    def _():
        acc_ref[...] = part

    @pl.when(i > 0)
    def _():
        acc_ref[...] += part

    cols = pl.ds(pl.multiple_of(i * (D // BLOCKS), D // BLOCKS), D // BLOCKS)
    acc_ref[:, cols] += base_ref[...].astype(f32)

    @pl.when(i == pl.num_programs(0) - 1)
    def _():
        out_ref[...] = acc_ref[...].astype(out_ref.dtype)


def combine(wgt, returned, base, kind):
    n = SB * MAIN + SB
    return pl.pallas_call(
        combine_kernel,
        grid=(BLOCKS,),
        in_specs=[
            pl.BlockSpec((1, TOK, n), lambda i: (i, 0, 0)),
            pl.BlockSpec((SB, ROWS, QW), lambda i: (i, 0, 0)),
            pl.BlockSpec((TOK, D // BLOCKS), lambda i: (0, i)),
        ],
        out_specs=pl.BlockSpec((TOK, D), lambda i: (0, 0)),
        out_shape=jax.ShapeDtypeStruct((TOK, D), kind),
        scratch_shapes=[pltpu.VMEM((TOK, D), f32)],
        compiler_params=params(BIG),
        cost_estimate=pl.CostEstimate(flops=1 << 32, bytes_accessed=9 << 20, transcendentals=0),
        name="combine",
    )(wgt, returned, base)


def body(
    hidden_in, mix_values, mix_gate, state_proj, step_raw, step_bias, decay_rate, skip_gain,
    norm_gain, out_weight, ffn_gain, expert_ids, route_weights, gate_up, down_proj, doc_lengths,
):
    both = ("dp", "seq")
    seq_rank = lax.axis_index("seq")
    dp_rank = lax.axis_index("dp")
    scal = jnp.concatenate([doc_lengths[0], (seq_rank * TOK).astype(jnp.int32)[None]])

    x, y, z, core = dp_rank % 4, dp_rank // 4, seq_rank // 2, seq_rank % 2
    around = jnp.array([0, -1, 1, 2], jnp.int32)
    zs, xs_at, ys_at = ((v + around) % 4 for v in (z, x, y))
    order = jnp.concatenate([zs * 2 + core, zs, xs_at, ys_at]).astype(jnp.int32)
    near_z = fetch_weight(out_weight, x, y)

    hit, wgt = route_tables(expert_ids.T, route_weights.T)
    fresh, cum, xs = span_states(
        scal, step_raw.T, step_bias[None], decay_rate[None], mix_values, state_proj
    )
    xa, yb = slabs(near_z)
    near_x, near_y = near(xa, shift_x), near(yb, shift_y)
    fresh = lax.all_to_all(fresh, "seq", split_axis=0, concat_axis=0, tiled=True)
    carry = prefix(scal, fresh)
    carry, near_x, near_y = lax.optimization_barrier((carry, near_x, near_y))
    far_x, far_y = far(near_x, shift_x), far(near_y, shift_y)
    carry = lax.all_to_all(carry, "seq", split_axis=0, concat_axis=0, tiled=True)
    normed_mix = mixer(
        scal, mix_values, mix_gate, state_proj, xs, cum, carry, skip_gain[None], norm_gain[None]
    )
    other = lax.dynamic_index_in_dim(
        normed_mix.reshape(4, 2, SLICES, TOK, LANES), 1 - core, axis=1, keepdims=False
    )
    other, far_x, far_y = lax.optimization_barrier((other, far_x, far_y))
    slices = [xa] + near_x + far_x + [yb] + near_y + far_y
    keep, send = project(order, normed_mix, swap_cores(other), out_weight, slices)
    merged, normed, first = merge(keep, swap_cores(send), hidden_in, ffn_gain[None], hit[0])

    def exchange(v):
        return lax.all_to_all(v, both, split_axis=0, concat_axis=0, tiled=True)

    arrived = [exchange(first), exchange(dispatch(hit[1], normed))]
    returned = [exchange(expert_ffn(a, gate_up, down_proj)) for a in arrived]
    partial = combine(wgt[0], returned[0], merged, f32)
    return combine(wgt[1], returned[1], partial, bf16)


def solution(mesh):
    tok = P(("dp", "seq"), None)
    in_specs = (
        tok, tok, tok, tok, tok, P(), P(), P(), P(), P("seq", None), P(), tok, tok,
        P(("dp", "seq"), None, None), P(("dp", "seq"), None, None), P("dp", None),
    )
    return jax.shard_map(body, mesh=mesh, in_specs=in_specs, out_specs=tok, check_vma=False)
```
